32 devices in a mesh: dp: 2 (over y), ctx: 4 (over z), tp: 4 (over x, core).
Axes of the slice: x: 2, y: 2, z: 4, core: 2. Of those that a mesh axis runs over, the one named last changes fastest.
Arguments:
- layer_input: bfloat16 [2, 4096, 1024], P('dp', 'ctx'), may hold values from -6 to 6
- segments: int32 [2, 4096], P('dp', 'ctx'), may hold values from 0 to 16, as said below
- positions: int32 [2, 4096], P('dp', 'ctx'), may hold values from 0 to 4094, as said below
- w_q: bfloat16 [1024, 1024], P('dp', 'tp'), may hold values from -0.1875 to 0.1875
- w_k: bfloat16 [1024, 1024], P('dp', 'tp'), may hold values from -0.1875 to 0.1875
- w_v: bfloat16 [1024, 1024], P('dp', 'tp'), may hold values from -0.1875 to 0.1875
- w_o: bfloat16 [1024, 1024], P('tp', 'dp'), may hold values from -0.75 to 0.75
- w_in: bfloat16 [1024, 4096], P('dp', 'tp'), may hold values from -0.1875 to 0.1875
- w_out: bfloat16 [4096, 1024], P('tp', 'dp'), may hold values from -0.09375 to 0.09375
- ln1_gain: bfloat16 [1024], P('dp'), may hold values from 0.25 to 1.75
- ln1_bias: bfloat16 [1024], P('dp'), may hold values from -1 to 1
- ln2_gain: bfloat16 [1024], P('dp'), may hold values from 0.25 to 1.75
- ln2_bias: bfloat16 [1024], P('dp'), may hold values from -1 to 1
- cotangent: bfloat16 [2, 4096, 1024], P('dp', 'ctx'), may hold values from -6 to 6
Outputs:
- layer_output: float32 [2, 4096, 1024], P('dp', 'ctx')
- x_grad: float32 [2, 4096, 1024], P('dp', 'ctx')
- w_q_grad: float32 [1024, 1024], P('dp', 'tp')
- w_k_grad: float32 [1024, 1024], P('dp', 'tp')
- w_v_grad: float32 [1024, 1024], P('dp', 'tp')
- w_o_grad: float32 [1024, 1024], P('tp', 'dp')
- w_in_grad: float32 [1024, 4096], P('dp', 'tp')
- w_out_grad: float32 [4096, 1024], P('tp', 'dp')
- ln1_gain_grad: float32 [1024], P('dp')
- ln1_bias_grad: float32 [1024], P('dp')
- ln2_gain_grad: float32 [1024], P('dp')
- ln2_bias_grad: float32 [1024], P('dp')
The draws below stay inside these ranges and needn't reach their ends.
Inputs may be any that keep to these rules, and one draw needn't show every extreme that they name: `segments`: along a sequence the document number never falls; it is 0 at the first slot and 16 at the last. `positions`: A slot's position is its offset from the first slot of its document.
All inputs are finite; a program needn't handle non-finite values.
Results may differ from the reference program's by a relative error of at most 0.023.
Values may be sent and summed in bfloat16 or wider, within the bound.
No kernel may reach another device: no remote copies, remote signals or barrier semaphores. Data moves between devices by JAX's collectives and lax.ppermute only.
A program may use at most 256 MiB of HBM per device.

```python
import jax
import jax.numpy as jnp
from jax import lax

D = 1024
H = 16
FF = 4096
HD = 64
LEN = 4096
CUTS = 16
SEQ = 2


def document_layout(key):
    picks = jax.random.randint(jax.random.fold_in(key, 7), (SEQ, CUTS), 0, 64)
    rows = jnp.arange(SEQ, dtype=jnp.int32)
    picks = picks * (rows[:, None] != 0).astype(jnp.int32)
    bounds = 1 + picks * picks * picks * (LEN - 1) // 262144
    slots = jnp.arange(LEN, dtype=jnp.int32)
    before = bounds[:, None, :] <= slots[None, :, None]
    docs = jnp.sum(before.astype(jnp.int32), axis=-1).astype(jnp.int32)
    first_slot = jnp.max(jnp.where(before, bounds[:, None, :], 0), axis=-1)
    places = (slots[None, :] - first_slot).astype(jnp.int32)
    return (docs, places)


def draw_segments(key, part):
    return document_layout(key)[0]


def draw_positions(key, part):
    return document_layout(key)[1]


def steps_of(rng, shape, pieces, low, largest):
    def one(dim, shards_of):
        steps = jax.random.uniform(jax.random.fold_in(jax.random.fold_in(rng, 6), dim), (shards_of,), jnp.float32, low / len(pieces), largest / len(pieces))
        return jnp.repeat(jnp.exp(steps), shape[dim] // shards_of).reshape((-1,) + (1,) * (len(shape) - dim - 1))

    factor_of = one(*pieces[0])
    for cut in pieces[1:]:
        factor_of = factor_of * one(*cut)
    return factor_of


def centred(stream_key, extent, scale, bound, cuts=(), kind=jnp.bfloat16):
    drawn = jax.random.normal(stream_key, extent, jnp.float32) * scale
    if len(cuts) > 0:
        drawn = steps_of(stream_key, extent, cuts, -0.22, 0.18) * drawn
    return jnp.clip(drawn, min=-bound, max=bound).astype(kind)


def setup_inputs(seed: int = 0) -> dict:
    splits = jax.random.split(jax.random.key(seed), 15)
    layer_input = centred(splits[0], (SEQ, LEN, D), 1.0, 6.0, ((0, 2), (1, 4)))
    segments = draw_segments(jax.random.fold_in(splits[14], 71), 0)
    positions = draw_positions(jax.random.fold_in(splits[14], 71), 0)
    w_q = centred(splits[3], (D, D), D ** -0.5, 0.1875, ((0, 2), (1, 4)))
    w_k = centred(splits[4], (D, D), D ** -0.5, 0.1875, ((0, 2), (1, 4)))
    w_v = centred(splits[5], (D, D), D ** -0.5, 0.1875, ((0, 2), (1, 4)))
    w_o = centred(splits[6], (D, D), (D // 16) ** -0.5, 0.75, ((0, 4), (1, 2)))
    w_in = centred(splits[7], (D, FF), D ** -0.5, 0.1875, ((0, 2), (1, 4)))
    w_out = centred(splits[8], (FF, D), FF ** -0.5, 0.09375, ((0, 4), (1, 2)))
    ln1_gain = jnp.clip(1.0 + 0.15 * jax.random.normal(splits[9], (D,), jnp.float32), 0.25, 1.75).astype(jnp.bfloat16)
    ln1_bias = centred(splits[10], (D,), 0.2, 1.0, ((0, 2),))
    ln2_gain = jnp.clip(1.0 + 0.15 * jax.random.normal(splits[11], (D,), jnp.float32), 0.25, 1.75).astype(jnp.bfloat16)
    ln2_bias = centred(splits[12], (D,), 0.2, 1.0, ((0, 2),))
    cotangent = centred(splits[13], (SEQ, LEN, D), 1.0, 6.0, ((0, 2), (1, 4)))
    return {"layer_input": layer_input, "segments": segments, "positions": positions, "w_q": w_q, "w_k": w_k, "w_v": w_v, "w_o": w_o, "w_in": w_in, "w_out": w_out, "ln1_gain": ln1_gain, "ln1_bias": ln1_bias, "ln2_gain": ln2_gain, "ln2_bias": ln2_bias, "cotangent": cotangent}


@jax.custom_vjp
def low(v):
    return lax.optimization_barrier(v.astype(jnp.bfloat16)).astype(jnp.float32)

@jax.custom_vjp
def low_back(v):
    return v

def low_keep(v):
    return (low(v), None)

def low_pass(kept, grad):
    return (grad,)

def back_keep(v):
    return (v, None)

def back_low(kept, grad):
    return (low(grad),)
low.defvjp(low_keep, low_pass)
low_back.defvjp(back_keep, back_low)

def matmul(left, right):
    return jnp.dot(left, right, precision=lax.Precision.HIGHEST)

def rotary(values, positions):
    half = HD // 2
    freq = 10000.0 ** (-jnp.arange(half, dtype=jnp.float32) * 2.0 / HD)
    angles = positions.astype(jnp.float32)[:, None] * freq[None, :]
    cosine = jnp.cos(angles)[:, None, :]
    sine = jnp.sin(angles)[:, None, :]
    first = values[..., :half]
    second = values[..., half:]
    return jnp.concatenate([first * cosine - second * sine, second * cosine + first * sine], axis=-1)

def layer_norm(values, gain, shift):
    centered = values - lax.optimization_barrier(jnp.mean(values, axis=-1, keepdims=True))
    inverse = lax.rsqrt(lax.optimization_barrier(jnp.mean(centered * centered, axis=-1, keepdims=True)) + 1e-05)
    return centered * inverse * gain + shift

def attend(query_block, doc_block, keys, values, doc_keys):
    scores = jnp.einsum('qhd,khd->hqk', query_block, keys, precision=lax.Precision.HIGHEST)
    scores = low_back(scores * HD ** (-0.5))
    same = doc_block[:, None] == doc_keys[None, :]
    scores = jnp.where(same[None], scores, -1e+30)
    scores = scores - lax.optimization_barrier(jnp.max(scores, axis=-1, keepdims=True))
    weights = jnp.exp(scores)
    probs = low(weights / lax.optimization_barrier(jnp.sum(weights, axis=-1, keepdims=True)))
    return jnp.einsum('hqk,khd->qhd', probs, values, precision=lax.Precision.HIGHEST)

def one_sequence(tokens, docs, places, params):
    w_q, w_k, w_v, w_o, w_in, w_out, gain_one, shift_one, gain_two, shift_two = params

    def project(weight):
        return low_back(matmul(tokens, weight)).reshape(LEN, H, HD)
    queries = low(rotary(project(w_q), places))
    keys = low(rotary(project(w_k), places))
    values = low(project(w_v))
    block = min(512, LEN)
    query_blocks = queries.reshape(LEN // block, block, H, HD)
    doc_blocks = docs.reshape(LEN // block, block)
    attend_block = jax.checkpoint(lambda pair: attend(pair[0], pair[1], keys, values, docs))
    attended = lax.map(attend_block, (query_blocks, doc_blocks)).reshape(LEN, D)
    attended = low(low_back(attended))
    mixed = low_back(matmul(attended, w_o))
    hidden = layer_norm(tokens + mixed, gain_one, shift_one)
    pre_act = low_back(matmul(low(hidden), w_in))
    activated = low(jax.nn.gelu(pre_act, approximate=False))
    branch = low_back(matmul(activated, w_out))
    return layer_norm(hidden + branch, gain_two, shift_two)

def reference(layer_input, segments, positions, w_q, w_k, w_v, w_o, w_in, w_out, ln1_gain, ln1_bias, ln2_gain, ln2_bias, cotangent):
    params = tuple((p.astype(jnp.float32) for p in (w_q, w_k, w_v, w_o, w_in, w_out, ln1_gain, ln1_bias, ln2_gain, ln2_bias)))
    inputs = layer_input.astype(jnp.float32)

    def forward(tokens_all, weights):
        return lax.map(lambda item: one_sequence(item[0], item[1], item[2], weights), (tokens_all, segments, positions))
    output, pullback = jax.vjp(forward, inputs, params)
    input_grad, grads = pullback(cotangent.astype(jnp.float32))
    return (output, input_grad, grads[0], grads[1], grads[2], grads[3], grads[4], grads[5], grads[6], grads[7], grads[8], grads[9])
```

```python
import functools

import jax
import jax.numpy as jnp
from jax import lax
from jax.experimental import pallas as pl
from jax.experimental.pallas import tpu as pltpu
from jax.sharding import PartitionSpec as P

D = 1024
H = 16
HEAD = D // H
LANES = 128
DOCS = 17
NCH = 2

NEG_BIG = -1e30
SQRT_HALF = 0.7071067811865476
INV_SQRT_TAU = 0.3989422804014327
LOG2E = 1.4426950408889634
LN2 = 0.6931471805599453
F32 = jnp.float32
BF16 = jnp.bfloat16
NT = (((1,), (1,)), ((), ()))
VMEM_LIMIT = 60 * 1024 * 1024


def order(n):
    found, bit = [0], n >> 1
    while bit:
        found = found + [d | bit for d in found]
        bit >>= 1
    return found


def swap(value, axis, bit):
    n = lax.axis_size(axis)
    return lax.ppermute(value, axis, [(i, i ^ bit) for i in range(n)])


def gather(value, axis):
    parts, bit = [value], lax.axis_size(axis) >> 1
    while bit:
        parts = parts + [swap(p, axis, bit) for p in parts]
        bit >>= 1
    return parts


def part_of(value, dim, start, size):
    return lax.slice_in_dim(value, start, start + size, axis=dim)


def scatter(send, keep, axis, dim):
    n, bit = lax.axis_size(axis), 1
    while True:
        got = swap(send, axis, bit)
        bit <<= 1
        if bit >= n:
            return keep, got
        half = keep.shape[dim] // 2
        upper = part_of(keep, dim, half, half) + part_of(got, dim, half, half).astype(F32)
        keep = part_of(keep, dim, 0, half) + part_of(got, dim, 0, half).astype(F32)
        send = upper.astype(BF16)


def call(body, out_shape, *args, grid=None, in_specs=None, out_specs=None, scratch=(), flops=0, trans=0, name=None):
    size = sum(a.size * a.dtype.itemsize for a in args)
    outs = out_shape if isinstance(out_shape, (list, tuple)) else [out_shape]
    size += sum(o.size * o.dtype.itemsize for o in outs)
    extra = {}
    if grid is not None:
        extra["grid"] = grid
    if in_specs is not None:
        extra["in_specs"] = in_specs
    if out_specs is not None:
        extra["out_specs"] = out_specs
    return pl.pallas_call(
        body,
        out_shape=out_shape,
        scratch_shapes=list(scratch),
        compiler_params=pltpu.CompilerParams(vmem_limit_bytes=VMEM_LIMIT),
        cost_estimate=pl.CostEstimate(flops=int(flops), bytes_accessed=int(size), transcendentals=int(trans)),
        name=name,
        **extra,
    )(*args)


def shape(dims, dtype):
    return jax.ShapeDtypeStruct(dims, dtype)


SMEM = pl.BlockSpec(memory_space=pltpu.SMEM)
FULL = pl.BlockSpec(memory_space=pltpu.VMEM)


def whole_block(value):
    return pl.BlockSpec(value.shape, lambda i: (0,) * len(value.shape))


def arrange_body(ids, src, out, *, tp, dp, shares):
    rows, width = src.shape
    share, cols = rows // tp, width // dp
    piece = share // NCH
    for a in range(NCH):
        for j, d in enumerate(shares):
            for e, f in enumerate(order(dp)):
                row = pl.multiple_of((ids[2] ^ d) * share + a * piece, piece)
                col = pl.multiple_of((ids[0] ^ f) * cols, cols)
                at = (a * len(shares) + j) * piece
                out[at : at + piece, e * cols : (e + 1) * cols] = src[pl.ds(row, piece), pl.ds(col, cols)]


def arrange(ids, src, tp, dp, shares):
    rows = src.shape[0] // tp * len(shares)
    return call(
        functools.partial(arrange_body, tp=tp, dp=dp, shares=shares),
        shape((rows, src.shape[1]), src.dtype),
        ids,
        src,
        in_specs=[SMEM, FULL],
        name="arrange",
    )


def place_body(ids, *refs, tp, dp):
    *parts, out = refs
    rows, width = out.shape
    share, cols = rows // tp, width // dp
    piece = share // NCH
    for a in range(NCH):
        for j, d in enumerate(order(tp)):
            for e, f in enumerate(order(dp)):
                row = pl.multiple_of((ids[2] ^ d) * share + a * piece, piece)
                col = pl.multiple_of((ids[0] ^ f) * cols, cols)
                out[pl.ds(row, piece), pl.ds(col, cols)] = parts[a * tp + j][:, e * cols : (e + 1) * cols].astype(F32)


def place(ids, parts, tp, dp, rows):
    return call(
        functools.partial(place_body, tp=tp, dp=dp),
        shape((rows, parts[0].shape[1]), F32),
        ids,
        *parts,
        in_specs=[SMEM] + [FULL] * len(parts),
        name="place",
    )


def place_grad_body(ids, *refs, n, widths):
    parts, outs = refs[:n], refs[n:]
    rows = parts[0].shape[0]
    for part, d in zip(parts, order(n)):
        who = ids[1] ^ d
        at, bit, size = 0, 1, n * rows
        while bit < n:
            size //= 2
            at = at + ((who // bit) % 2) * size
            bit *= 2
        lane = 0
        for out, width in zip(outs, widths):
            out[pl.ds(pl.multiple_of(at, rows), rows), :] = part[:, lane : lane + width].astype(F32)
            lane += width


def sum_over_ctx(ids, value, widths):
    n, bit = lax.axis_size("ctx"), 1
    me = lax.axis_index("ctx")
    while bit < n:
        half = value.shape[0] // 2
        mine = (me // bit) % 2
        send = lax.dynamic_slice_in_dim(value, (1 - mine) * half, half, 0).astype(BF16)
        value = lax.dynamic_slice_in_dim(value, mine * half, half, 0) + swap(send, "ctx", bit).astype(F32)
        bit *= 2
    parts = gather(value.astype(BF16), "ctx")
    rows = parts[0].shape[0] * n
    return call(
        functools.partial(place_grad_body, n=n, widths=widths),
        [shape((rows, w), F32) for w in widths],
        ids,
        *parts,
        in_specs=[SMEM] + [FULL] * n,
        name="place_grad",
    )


def swap_halves(tile, lane):
    return jnp.where(lane % HEAD < HEAD // 2, pltpu.roll(tile, LANES - HEAD // 2, 1), pltpu.roll(tile, HEAD // 2, 1))


def turn(tile):
    return pltpu.roll(tile, HEAD, 1)


def pick(me, values, index):
    chosen = values[index]
    for i in range(1, len(values)):
        chosen = jnp.where(me == i, values[i ^ index], chosen)
    return chosen


def rows_dot(x, pieces):
    total, at = None, 0
    for w in pieces:
        size = w.shape[0]
        term = jnp.dot(x[:, at : at + size], w[...], preferred_element_type=F32)
        total = term if total is None else total + term
        at += size
    return total


def kv_body(ids, x, *refs, dp, n):
    wk, wv = refs[:dp], refs[dp : 2 * dp]
    cosine, sine = refs[2 * dp], refs[2 * dp + 1]
    outs = refs[2 * dp + 2 :]
    me = ids[1]
    step = 256
    lane = lax.broadcasted_iota(jnp.int32, (step, LANES), 1)
    for i in range(x.shape[0] // step):
        rows = slice(i * step, (i + 1) * step)
        tokens = x[rows, :]
        key, value = rows_dot(tokens, wk), rows_dot(tokens, wv)
        heads = []
        for t in range(n // 2):
            kt = key[:, t * LANES : (t + 1) * LANES]
            vt = value[:, t * LANES : (t + 1) * LANES]
            kt = kt * cosine[rows, :] + swap_halves(kt, lane) * sine[rows, :]
            heads.append(jnp.where(lane < HEAD, kt, turn(vt)))
            heads.append(jnp.where(lane < HEAD, turn(kt), vt))
        for e in range(n):
            outs[e][rows, :] = pick(me, heads, e).astype(BF16)


def q_body(ids, x, *refs, dp, n, half):
    wq = refs[:dp]
    cosine, sine = refs[dp], refs[dp + 1]
    outs = refs[dp + 2 :]
    me = ids[1]
    lane = lax.broadcasted_iota(jnp.int32, (half, LANES), 1)
    for a in range(NCH):
        sides = []
        for h in range(2):
            rows = slice((2 * a + h) * half, (2 * a + h + 1) * half)
            query = rows_dot(x[rows, :], wq)
            heads = []
            for t in range(n // 2):
                qt = query[:, t * LANES : (t + 1) * LANES]
                qt = qt * cosine[rows, :] + swap_halves(qt, lane) * sine[rows, :]
                qt = qt * (HEAD**-0.5 * LOG2E)
                other = turn(qt)
                heads.extend([qt, other] if h == 0 else [other, qt])
            sides.append(heads)
        packed = [jnp.where(lane < HEAD, lo, hi) for lo, hi in zip(*sides)]
        for e in range(n):
            outs[a * n + e][...] = pick(me, packed, e).astype(BF16)


def unpack_pairs(me, packed, n, h, lane):
    tiles = []
    for t in range(n // 2):
        lo, hi = pick(me, packed, 2 * t), pick(me, packed, 2 * t + 1)
        if h == 0:
            tiles.append(jnp.where(lane < HEAD, lo, turn(hi)))
        else:
            tiles.append(jnp.where(lane < HEAD, turn(lo), hi))
    return tiles


def out_proj_body(ids, *refs, dp, n):
    packed, wo = refs[:n], refs[n : n + dp]
    heads, send, keep = refs[n + dp :]
    half = packed[0].shape[0]
    lane = lax.broadcasted_iota(jnp.int32, (half, LANES), 1)
    pieces = [p[...].astype(F32) for p in packed]
    for h, target in ((1, send), (0, keep)):
        tiles = unpack_pairs(ids[1], pieces, n, h, lane)
        low = jnp.concatenate(tiles, axis=1).astype(BF16)
        heads[h * half : (h + 1) * half, :] = low
        at = 0
        for w in wo:
            cols = w.shape[1]
            target[:, at : at + cols] = jnp.dot(low, w[...], preferred_element_type=F32).astype(target.dtype)
            at += cols


def head_grad_body(ids, *refs, tp, dp, n):
    rows, wo = refs[:tp], refs[tp : tp + dp]
    whole, outs = refs[tp + dp], refs[tp + dp + 1 :]
    piece = rows[0].shape[0]
    for j in range(tp):
        whole[j * piece : (j + 1) * piece, :] = rows[j][...]
    half = tp * piece // 2
    lane = lax.broadcasted_iota(jnp.int32, (half, LANES), 1)
    sides = []
    for h in range(2):
        grad, at = None, 0
        for w in wo:
            cols = w.shape[1]
            term = lax.dot_general(
                whole[h * half : (h + 1) * half, at : at + cols], w[...], NT, preferred_element_type=F32
            )
            grad = term if grad is None else grad + term
            at += cols
        heads = []
        for t in range(n // 2):
            tile = grad[:, t * LANES : (t + 1) * LANES]
            heads.extend([tile, turn(tile)] if h == 0 else [turn(tile), tile])
        sides.append(heads)
    packed = [jnp.where(lane < HEAD, lo, hi) for lo, hi in zip(*sides)]
    for e in range(n):
        outs[e][...] = pick(ids[1], packed, e).astype(BF16)


BQ = 256
KC = 1024


def fill_keys(kv, marks, ka, va):
    size = kv[0].shape[0]
    lane = lax.broadcasted_iota(jnp.int32, (size, LANES), 1)
    ones = jnp.where(lane < 3, 1.0, 0.0).astype(BF16)
    for e, ref in enumerate(kv):
        rows = slice(e * size, (e + 1) * size)
        both = ref[...]
        ka[rows, :] = jnp.where(lane < HEAD, both, marks[rows, :])
        va[rows, :] = jnp.where(lane < HEAD, ones, both)


def query_marks(marks, row, lane):
    there = (lane >= HEAD) & (lane < HEAD + DOCS)
    bias = (marks[pl.ds(row, BQ), :].astype(F32) - 1.0) * -NEG_BIG
    return jnp.where(there, bias, 0.0)


def block_of(i, half, length, first):
    block, h = i // 2, i % 2
    blocks = half // BQ
    token = (block // blocks) * length + first + h * half + (block % blocks) * BQ
    return pl.multiple_of(block * BQ, BQ), h, pl.multiple_of(token, BQ)


def attend_body(*refs, n, first):
    queries, kv = refs[:n], refs[n : 2 * n]
    marks = refs[2 * n]
    outs, lse = refs[2 * n + 1 : 3 * n + 1], refs[3 * n + 1]
    qs, ka, va, os = refs[3 * n + 2 :]
    half, length = queries[0].shape[0], kv[0].shape[0]
    i = pl.program_id(0)

    @pl.when(i == 0)
    def _():
        fill_keys(kv, marks, ka, va)
        for e in range(n):
            qs[e * half : (e + 1) * half, :] = queries[e][...]

    at, h, token = block_of(i, half, length, first)
    lane = lax.broadcasted_iota(jnp.int32, (BQ, LANES), 1)
    q = qs[pl.ds(at, BQ), :].astype(F32)
    q = jnp.where(h == 1, turn(q), q)
    q = jnp.where(lane < HEAD, q, query_marks(marks, token, lane)).astype(BF16)
    scores, top = [], None
    for j in range(n * length // KC):
        s = lax.dot_general(q, ka[j * KC : (j + 1) * KC, :], NT, preferred_element_type=F32)
        scores.append(s)
        for t in range(KC // LANES):
            tile = s[:, t * LANES : (t + 1) * LANES]
            top = tile if top is None else jnp.maximum(top, tile)
    top = jnp.max(top, axis=1, keepdims=True)
    total = jnp.zeros((BQ, LANES), F32)
    for j, s in enumerate(scores):
        p = jnp.exp2(s - top).astype(BF16)
        total += jnp.dot(p, va[j * KC : (j + 1) * KC, :], preferred_element_type=F32)
    weight = total[:, :1]
    o = total / weight
    o = jnp.where(h == 0, turn(o), o)
    log = jnp.broadcast_to(top + jnp.log2(weight), (BQ, LANES))
    other = (lane < HEAD) & (h == 1)
    os[pl.ds(at, BQ), :] = jnp.where(other, os[pl.ds(at, BQ), :], o)
    lse[pl.ds(at, BQ), :] = jnp.where(other, lse[pl.ds(at, BQ), :], log)

    @pl.when(i == pl.num_programs(0) - 1)
    def _():
        for e in range(n):
            outs[e][...] = os[e * half : (e + 1) * half, :].astype(BF16)


def attend(queries, kv, marks, first):
    n, (half, _), length = len(kv), queries[0].shape, kv[0].shape[0]
    steps = n * 2 * half // BQ
    args = [*queries, *kv, marks]
    outs = [shape((half, LANES), BF16)] * n + [shape((n * half, LANES), F32)]
    out = call(
        functools.partial(attend_body, n=n, first=first),
        outs,
        *args,
        grid=(steps,),
        in_specs=[whole_block(a) for a in args],
        out_specs=[whole_block(o) for o in outs],
        scratch=[
            pltpu.VMEM((n * half, LANES), BF16),
            pltpu.VMEM((n * length, LANES), BF16),
            pltpu.VMEM((n * length, LANES), BF16),
            pltpu.VMEM((n * half, LANES), F32),
        ],
        flops=4 * steps * BQ * n * length * 256,
        trans=steps * BQ * n * length,
        name="attend",
    )
    return out[:n], out[n]


def split3(value):
    high = value.astype(BF16).astype(F32)
    rest = value - high
    middle = rest.astype(BF16).astype(F32)
    return high, middle, rest - middle


def attend_back_body(*refs, n, first, start, end):
    queries, grads, outs, kv = (refs[k * n : (k + 1) * n] for k in range(4))
    lse, marks = refs[4 * n], refs[4 * n + 1]
    at = 4 * n + 2
    before = None
    if not start:
        before, at = refs[at], at + 1
    dqs, at = refs[at : at + n], at + n
    if end:
        dkvs, at = refs[at : at + n], at + n
        qs, gs, os, ds_, ka, va, acc = refs[at:]
    else:
        acc, at = refs[at], at + 1
        qs, gs, os, ds_, ka, va = refs[at:]
    half, length = queries[0].shape[0], kv[0].shape[0]
    i = pl.program_id(0)

    @pl.when(i == 0)
    def _():
        fill_keys(kv, marks, ka, va)
        for e in range(n):
            rows = slice(e * half, (e + 1) * half)
            qs[rows, :] = queries[e][...]
            gs[rows, :] = grads[e][...]
            os[rows, :] = outs[e][...]
        acc[...] = jnp.zeros_like(acc) if start else before[...]

    row, h, token = block_of(i, half, length, first)
    lane = lax.broadcasted_iota(jnp.int32, (BQ, LANES), 1)
    here = pl.ds(row, BQ)
    q = qs[here, :].astype(F32)
    g = gs[here, :].astype(F32)
    o = os[here, :].astype(F32)
    log = lse[here, :]
    q = jnp.where(h == 1, turn(q), q)
    g = jnp.where(h == 0, turn(g), g)
    o = jnp.where(h == 0, turn(o), o)
    log = jnp.where(h == 1, turn(log), log)[:, :1]
    dot = jnp.sum(jnp.where(lane >= HEAD, g * o, 0.0), axis=1, keepdims=True)
    b0, b1, b2 = split3(-log)
    q_marks = query_marks(marks, token, lane)
    first_lane = HEAD + DOCS
    qa = jnp.where(lane == first_lane, b0, q_marks)
    qa = jnp.where(lane == first_lane + 1, b1, qa)
    qa = jnp.where(lane == first_lane + 2, b2, qa)
    qa = jnp.where(lane < HEAD, q, qa).astype(BF16)
    b0, b1, b2 = split3(-dot)
    ga = jnp.where(lane == 0, b0, jnp.where(lane == 1, b1, jnp.where(lane == 2, b2, 0.0)))
    ga = jnp.where(lane >= HEAD, g, ga).astype(BF16)
    q_t = q.T[:HEAD].astype(BF16)
    g_t = g.T[HEAD:].astype(BF16)
    total = jnp.zeros((BQ, LANES), F32)
    for j in range(n * length // KC):
        cols = slice(j * KC, (j + 1) * KC)
        s = lax.dot_general(qa, ka[cols, :], NT, preferred_element_type=F32)
        t = lax.dot_general(ga, va[cols, :], NT, preferred_element_type=F32)
        p = jnp.exp2(s)
        ds = (p * t).astype(BF16)
        p = p.astype(BF16)
        acc[HEAD:, cols] += jnp.dot(g_t, p, preferred_element_type=F32)
        acc[:HEAD, cols] += jnp.dot(q_t, ds, preferred_element_type=F32)
        total += jnp.dot(ds, ka[cols, :], preferred_element_type=F32)
    total = total * (HEAD**-0.5)
    total = jnp.where(h == 1, turn(total), total)
    other = (lane < HEAD) & (h == 1)
    ds_[here, :] = jnp.where(other, ds_[here, :], total)

    @pl.when(i == pl.num_programs(0) - 1)
    def _():
        for e in range(n):
            dqs[e][...] = ds_[e * half : (e + 1) * half, :].astype(BF16)
        if end:
            for e in range(n):
                cols = slice(e * length, (e + 1) * length)
                turned = acc[:, cols].T
                key_lane = lax.broadcasted_iota(jnp.int32, (length, LANES), 1)
                dkvs[e][...] = jnp.where(key_lane < HEAD, turned * LN2, turned).astype(BF16)


def attend_back(queries, grads, outs, kv, lse, marks, before, first, end):
    n, (half, _), length = len(kv), queries[0].shape, kv[0].shape[0]
    steps = n * 2 * half // BQ
    start = before is None
    args = [*queries, *grads, *outs, *kv, lse, marks] + ([] if start else [before])
    results = [shape((half, LANES), BF16)] * n
    results += [shape((length, LANES), BF16)] * n if end else [shape((LANES, n * length), F32)]
    out = call(
        functools.partial(attend_back_body, n=n, first=first, start=start, end=end),
        results,
        *args,
        grid=(steps,),
        in_specs=[whole_block(a) for a in args],
        out_specs=[whole_block(o) for o in results],
        scratch=[pltpu.VMEM((n * half, LANES), BF16)] * 3
        + [pltpu.VMEM((n * half, LANES), F32)]
        + [pltpu.VMEM((n * length, LANES), BF16)] * 2
        + ([pltpu.VMEM((LANES, n * length), F32)] if end else []),
        flops=10 * steps * BQ * n * length * 256,
        trans=steps * BQ * n * length,
        name="attend_back",
    )
    return out[:n], out[n:]


def input_grad_body(ids, *refs, dp, n, half):
    dqs, dkvs = refs[: NCH * n], refs[NCH * n : NCH * n + n]
    at = NCH * n + n
    ws = [refs[at + k * dp : at + (k + 1) * dp] for k in range(3)]
    at += 3 * dp
    cosine, sine = refs[at], refs[at + 1]
    whole = refs[at + 2]
    sends, keeps = refs[at + 3 : at + 3 + NCH], refs[at + 3 + NCH :]
    me = ids[1]
    lane = lax.broadcasted_iota(jnp.int32, (half, LANES), 1)
    for a in range(NCH):
        pieces = [dqs[a * n + e][...].astype(F32) for e in range(n)]
        for h, target in ((1, sends[a]), (0, keeps[a])):
            rows = slice((2 * a + h) * half, (2 * a + h + 1) * half)
            kv = [dkvs[e][rows, :].astype(F32) for e in range(n)]
            qt = unpack_pairs(me, pieces, n, h, lane)
            kt = unpack_pairs(me, kv, n, 0, lane)
            vt = unpack_pairs(me, kv, n, 1, lane)
            back = [x * cosine[rows, :] - swap_halves(x, lane) * sine[rows, :] for x in qt + kt]
            low = jnp.concatenate(back + vt, axis=1).astype(BF16)
            whole[rows, :] = low
            wide = low.shape[1] // 3
            col = 0
            for e in range(dp):
                total = None
                for k in range(3):
                    term = lax.dot_general(
                        low[:, k * wide : (k + 1) * wide], ws[k][e][...], NT, preferred_element_type=F32
                    )
                    total = term if total is None else total + term
                size = total.shape[1]
                target[:, col : col + size] = total.astype(target.dtype)
                col += size


FB = 256


def ffn_body(*refs, tp, dp):
    rows, w_in, w_out = refs[:tp], refs[tp : tp + dp], refs[tp + dp : tp + 2 * dp]
    whole, act, slope, send, keep, acc = refs[tp + 2 * dp :]
    piece = rows[0].shape[0]
    half = tp * piece // 2
    i = pl.program_id(0)

    @pl.when(i == 0)
    def _():
        for j in range(tp):
            whole[j * piece : (j + 1) * piece, :] = rows[j][...]
        acc[...] = jnp.zeros_like(acc)

    h = rows_dot(whole[...], w_in)
    phi = 0.5 * (1.0 + lax.erf(h * SQRT_HALF))
    low = (h * phi).astype(BF16)
    act[...] = low
    slope[...] = (phi + h * jnp.exp(-0.5 * h * h) * INV_SQRT_TAU).astype(BF16)
    at = 0
    for w in w_out:
        cols = w.shape[1]
        acc[:, at : at + cols] += jnp.dot(low, w[...], preferred_element_type=F32)
        at += cols

    @pl.when(i == pl.num_programs(0) - 1)
    def _():
        send[...] = acc[half:, :].astype(BF16)
        keep[...] = acc[:half, :]


def ffn_specs(rows, w_in, w_out):
    block = min(FB, w_in[0].shape[1])
    specs = [whole_block(r) for r in rows]
    specs += [pl.BlockSpec((w.shape[0], block), lambda i: (0, i)) for w in w_in]
    specs += [pl.BlockSpec((block, w.shape[1]), lambda i: (i, 0)) for w in w_out]
    return block, specs


def ffn(rows, w_in, w_out):
    tp, dp = len(rows), len(w_in)
    total, width, hidden = tp * rows[0].shape[0], rows[0].shape[1], w_in[0].shape[1]
    block, specs = ffn_specs(rows, w_in, w_out)
    outs = [
        shape((total, width), BF16),
        shape((total, hidden), BF16),
        shape((total, hidden), BF16),
        shape((total // 2, width), BF16),
        shape((total // 2, width), F32),
    ]
    wide = pl.BlockSpec((total, block), lambda i: (0, i))
    return call(
        functools.partial(ffn_body, tp=tp, dp=dp),
        outs,
        *rows,
        *w_in,
        *w_out,
        grid=(hidden // block,),
        in_specs=specs,
        out_specs=[whole_block(outs[0]), wide, wide, whole_block(outs[3]), whole_block(outs[4])],
        scratch=[pltpu.VMEM((total, width), F32)],
        flops=4 * total * width * hidden,
        trans=3 * total * hidden,
        name="ffn",
    )


def ffn_back_body(*refs, tp, dp):
    rows, w_in, w_out = refs[:tp], refs[tp : tp + dp], refs[tp + dp : tp + 2 * dp]
    slope, whole, pre, send, keep, acc = refs[tp + 2 * dp :]
    piece = rows[0].shape[0]
    half = tp * piece // 2
    i = pl.program_id(0)

    @pl.when(i == 0)
    def _():
        for j in range(tp):
            whole[j * piece : (j + 1) * piece, :] = rows[j][...]
        acc[...] = jnp.zeros_like(acc)

    grad, at = None, 0
    for w in w_out:
        cols = w.shape[1]
        term = lax.dot_general(whole[:, at : at + cols], w[...], NT, preferred_element_type=F32)
        grad = term if grad is None else grad + term
        at += cols
    low = (grad * slope[...].astype(F32)).astype(BF16)
    pre[...] = low
    at = 0
    for w in w_in:
        cols = w.shape[0]
        acc[:, at : at + cols] += lax.dot_general(low, w[...], NT, preferred_element_type=F32)
        at += cols

    @pl.when(i == pl.num_programs(0) - 1)
    def _():
        send[...] = acc[half:, :].astype(BF16)
        keep[...] = acc[:half, :]


def ffn_back(rows, w_in, w_out, slope):
    tp, dp = len(rows), len(w_in)
    total, width, hidden = tp * rows[0].shape[0], rows[0].shape[1], w_in[0].shape[1]
    block, specs = ffn_specs(rows, w_in, w_out)
    outs = [
        shape((total, width), BF16),
        shape((total, hidden), BF16),
        shape((total // 2, width), BF16),
        shape((total // 2, width), F32),
    ]
    wide = pl.BlockSpec((total, block), lambda i: (0, i))
    return call(
        functools.partial(ffn_back_body, tp=tp, dp=dp),
        outs,
        *rows,
        *w_in,
        *w_out,
        slope,
        grid=(hidden // block,),
        in_specs=specs + [wide],
        out_specs=[whole_block(outs[0]), wide, whole_block(outs[2]), whole_block(outs[3])],
        scratch=[pltpu.VMEM((total, width), F32)],
        flops=4 * total * width * hidden,
        name="ffn_back",
    )


def normed_of(value):
    centered = value - jnp.mean(value, axis=-1, keepdims=True)
    inverse = lax.rsqrt(jnp.mean(centered * centered, axis=-1, keepdims=True) + 1e-05)
    return centered * inverse, inverse


def norm_one_body(keep, got, tokens, gains, hidden, low, normed, inverse):
    z = keep[...] + got[...].astype(F32) + tokens[...].astype(F32)
    n, r = normed_of(z)
    out = n * gains[0:1, :] + gains[1:2, :]
    hidden[...] = out
    low[...] = out.astype(BF16)
    normed[...] = n
    inverse[...] = jnp.broadcast_to(r, inverse.shape)


def back_of(grad, normed, inverse, gain):
    scaled = grad * gain
    inner = (
        scaled
        - jnp.mean(scaled, axis=-1, keepdims=True)
        - normed * jnp.mean(scaled * normed, axis=-1, keepdims=True)
    )
    return inverse * inner


def norm_two_body(keep, got, hidden, gains, cotangent, out, second, low, terms):
    z = keep[...] + got[...].astype(F32) + hidden[...]
    n, r = normed_of(z)
    out[...] = (n * gains[2:3, :] + gains[3:4, :]).astype(BF16)
    grad = cotangent[...].astype(F32)
    result = back_of(grad, n, r, gains[2:3, :])
    second[...] = result
    low[...] = result.astype(BF16)
    terms[0:1, :] = jnp.sum(grad * n, axis=0, keepdims=True)
    terms[1:2, :] = jnp.sum(grad, axis=0, keepdims=True)


def norm_one_back_body(keep, got, second, normed, inverse, gains, first, low, terms):
    grad = keep[...] + got[...].astype(F32) + second[...]
    n = normed[...]
    result = back_of(grad, n, inverse[:, :1], gains[0:1, :])
    first[...] = result
    low[...] = result.astype(BF16)
    terms[0:1, :] = jnp.sum(grad * n, axis=0, keepdims=True)
    terms[1:2, :] = jnp.sum(grad, axis=0, keepdims=True)


def rotate_heads(values, angles, sign):
    half = HEAD // 2
    cosine = jnp.cos(angles)[:, None, :half]
    sine = sign * jnp.sin(angles)[:, None, :half]
    first, second = values[..., :half], values[..., half:]
    return jnp.concatenate([first * cosine - second * sine, second * cosine + first * sine], axis=-1)


def gathered_attention(tokens, weights, angles, docs):
    rows, width = tokens.shape[0], weights[0].shape[1]
    heads = width // HEAD
    scale = HEAD**-0.5

    def project(w):
        return jnp.dot(tokens, w, preferred_element_type=F32).reshape(rows, heads, HEAD)

    q = rotate_heads(project(weights[0]), angles, 1.0).astype(BF16)
    k = rotate_heads(project(weights[1]), angles, 1.0).astype(BF16)
    v = project(weights[2]).astype(BF16)
    keys = jnp.concatenate(gather(k, "ctx"))
    values = jnp.concatenate(gather(v, "ctx"))
    all_docs = jnp.concatenate(gather(docs, "ctx"))

    def masked():
        s = jnp.einsum("qhd,khd->hqk", q, keys, preferred_element_type=F32) * scale
        return jnp.where(docs[None, :, None] == all_docs[None, None, :], s, NEG_BIG)

    s = masked()
    top = jnp.max(s, axis=-1, keepdims=True)
    p = jnp.exp(s - top)
    total = jnp.sum(p, axis=-1)
    out = jnp.einsum("hqk,khd->qhd", p.astype(BF16), values, preferred_element_type=F32)
    out = out / total.T[..., None]
    log = top[..., 0] + jnp.log(total)

    def backward(grad):
        grad = grad.astype(BF16).reshape(rows, heads, HEAD)
        dot = jnp.sum(grad.astype(F32) * out, axis=-1).T
        p = jnp.exp(masked() - log[..., None])
        dv = jnp.einsum("hqk,qhd->khd", p.astype(BF16), grad, preferred_element_type=F32)
        dp = jnp.einsum("qhd,khd->hqk", grad, values, preferred_element_type=F32)
        ds = (p * (dp - dot[..., None])).astype(BF16)
        dq = jnp.einsum("hqk,khd->qhd", ds, keys, preferred_element_type=F32) * scale
        dk = jnp.einsum("hqk,qhd->khd", ds, q, preferred_element_type=F32) * scale

        def owned(value):
            half = value.shape[0] // 2
            keep, got = scatter(value[half:].astype(BF16), value[:half], "ctx", 0)
            return keep + got.astype(F32)

        dq = rotate_heads(dq, angles, -1.0)
        dk = rotate_heads(owned(dk), angles, -1.0)
        return jnp.concatenate([x.astype(BF16).reshape(rows, width) for x in (dq, dk, owned(dv))], axis=1)

    return out.astype(BF16).reshape(rows, width), backward


def body(
    layer_input,
    segments,
    positions,
    w_q,
    w_k,
    w_v,
    w_o,
    w_in,
    w_out,
    ln1_gain,
    ln1_bias,
    ln2_gain,
    ln2_bias,
    cotangent,
):
    seqs, length, width = layer_input.shape
    assert seqs == 1
    tp, dp, ctx = lax.axis_size("tp"), lax.axis_size("dp"), lax.axis_size("ctx")
    local_width = w_q.shape[1]
    heads = local_width // HEAD
    ids = jnp.stack([lax.axis_index("dp"), lax.axis_index("ctx"), lax.axis_index("tp")]).astype(jnp.int32)
    share = length // tp
    piece = share // NCH
    chunk = piece * tp
    half = chunk // 2
    spread = heads == ctx and heads % 2 == 0 and half % BQ == 0

    wk, wv, wq = gather(w_k, "dp"), gather(w_v, "dp"), gather(w_q, "dp")
    gains = jnp.concatenate(gather(jnp.stack([ln1_gain, ln1_bias, ln2_gain, ln2_bias]), "dp"), axis=1).astype(F32)
    wo, wi, wd = gather(w_o, "dp"), gather(w_in, "dp"), gather(w_out, "dp")

    x = arrange(ids, layer_input.reshape(length, width), tp, dp, order(tp))
    out_grad = arrange(ids, cotangent.reshape(length, width), tp, dp, [0])

    def arrange_tokens(value):
        table = value.reshape(tp, NCH, piece)
        picked = [lax.dynamic_index_in_dim(table, ids[2] ^ d, 0, keepdims=False) for d in order(tp)]
        return jnp.stack(picked, axis=1).reshape(length)

    docs = arrange_tokens(segments.reshape(length))
    places = arrange_tokens(positions.reshape(length)).astype(F32)
    freq = 10000.0 ** (-(jnp.arange(LANES, dtype=jnp.int32) % (HEAD // 2)).astype(F32) * 2.0 / HEAD)
    angles = places[:, None] * freq[None, :]

    if spread:
        side = jnp.where(jnp.arange(LANES) % HEAD < HEAD // 2, -1.0, 1.0)
        cosine, sine = jnp.cos(angles), jnp.sin(angles) * side[None, :]
        all_docs = jnp.concatenate([docs] + [swap(docs, "ctx", e) for e in range(1, ctx)])
        lane = jnp.arange(LANES)[None, :]
        in_docs = (lane >= HEAD) & (lane < HEAD + DOCS)
        marked = jnp.where(in_docs, lane - HEAD != all_docs[:, None], (lane >= HEAD + DOCS) & (lane < HEAD + DOCS + 3))
        marks = marked.astype(BF16)

        def exchange(parts):
            return [parts[0]] + [swap(parts[e], "ctx", e) for e in range(1, ctx)]

        kv = call(
            functools.partial(kv_body, dp=dp, n=heads),
            [shape((length, LANES), BF16)] * ctx,
            ids,
            x,
            *wk,
            *wv,
            cosine,
            sine,
            in_specs=[SMEM] + [FULL] * (3 + 2 * dp),
            flops=4 * length * width * local_width,
            name="project_kv",
        )
        kv = exchange(kv)
        qs = call(
            functools.partial(q_body, dp=dp, n=heads, half=half),
            [shape((half, LANES), BF16)] * (ctx * NCH),
            ids,
            x,
            *wq,
            cosine,
            sine,
            in_specs=[SMEM] + [FULL] * (3 + dp),
            flops=2 * length * width * local_width,
            name="project_q",
        )
        queries = [exchange(qs[a * ctx : (a + 1) * ctx]) for a in range(NCH)]
    else:
        attended, attend_backward = gathered_attention(
            x, [jnp.concatenate(w) for w in (wq, wk, wv)], angles, docs
        )

    outs, logs, attended_low = [], [], []
    normed_one, inverse_one, hidden_low, activated, slopes = [], [], [], [], []
    second_grad, second_low, norm_two_terms, out_parts = [], [], [], []
    pre_grad, first_grad, first_low, norm_one_terms, head_grads = [], [], [], [], []
    chunk_flops = 2 * chunk * width * local_width
    for a in range(NCH):
        if spread:
            o, log = attend(queries[a], kv, marks, a * chunk)
            outs.append(o)
            logs.append(log)
            low, send, keep = call(
                functools.partial(out_proj_body, dp=dp, n=heads),
                [shape((chunk, local_width), BF16), shape((half, width), BF16), shape((half, width), F32)],
                ids,
                *exchange(o),
                *wo,
                in_specs=[SMEM] + [FULL] * (ctx + dp),
                flops=chunk_flops,
                name="project_out",
            )
        else:
            low = attended[a * chunk : (a + 1) * chunk]
            mixed = jnp.concatenate([jnp.dot(low, w, preferred_element_type=F32) for w in wo], axis=1)
            send, keep = mixed[half:].astype(BF16), mixed[:half]
        attended_low.append(low)
        keep, got = scatter(send, keep, "tp", 0)
        hidden, low, normed, inverse = call(
            norm_one_body,
            [
                shape((piece, width), F32),
                shape((piece, width), BF16),
                shape((piece, width), F32),
                shape((piece, LANES), F32),
            ],
            keep,
            got,
            x[a * chunk : a * chunk + piece],
            gains,
            name="norm_one",
        )
        normed_one.append(normed)
        inverse_one.append(inverse)
        whole, act, slope, send, keep = ffn(gather(low, "tp"), wi, wd)
        hidden_low.append(whole)
        activated.append(act)
        slopes.append(slope)
        keep, got = scatter(send, keep, "tp", 0)
        out, second, low, terms = call(
            norm_two_body,
            [
                shape((piece, width), BF16),
                shape((piece, width), F32),
                shape((piece, width), BF16),
                shape((2, width), F32),
            ],
            keep,
            got,
            hidden,
            gains,
            out_grad[a * piece : (a + 1) * piece],
            name="norm_two",
        )
        out_parts.extend(gather(out, "tp"))
        norm_two_terms.append(terms)
        whole, pre, send, keep = ffn_back(gather(low, "tp"), wi, wd, slope)
        second_low.append(whole)
        pre_grad.append(pre)
        keep, got = scatter(send, keep, "tp", 0)
        first, low, terms = call(
            norm_one_back_body,
            [shape((piece, width), F32), shape((piece, width), BF16), shape((2, width), F32)],
            keep,
            got,
            second,
            normed,
            inverse,
            gains,
            name="norm_one_back",
        )
        first_grad.append(first)
        norm_one_terms.append(terms)
        rows = gather(low, "tp")
        if spread:
            whole, *grads = call(
                functools.partial(head_grad_body, tp=tp, dp=dp, n=heads),
                [shape((chunk, width), BF16)] + [shape((half, LANES), BF16)] * ctx,
                ids,
                *rows,
                *wo,
                in_specs=[SMEM] + [FULL] * (tp + dp),
                flops=chunk_flops,
                name="head_grad",
            )
            first_low.append(whole)
            head_grads.append(exchange(grads))
        else:
            whole = jnp.concatenate(rows)
            first_low.append(whole)
            head_grads.append(
                lax.dot_general(whole, jnp.concatenate(wo, axis=1), NT, preferred_element_type=F32)
            )

    def weight_grad(left, right, dim, widths):
        halves = []
        mid = width // 2
        for start in (mid, 0):
            total = None
            for l, r in zip(left, right):
                if dim == 0:
                    l = l[:, start : start + mid]
                else:
                    r = r[:, start : start + mid]
                term = lax.dot_general(l, r, (((0,), (0,)), ((), ())), preferred_element_type=F32)
                total = term if total is None else total + term
            halves.append(total)
        keep, got = scatter(halves[0].astype(BF16), halves[1], "dp", dim)
        return sum_over_ctx(ids, keep + got.astype(F32), widths)

    (w_out_grad,) = weight_grad(activated, second_low, 1, [width // dp])
    (w_in_grad,) = weight_grad(hidden_low, pre_grad, 0, [w_in.shape[1]])
    (w_o_grad,) = weight_grad(attended_low, first_low, 1, [width // dp])

    if spread:
        query_grads, carried = [], None
        for a in range(NCH):
            end = a == NCH - 1
            grads, rest = attend_back(
                queries[a], head_grads[a], outs[a], kv, logs[a], marks, carried, a * chunk, end
            )
            query_grads.extend(exchange(grads))
            if end:
                kv_grads = exchange(rest)
            else:
                (carried,) = rest
        whole, *parts = call(
            functools.partial(input_grad_body, dp=dp, n=heads, half=half),
            [shape((length, 3 * local_width), BF16)]
            + [shape((half, width), BF16)] * NCH
            + [shape((half, width), F32)] * NCH,
            ids,
            *query_grads,
            *kv_grads,
            *wq,
            *wk,
            *wv,
            cosine,
            sine,
            in_specs=[SMEM] + [FULL] * (NCH * ctx + ctx + 3 * dp + 2),
            flops=6 * length * width * local_width,
            name="input_grad",
        )
        sends, keeps = parts[:NCH], parts[NCH:]
    else:
        whole = attend_backward(jnp.concatenate(head_grads))
        weights = jnp.concatenate([jnp.concatenate(w) for w in (wq, wk, wv)], axis=1)
        total = lax.dot_general(whole, weights, NT, preferred_element_type=F32)
        sends = [total[a * chunk + half : (a + 1) * chunk].astype(BF16) for a in range(NCH)]
        keeps = [total[a * chunk : a * chunk + half] for a in range(NCH)]

    grad_parts = []
    for a in range(NCH):
        keep, got = scatter(sends[a], keeps[a], "tp", 0)
        grad_parts.extend(gather((first_grad[a] + keep + got.astype(F32)).astype(BF16), "tp"))
    w_q_grad, w_k_grad, w_v_grad = weight_grad([x], [whole], 0, [local_width] * 3)

    terms = jnp.concatenate([sum(norm_one_terms), sum(norm_two_terms)])
    for axis, n in (("tp", tp), ("ctx", ctx)):
        bit = 1
        while bit < n:
            terms = terms + swap(terms, axis, bit)
            bit *= 2
    bit = 1
    while bit < dp:
        mid = terms.shape[1] // 2
        terms = terms[:, :mid] + swap(terms[:, mid:], "dp", bit)
        bit *= 2

    output = place(ids, out_parts, tp, dp, length)
    input_grad = place(ids, grad_parts, tp, dp, length)
    return (
        output[None],
        input_grad[None],
        w_q_grad,
        w_k_grad,
        w_v_grad,
        w_o_grad,
        w_in_grad,
        w_out_grad,
        terms[0],
        terms[1],
        terms[2],
        terms[3],
    )


def solution(mesh):
    return jax.shard_map(
        body,
        mesh=mesh,
        in_specs=(
            P("dp", "ctx", None),
            P("dp", "ctx"),
            P("dp", "ctx"),
            P("dp", "tp"),
            P("dp", "tp"),
            P("dp", "tp"),
            P("tp", "dp"),
            P("dp", "tp"),
            P("tp", "dp"),
            P("dp"),
            P("dp"),
            P("dp"),
            P("dp"),
            P("dp", "ctx", None),
        ),
        out_specs=(
            P("dp", "ctx", None),
            P("dp", "ctx", None),
            P("dp", "tp"),
            P("dp", "tp"),
            P("dp", "tp"),
            P("tp", "dp"),
            P("dp", "tp"),
            P("tp", "dp"),
            P("dp"),
            P("dp"),
            P("dp"),
            P("dp"),
        ),
        check_vma=False,
    )
```

```python
import functools

import jax
import jax.numpy as jnp
from jax import lax
from jax.experimental import pallas as pl
from jax.experimental.pallas import tpu as pltpu
from jax.sharding import PartitionSpec as P

D = 1024
H = 16
HEAD = D // H
LANES = 128
DOCS = 17

NEG_BIG = -1e30
SQRT_HALF = 0.7071067811865476
INV_SQRT_TAU = 0.3989422804014327
LOG2E = 1.4426950408889634
LN2 = 0.6931471805599453
F32 = jnp.float32
BF16 = jnp.bfloat16
NT = (((1,), (1,)), ((), ()))
VMEM_LIMIT = 60 * 1024 * 1024


def order(n):
    found, bit = [0], n >> 1
    while bit:
        found = found + [d | bit for d in found]
        bit >>= 1
    return found


def swap(value, axis, bit):
    n = lax.axis_size(axis)
    return lax.ppermute(value, axis, [(i, i ^ bit) for i in range(n)])


def gather(value, axis):
    parts, bit = [value], lax.axis_size(axis) >> 1
    while bit:
        parts = parts + [swap(p, axis, bit) for p in parts]
        bit >>= 1
    return parts


def gather_weight(value):
    tp, dp = lax.axis_size("tp"), lax.axis_size("dp")
    parts = {(0, 0): value}

    def double(axis, bit):
        for d, f in list(parts):
            key = (d | bit, f) if axis == "tp" else (d, f | bit)
            parts[key] = swap(parts[d, f], axis, bit)

    bit = tp >> 1
    while bit > 1:
        double("tp", bit)
        bit >>= 1
    bit = dp >> 1
    while bit:
        double("dp", bit)
        bit >>= 1
    if tp > 1:
        double("tp", 1)
    return [parts[d, f] for d in order(tp) for f in order(dp)]


def after(value, *others):
    return lax.optimization_barrier((value, *others))[0]


LINE = []


def in_line(value):
    return after(value, LINE[-1]) if LINE else value


def step(function, *args):
    result = function(in_line(args[0]), *args[1:])
    LINE[:] = [result[0] if isinstance(result, (list, tuple)) else result]
    return result


def part_of(value, dim, start, size):
    return lax.slice_in_dim(value, start, start + size, axis=dim)


def split_sum(got, keep, dim):
    half = keep.shape[dim] // 2
    upper = part_of(keep, dim, half, half) + part_of(got, dim, half, half).astype(F32)
    return upper.astype(BF16), part_of(keep, dim, 0, half) + part_of(got, dim, 0, half).astype(F32)


def scatter(send, keep, axis, dim, got=None):
    n, bit = lax.axis_size(axis), 1
    while True:
        got = swap(send, axis, bit) if got is None else got
        bit <<= 1
        if bit >= n:
            return keep, got
        send, keep = step(functools.partial(split_sum, dim=dim), got, keep)
        got = None


def call(body, out_shape, *args, grid=None, in_specs=None, out_specs=None, scratch=(), flops=0, trans=0, name=None):
    size = sum(a.size * a.dtype.itemsize for a in args)
    outs = out_shape if isinstance(out_shape, (list, tuple)) else [out_shape]
    size += sum(o.size * o.dtype.itemsize for o in outs)
    extra = {}
    if grid is not None:
        extra["grid"] = grid
    if in_specs is not None:
        extra["in_specs"] = in_specs
    if out_specs is not None:
        extra["out_specs"] = out_specs
    args = list(args)
    first = 1 if args[0].shape == (3,) else 0
    args[first] = in_line(args[first])
    result = pl.pallas_call(
        body,
        out_shape=out_shape,
        scratch_shapes=list(scratch),
        compiler_params=pltpu.CompilerParams(vmem_limit_bytes=VMEM_LIMIT),
        cost_estimate=pl.CostEstimate(flops=int(flops), bytes_accessed=int(size), transcendentals=int(trans)),
        name=name,
        **extra,
    )(*args)
    LINE[:] = [result[0] if isinstance(result, (list, tuple)) else result]
    return result


def shape(dims, dtype):
    return jax.ShapeDtypeStruct(dims, dtype)


SMEM = pl.BlockSpec(memory_space=pltpu.SMEM)
FULL = pl.BlockSpec(memory_space=pltpu.VMEM)


def whole_block(value):
    return pl.BlockSpec(value.shape, lambda i: (0,) * len(value.shape))


def arrange_body(ids, src, out, *, tp, dp, shares):
    rows, width = src.shape
    share, cols = rows // tp, width // dp
    for j, d in enumerate(shares):
        for e, f in enumerate(order(dp)):
            row = pl.multiple_of((ids[2] ^ d) * share, share)
            col = pl.multiple_of((ids[0] ^ f) * cols, cols)
            out[j * share : (j + 1) * share, e * cols : (e + 1) * cols] = src[pl.ds(row, share), pl.ds(col, cols)]


def arrange(ids, src, tp, dp, shares):
    rows = src.shape[0] // tp * len(shares)
    return call(
        functools.partial(arrange_body, tp=tp, dp=dp, shares=shares),
        shape((rows, src.shape[1]), src.dtype),
        ids,
        src,
        in_specs=[SMEM, FULL],
        name="arrange",
    )


def place_body(ids, *refs, tp, dp, first):
    *parts, out = refs
    rows, width = out.shape
    share, cols = rows // tp, width // dp
    for j, d in enumerate(order(tp)):
        for e, f in enumerate(order(dp)):
            row = pl.multiple_of((ids[2] ^ d) * share, share)
            col = pl.multiple_of((ids[0] ^ f) * cols, cols)
            block = parts[j][first : first + share, e * cols : (e + 1) * cols]
            out[pl.ds(row, share), pl.ds(col, cols)] = block.astype(F32)


def place(ids, parts, tp, dp, rows, first=0):
    return call(
        functools.partial(place_body, tp=tp, dp=dp, first=first),
        shape((rows, parts[0].shape[1]), F32),
        ids,
        *parts,
        in_specs=[SMEM] + [FULL] * len(parts),
        name="place",
    )


def split_body(ids, got, keep, *outs):
    n, rows = len(outs), outs[0].shape[0]
    for e in range(n):
        at = pl.multiple_of((ids[1] ^ e) * rows, rows)
        total = keep[pl.ds(at, rows), :] + got[pl.ds(at, rows), :].astype(F32)
        outs[e][...] = total.astype(outs[e].dtype)


def merge_body(own, *refs):
    *others, out = refs
    total = own[...]
    for other in others:
        total = total + other[...].astype(F32)
    out[...] = total.astype(BF16)


def place_columns_body(ids, *refs, n, widths):
    parts, outs = refs[:n], refs[n:]
    rows = parts[0].shape[0]
    for e, part in enumerate(parts):
        at = pl.multiple_of((ids[1] ^ e) * rows, rows)
        lane = 0
        for out, width in zip(outs, widths):
            out[pl.ds(at, rows), :] = part[:, lane : lane + width].astype(F32)
            lane += width


def place_rows_body(ids, *refs, n):
    parts, (first, second, terms, whole) = refs[:n], refs[n:]
    rows = parts[0].shape[0]
    for e, part in enumerate(parts):
        at = pl.multiple_of((ids[1] ^ e) * rows, rows)
        whole[pl.ds(at, rows), :] = part[...].astype(F32)
    hidden, middle = first.shape[1], second.shape[0]
    first[...] = whole[:hidden, :].T
    second[...] = whole[hidden : hidden + middle, :]
    terms[...] = whole[hidden + middle : hidden + middle + 8, :]


class GradSum:
    def __init__(self, ids, dim, product):
        self.ids, self.dim, self.product = ids, dim, product

    def begin(self, width):
        mid = width // 2
        send = step(lambda *a: self.product(mid, mid, *a).astype(BF16), *self.operands)
        self.got = swap(send, "dp", 1)
        self.keep = step(lambda *a: self.product(0, mid, *a), *self.operands)

    def over_dp(self):
        keep, got = scatter(None, self.keep, "dp", self.dim, self.got)
        n = lax.axis_size("ctx")
        rows, cols = keep.shape
        block = rows // n
        self.own, *sends = call(
            split_body,
            [shape((block, cols), F32)] + [shape((block, cols), BF16)] * (n - 1),
            self.ids,
            got,
            keep,
            in_specs=[SMEM, FULL, FULL],
            name="split",
        )
        self.parts = [swap(sends[e - 1], "ctx", e) for e in range(1, n)]

    def over_ctx(self):
        own = call(merge_body, shape(self.own.shape, BF16), self.own, *self.parts, name="merge")
        self.parts = [own] + [swap(own, "ctx", e) for e in range(1, lax.axis_size("ctx"))]

    def columns(self, widths):
        n = len(self.parts)
        rows = self.parts[0].shape[0] * n
        return call(
            functools.partial(place_columns_body, n=n, widths=widths),
            [shape((rows, w), F32) for w in widths],
            self.ids,
            *self.parts,
            in_specs=[SMEM] + [FULL] * n,
            name="place_columns",
        )

    def rows(self, hidden, middle):
        n = len(self.parts)
        rows, cols = self.parts[0].shape
        return call(
            functools.partial(place_rows_body, n=n),
            [shape((cols, hidden), F32), shape((middle, cols), F32), shape((8, cols), F32)],
            self.ids,
            *self.parts,
            in_specs=[SMEM] + [FULL] * n,
            scratch=[pltpu.VMEM((n * rows, cols), F32)],
            name="place_rows",
        )


def over_rows(left, right):
    return lax.dot_general(left, right, (((0,), (0,)), ((), ())), preferred_element_type=F32)


def sum_over_rows(left, right, start, size):
    total = None
    for l, r in zip(left, right):
        term = over_rows(l, r[: l.shape[0], start : start + size])
        total = term if total is None else total + term
    return total


def swap_halves(tile, lane):
    return jnp.where(lane % HEAD < HEAD // 2, pltpu.roll(tile, LANES - HEAD // 2, 1), pltpu.roll(tile, HEAD // 2, 1))


def turn(tile):
    return pltpu.roll(tile, HEAD, 1)


def pick(me, values, index):
    chosen = values[index]
    for i in range(1, len(values)):
        chosen = jnp.where(me == i, values[i ^ index], chosen)
    return chosen


def rows_dot(x, pieces, start, size):
    total, at = None, 0
    for w in pieces:
        depth = w.shape[0]
        term = jnp.dot(x[:, at : at + depth], w[:, start : start + size], preferred_element_type=F32)
        total = term if total is None else total + term
        at += depth
    return total


def kv_body(ids, x, *refs, dp, n):
    ws = refs[:dp]
    cosine, sine = refs[dp], refs[dp + 1]
    outs = refs[dp + 2 :]
    me = ids[1]
    step = 256
    width = n * HEAD
    lane = lax.broadcasted_iota(jnp.int32, (step, LANES), 1)
    for i in range(x.shape[0] // step):
        rows = slice(i * step, (i + 1) * step)
        tokens = x[rows, :]
        both = rows_dot(tokens, ws, width, 2 * width)
        heads = []
        for t in range(n // 2):
            kt = both[:, t * LANES : (t + 1) * LANES]
            vt = both[:, width + t * LANES : width + (t + 1) * LANES]
            kt = kt * cosine[rows, :] + swap_halves(kt, lane) * sine[rows, :]
            heads.append(jnp.where(lane < HEAD, kt, turn(vt)))
            heads.append(jnp.where(lane < HEAD, turn(kt), vt))
        for e in range(n):
            outs[e][rows, :] = pick(me, heads, e).astype(BF16)


def q_body(ids, x, *refs, dp, n):
    ws = refs[:dp]
    cosine, sine = refs[dp], refs[dp + 1]
    outs = refs[dp + 2 :]
    me = ids[1]
    step = 256
    half = outs[0].shape[0]
    lane = lax.broadcasted_iota(jnp.int32, (step, LANES), 1)
    for i in range(half // step):
        sides = []
        for h in range(2):
            rows = slice(h * half + i * step, h * half + (i + 1) * step)
            query = rows_dot(x[rows, :], ws, 0, n * HEAD)
            heads = []
            for t in range(n // 2):
                qt = query[:, t * LANES : (t + 1) * LANES]
                qt = qt * cosine[rows, :] + swap_halves(qt, lane) * sine[rows, :]
                qt = qt * (HEAD**-0.5 * LOG2E)
                other = turn(qt)
                heads.extend([qt, other] if h == 0 else [other, qt])
            sides.append(heads)
        packed = [jnp.where(lane < HEAD, lo, hi) for lo, hi in zip(*sides)]
        for e in range(n):
            outs[e][i * step : (i + 1) * step, :] = pick(me, packed, e).astype(BF16)


def unpack_pairs(me, packed, n, h, lane):
    tiles = []
    for t in range(n // 2):
        lo, hi = pick(me, packed, 2 * t), pick(me, packed, 2 * t + 1)
        if h == 0:
            tiles.append(jnp.where(lane < HEAD, lo, turn(hi)))
        else:
            tiles.append(jnp.where(lane < HEAD, turn(lo), hi))
    return tiles


def unpack_body(ids, *refs, n):
    packed, outs = refs[:n], refs[n:]
    half, share = packed[0].shape[0], outs[0].shape[0]
    lane = lax.broadcasted_iota(jnp.int32, (share, LANES), 1)
    for i in range(half // share):
        pieces = [p[i * share : (i + 1) * share, :].astype(F32) for p in packed]
        for h in range(2):
            tiles = unpack_pairs(ids[1], pieces, n, h, lane)
            out = outs[h * (half // share) + i]
            for t, tile in enumerate(tiles):
                out[:, t * LANES : (t + 1) * LANES] = tile.astype(BF16)


def pack_body(ids, *refs, tp, n):
    parts, outs = refs[:tp], refs[tp:]
    half, share = outs[0].shape[0], parts[0].shape[0]
    lane = lax.broadcasted_iota(jnp.int32, (share, LANES), 1)
    for i in range(half // share):
        sides = []
        for h in range(2):
            grad = parts[h * (half // share) + i]
            heads = []
            for t in range(n // 2):
                tile = grad[:, t * LANES : (t + 1) * LANES].astype(F32)
                heads.extend([tile, turn(tile)] if h == 0 else [turn(tile), tile])
            sides.append(heads)
        packed = [jnp.where(lane < HEAD, lo, hi) for lo, hi in zip(*sides)]
        for e in range(n):
            outs[e][i * share : (i + 1) * share, :] = pick(ids[1], packed, e).astype(BF16)


BQ = 256
KC = 1024


def fill_keys(kv, marks, ka, va):
    size = kv[0].shape[0]
    lane = lax.broadcasted_iota(jnp.int32, (size, LANES), 1)
    ones = jnp.where(lane < 3, 1.0, 0.0).astype(BF16)
    for e, ref in enumerate(kv):
        rows = slice(e * size, (e + 1) * size)
        both = ref[...]
        ka[rows, :] = jnp.where(lane < HEAD, both, marks[rows, :])
        va[rows, :] = jnp.where(lane < HEAD, ones, both)


def query_marks(marks, row, lane):
    there = (lane >= HEAD) & (lane < HEAD + DOCS)
    bias = (marks[pl.ds(row, BQ), :].astype(F32) - 1.0) * -NEG_BIG
    return jnp.where(there, bias, 0.0)


def block_of(i, half, length, first):
    block, h = i // 2, i % 2
    blocks = half // BQ
    token = (first + block // blocks) * length + h * half + (block % blocks) * BQ
    return pl.multiple_of(block * BQ, BQ), h, pl.multiple_of(token, BQ)


def attend_body(*refs, m, n, first):
    queries, kv = refs[:m], refs[m : m + n]
    marks = refs[m + n]
    outs, lse = refs[m + n + 1 : 2 * m + n + 1], refs[2 * m + n + 1]
    qs, ka, va, os = refs[2 * m + n + 2 :]
    half, length = queries[0].shape[0], kv[0].shape[0]
    i = pl.program_id(0)

    @pl.when(i == 0)
    def _():
        fill_keys(kv, marks, ka, va)
        for e in range(m):
            qs[e * half : (e + 1) * half, :] = queries[e][...]

    at, h, token = block_of(i, half, length, first)
    lane = lax.broadcasted_iota(jnp.int32, (BQ, LANES), 1)
    q = qs[pl.ds(at, BQ), :].astype(F32)
    q = jnp.where(h == 1, turn(q), q)
    q = jnp.where(lane < HEAD, q, query_marks(marks, token, lane)).astype(BF16)
    scores, top = [], None
    for j in range(n * length // KC):
        s = lax.dot_general(q, ka[j * KC : (j + 1) * KC, :], NT, preferred_element_type=F32)
        scores.append(s)
        for t in range(KC // LANES):
            tile = s[:, t * LANES : (t + 1) * LANES]
            top = tile if top is None else jnp.maximum(top, tile)
    top = jnp.max(top, axis=1, keepdims=True)
    total = jnp.zeros((BQ, LANES), F32)
    for j, s in enumerate(scores):
        p = jnp.exp2(s - top).astype(BF16)
        total += jnp.dot(p, va[j * KC : (j + 1) * KC, :], preferred_element_type=F32)
    weight = total[:, :1]
    o = total / weight
    o = jnp.where(h == 0, turn(o), o)
    log = jnp.broadcast_to(top + jnp.log2(weight), (BQ, LANES))
    other = (lane < HEAD) & (h == 1)
    os[pl.ds(at, BQ), :] = jnp.where(other, os[pl.ds(at, BQ), :], o)
    lse[pl.ds(at, BQ), :] = jnp.where(other, lse[pl.ds(at, BQ), :], log)

    @pl.when(i == pl.num_programs(0) - 1)
    def _():
        for e in range(m):
            outs[e][...] = os[e * half : (e + 1) * half, :].astype(BF16)


def attend(queries, kv, marks, first):
    m, n, (half, _), length = len(queries), len(kv), queries[0].shape, kv[0].shape[0]
    steps = m * 2 * half // BQ
    args = [*queries, *kv, marks]
    outs = [shape((half, LANES), BF16)] * m + [shape((m * half, LANES), F32)]
    out = call(
        functools.partial(attend_body, m=m, n=n, first=first),
        outs,
        *args,
        grid=(steps,),
        in_specs=[whole_block(a) for a in args],
        out_specs=[whole_block(o) for o in outs],
        scratch=[
            pltpu.VMEM((m * half, LANES), BF16),
            pltpu.VMEM((n * length, LANES), BF16),
            pltpu.VMEM((n * length, LANES), BF16),
            pltpu.VMEM((m * half, LANES), F32),
        ],
        flops=4 * steps * BQ * n * length * 256,
        trans=steps * BQ * n * length,
        name="attend",
    )
    return out[:m], out[m]


def split3(value):
    high = value.astype(BF16).astype(F32)
    rest = value - high
    middle = rest.astype(BF16).astype(F32)
    return high, middle, rest - middle


def attend_back_body(*refs, m, n, first, start, end):
    queries, grads, outs = (refs[k * m : (k + 1) * m] for k in range(3))
    kv, lse, marks = refs[3 * m : 3 * m + n], refs[3 * m + n], refs[3 * m + n + 1]
    at = 3 * m + n + 2
    before = None
    if not start:
        before, at = refs[at], at + 1
    if end:
        earlier, at = refs[at : at + n - m], at + n - m
        results, at = refs[at : at + n], at + n
        qs, gs, os, ds_, ka, va, acc = refs[at:]
    else:
        dqs, at = refs[at : at + m], at + m
        acc, at = refs[at], at + 1
        qs, gs, os, ds_, ka, va = refs[at:]
    half, length = queries[0].shape[0], kv[0].shape[0]
    i = pl.program_id(0)

    @pl.when(i == 0)
    def _():
        fill_keys(kv, marks, ka, va)
        for e in range(m):
            rows = slice(e * half, (e + 1) * half)
            qs[rows, :] = queries[e][...]
            gs[rows, :] = grads[e][...]
            os[rows, :] = outs[e][...]
        acc[...] = jnp.zeros_like(acc) if start else before[...]

    row, h, token = block_of(i, half, length, first)
    lane = lax.broadcasted_iota(jnp.int32, (BQ, LANES), 1)
    here = pl.ds(row, BQ)
    q = qs[here, :].astype(F32)
    g = gs[here, :].astype(F32)
    o = os[here, :].astype(F32)
    log = lse[here, :]
    q = jnp.where(h == 1, turn(q), q)
    g = jnp.where(h == 0, turn(g), g)
    o = jnp.where(h == 0, turn(o), o)
    log = jnp.where(h == 1, turn(log), log)[:, :1]
    dot = jnp.sum(jnp.where(lane >= HEAD, g * o, 0.0), axis=1, keepdims=True)
    b0, b1, b2 = split3(-log)
    q_marks = query_marks(marks, token, lane)
    first_lane = HEAD + DOCS
    qa = jnp.where(lane == first_lane, b0, q_marks)
    qa = jnp.where(lane == first_lane + 1, b1, qa)
    qa = jnp.where(lane == first_lane + 2, b2, qa)
    qa = jnp.where(lane < HEAD, q, qa).astype(BF16)
    b0, b1, b2 = split3(-dot)
    ga = jnp.where(lane == 0, b0, jnp.where(lane == 1, b1, jnp.where(lane == 2, b2, 0.0)))
    ga = jnp.where(lane >= HEAD, g, ga).astype(BF16)
    q_t = q.T[:HEAD].astype(BF16)
    g_t = g.T[HEAD:].astype(BF16)
    total = jnp.zeros((BQ, LANES), F32)
    for j in range(n * length // KC):
        cols = slice(j * KC, (j + 1) * KC)
        s = lax.dot_general(qa, ka[cols, :], NT, preferred_element_type=F32)
        t = lax.dot_general(ga, va[cols, :], NT, preferred_element_type=F32)
        p = jnp.exp2(s)
        ds = (p * t).astype(BF16)
        p = p.astype(BF16)
        acc[HEAD:, cols] += jnp.dot(g_t, p, preferred_element_type=F32)
        acc[:HEAD, cols] += jnp.dot(q_t, ds, preferred_element_type=F32)
        total += jnp.dot(ds, ka[cols, :], preferred_element_type=F32)
    total = total * (HEAD**-0.5)
    total = jnp.where(h == 1, turn(total), total)
    other = (lane < HEAD) & (h == 1)
    ds_[here, :] = jnp.where(other, ds_[here, :], total)

    @pl.when(i == pl.num_programs(0) - 1)
    def _():
        if not end:
            for e in range(m):
                dqs[e][...] = ds_[e * half : (e + 1) * half, :].astype(BF16)
        else:
            for e in range(n):
                if e < n - m:
                    results[e][:half, :] = earlier[e][...]
                else:
                    at = (e - n + m) * half
                    results[e][:half, :] = ds_[at : at + half, :].astype(BF16)
                cols = slice(e * length, (e + 1) * length)
                turned = acc[:, cols].T
                key_lane = lax.broadcasted_iota(jnp.int32, (length, LANES), 1)
                results[e][half:, :] = jnp.where(key_lane < HEAD, turned * LN2, turned).astype(BF16)


def attend_back(queries, grads, outs, kv, lse, marks, before, earlier, first, end):
    m, n, (half, _), length = len(queries), len(kv), queries[0].shape, kv[0].shape[0]
    steps = m * 2 * half // BQ
    start = before is None
    args = [*queries, *grads, *outs, *kv, lse, marks] + ([] if start else [before]) + (list(earlier) if end else [])
    if end:
        results = [shape((half + length, LANES), BF16)] * n
    else:
        results = [shape((half, LANES), BF16)] * m + [shape((LANES, n * length), F32)]
    out = call(
        functools.partial(attend_back_body, m=m, n=n, first=first, start=start, end=end),
        results,
        *args,
        grid=(steps,),
        in_specs=[whole_block(a) for a in args],
        out_specs=[whole_block(o) for o in results],
        scratch=[pltpu.VMEM((m * half, LANES), BF16)] * 3
        + [pltpu.VMEM((m * half, LANES), F32)]
        + [pltpu.VMEM((n * length, LANES), BF16)] * 2
        + ([pltpu.VMEM((LANES, n * length), F32)] if end else []),
        flops=10 * steps * BQ * n * length * 256,
        trans=steps * BQ * n * length,
        name="attend_back",
    )
    return out if end else (out[:m], out[m])


def input_grad_body(ids, *refs, dp, n):
    pieces, ws = refs[:n], refs[n : n + dp]
    cosine, sine, whole, send, keep = refs[n + dp :]
    me = ids[1]
    half = send.shape[0]
    step = 256
    lane = lax.broadcasted_iota(jnp.int32, (step, LANES), 1)
    for h, target in ((1, send), (0, keep)):
        for i in range(half // step):
            rows = slice(h * half + i * step, h * half + (i + 1) * step)
            there = slice(i * step, (i + 1) * step)
            dq = [p[there, :].astype(F32) for p in pieces]
            kv = [p[half + rows.start : half + rows.stop, :].astype(F32) for p in pieces]
            qt = unpack_pairs(me, dq, n, h, lane)
            kt = unpack_pairs(me, kv, n, 0, lane)
            vt = unpack_pairs(me, kv, n, 1, lane)
            back = [x * cosine[rows, :] - swap_halves(x, lane) * sine[rows, :] for x in qt + kt]
            low = jnp.concatenate(back + vt, axis=1).astype(BF16)
            whole[rows, :] = low
            col = 0
            for w in ws:
                size = w.shape[0]
                total = lax.dot_general(low, w[...], NT, preferred_element_type=F32)
                target[there, col : col + size] = total.astype(target.dtype)
                col += size


def normed_of(value):
    centered = value - jnp.mean(value, axis=-1, keepdims=True)
    inverse = lax.rsqrt(jnp.mean(centered * centered, axis=-1, keepdims=True) + 1e-05)
    return centered * inverse, inverse


def back_of(grad, normed, inverse, gain):
    scaled = grad * gain
    inner = (
        scaled
        - jnp.mean(scaled, axis=-1, keepdims=True)
        - normed * jnp.mean(scaled * normed, axis=-1, keepdims=True)
    )
    return inverse * inner


RB = 64
CB = 512


def spans(total, size):
    size = min(size, total)
    return [slice(i, i + size) for i in range(0, total, size)]


class Copies:
    def __init__(self, sems):
        self.sems, self.count, self.groups = sems, 0, {}

    def start(self, group, src, dst):
        copy = pltpu.make_async_copy(src, dst, self.sems.at[self.count])
        copy.start()
        self.count += 1
        self.groups.setdefault(group, []).append(copy)

    def wait(self, group):
        for copy in self.groups[group]:
            copy.wait()


def weight_copies(copies, wod, wi, tp, dp, heads, gains, wi_all, wd_all, x=None, tokens=None):
    hidden = wi[0].shape[1]
    cols = wi[0].shape[0]
    lw = wod[0].shape[0] - hidden - 16

    def small():
        for f in range(dp):
            src = wod[f].at[pl.ds(hidden + lw, 16), :]
            copies.start("small", src, gains.at[:, pl.ds(f * cols, cols)])
        for d in range(tp):
            for f in range(dp):
                src = wod[d * dp + f].at[pl.ds(hidden, lw), :]
                copies.start("small", src, heads.at[pl.ds(d * lw, lw), pl.ds(f * cols, cols)])
        if x is not None:
            copies.start("small", x.at[pl.ds(0, tokens.shape[0]), :], tokens)

    def large():
        for d in range(tp):
            for f in range(dp):
                copies.start(d, wi[d * dp + f], wi_all.at[d, pl.ds(f * cols, cols), :])
                src = wod[d * dp + f].at[pl.ds(0, hidden), :]
                copies.start(d, src, wd_all.at[d, :, pl.ds(f * cols, cols)])

    return small, large


def forward_body(*refs, tp, dp):
    received, cotangent, x = refs[:tp], refs[tp], refs[tp + 1]
    at = tp + 2
    wod, wi = refs[at : at + tp * dp], refs[at + tp * dp : at + 2 * tp * dp]
    at += 2 * tp * dp
    lows, out_low, slope, normed, inverse, second, terms = refs[at : at + 7]
    act = refs[at + 7 : at + 7 + tp]
    heads, gains, wi_all, wd_all, tokens, attended, acc, sems = refs[at + 7 + tp :]
    share, width = tokens.shape
    hidden = wi[0].shape[1]
    lw = received[0].shape[1]
    copies = Copies(sems)
    small, large = weight_copies(copies, wod, wi, tp, dp, heads, gains, wi_all, wd_all, x, tokens)
    small()
    large()
    for j in range(tp):
        attended[:, j * lw : (j + 1) * lw] = received[j][...]
    copies.wait("small")
    for c in spans(width, CB):
        mixed = jnp.dot(attended[...], heads[:, c], preferred_element_type=F32)
        acc[:, c] = mixed + tokens[:, c].astype(F32)
    gain = gains[...].astype(F32)
    for b in spans(share, RB):
        n, r = normed_of(acc[b, :])
        out = n * gain[0:1, :] + gain[1:2, :]
        acc[b, :] = out
        lows[b, :] = out.astype(BF16)
        normed[b, :] = n
        inverse[b, :] = jnp.broadcast_to(r, (r.shape[0], LANES))
    for d in range(tp):
        copies.wait(d)
        for c in spans(hidden, CB):
            h = jnp.dot(lows[:share, :], wi_all[d, :, c], preferred_element_type=F32)
            phi = 0.5 * (1.0 + lax.erf(h * SQRT_HALF))
            act[d][:, c] = (h * phi).astype(BF16)
            there = slice(d * hidden + c.start, d * hidden + c.stop)
            slope[:, there] = (phi + h * jnp.exp(-0.5 * h * h) * INV_SQRT_TAU).astype(BF16)
        for c in spans(width, CB):
            acc[:, c] += jnp.dot(act[d][...], wd_all[d, :, c], preferred_element_type=F32)
    sums = [jnp.zeros((1, width), F32)] * 2
    for b in spans(share, RB):
        n, r = normed_of(acc[b, :])
        out_low[b, :] = (n * gain[2:3, :] + gain[3:4, :]).astype(BF16)
        grad = cotangent[b, :].astype(F32)
        result = back_of(grad, n, r, gain[2:3, :])
        second[b, :] = result
        lows[share + b.start : share + b.stop, :] = result.astype(BF16)
        sums = [sums[0] + jnp.sum(grad * n, axis=0, keepdims=True), sums[1] + jnp.sum(grad, axis=0, keepdims=True)]
    terms[0:1, :], terms[1:2, :] = sums


def middle_scratch(tp, dp, lw, hidden, width, share):
    return [
        pltpu.VMEM((tp * lw, width), BF16),
        pltpu.VMEM((16, width), BF16),
        pltpu.VMEM((tp, width, hidden), BF16),
        pltpu.VMEM((tp, hidden, width), BF16),
    ]


ANY = pl.BlockSpec(memory_space=pl.ANY)


def forward(received, cotangent, x, wod, wi, tp, dp):
    (share, lw), (cols, hidden) = received[0].shape, wi[0].shape
    width = cols * dp
    outs = [
        shape((2 * share, width), BF16),
        shape((share, width), BF16),
        shape((share, tp * hidden), BF16),
        shape((share, width), F32),
        shape((share, LANES), F32),
        shape((share, width), F32),
        shape((2, width), F32),
    ]
    out = call(
        functools.partial(forward_body, tp=tp, dp=dp),
        outs + [shape((share, hidden), BF16)] * tp,
        *received,
        cotangent,
        x,
        *wod,
        *wi,
        in_specs=[FULL] * (tp + 1) + [ANY] * (1 + 2 * tp * dp),
        scratch=middle_scratch(tp, dp, lw, hidden, width, share)
        + [
            pltpu.VMEM((share, width), BF16),
            pltpu.VMEM((share, tp * lw), BF16),
            pltpu.VMEM((share, width), F32),
            pltpu.SemaphoreType.DMA((dp + tp * dp * 3 + 1,)),
        ],
        flops=2 * share * width * (tp * lw + 2 * tp * hidden),
        trans=3 * share * tp * hidden,
        name="forward",
    )
    return out[:7], out[7:]


def backward_body(*refs, tp, dp):
    lows, out_low, slope, normed, inverse, second, terms = refs[:7]
    wod, wi = refs[7 : 7 + tp * dp], refs[7 + tp * dp : 7 + 2 * tp * dp]
    at = 7 + 2 * tp * dp
    rows, first = refs[at], refs[at + 1]
    pre, grads = refs[at + 2 : at + 2 + tp], refs[at + 2 + tp : at + 2 + 2 * tp]
    heads, gains, wi_all, wd_all, acc, edge, sems = refs[at + 2 + 2 * tp :]
    share, width = out_low.shape
    hidden, lw = pre[0].shape[1], grads[0].shape[1]
    copies = Copies(sems)
    small, large = weight_copies(copies, wod, wi, tp, dp, heads, gains, wi_all, wd_all)
    large()
    small()
    acc[...] = second[...]
    for d in range(tp):
        copies.wait(d)
        for c in spans(hidden, CB):
            grad = lax.dot_general(lows[share:, :], wd_all[d, c, :], NT, preferred_element_type=F32)
            there = slice(d * hidden + c.start, d * hidden + c.stop)
            pre[d][:, c] = (grad * slope[:, there].astype(F32)).astype(BF16)
        for c in spans(width, CB):
            acc[:, c] += lax.dot_general(pre[d][...], wi_all[d, c, :], NT, preferred_element_type=F32)
    copies.wait("small")
    gain = gains[...].astype(F32)
    sums = [jnp.zeros((1, width), F32)] * 2
    for b in spans(share, RB):
        grad, n = acc[b, :], normed[b, :]
        result = back_of(grad, n, inverse[b, :1], gain[0:1, :])
        first[b, :] = result
        rows[b, :] = result.astype(BF16)
        sums = [sums[0] + jnp.sum(grad * n, axis=0, keepdims=True), sums[1] + jnp.sum(grad, axis=0, keepdims=True)]
    for j in range(tp):
        part = lax.dot_general(rows[:share, :], heads[j * lw : (j + 1) * lw, :], NT, preferred_element_type=F32)
        grads[j][...] = part.astype(BF16)
    rows[share : 2 * share, :] = out_low[...]
    edge[...] = jnp.zeros_like(edge)
    edge[0:1, :], edge[1:2, :] = sums
    edge[2:4, :] = terms[...]
    rows[2 * share :, :] = edge[...].astype(BF16)


def backward(forwarded, wod, wi, tp, dp, lw):
    cols, hidden = wi[0].shape
    share, width = forwarded[1].shape
    out = call(
        functools.partial(backward_body, tp=tp, dp=dp),
        [shape((2 * share + 16, width), BF16), shape((share, width), F32)]
        + [shape((share, hidden), BF16)] * tp
        + [shape((share, lw), BF16)] * tp,
        *forwarded,
        *wod,
        *wi,
        in_specs=[FULL] * 7 + [ANY] * (2 * tp * dp),
        scratch=middle_scratch(tp, dp, lw, hidden, width, share)
        + [
            pltpu.VMEM((share, width), F32),
            pltpu.VMEM((16, width), F32),
            pltpu.SemaphoreType.DMA((dp + tp * dp * 3,)),
        ],
        flops=2 * share * width * (tp * lw + 2 * tp * hidden),
        name="backward",
    )
    return out[0], out[1], out[2 : 2 + tp], out[2 + tp :]


def rotate_heads(values, angles, sign):
    half = HEAD // 2
    cosine = jnp.cos(angles)[:, None, :half]
    sine = sign * jnp.sin(angles)[:, None, :half]
    first, second = values[..., :half], values[..., half:]
    return jnp.concatenate([first * cosine - second * sine, second * cosine + first * sine], axis=-1)


def gathered_attention(tokens, weights, angles, docs):
    rows, width = tokens.shape[0], weights[0].shape[1]
    heads = width // HEAD
    scale = HEAD**-0.5

    def project(w):
        return jnp.dot(tokens, w, preferred_element_type=F32).reshape(rows, heads, HEAD)

    q = rotate_heads(project(weights[0]), angles, 1.0).astype(BF16)
    k = rotate_heads(project(weights[1]), angles, 1.0).astype(BF16)
    v = project(weights[2]).astype(BF16)
    keys = jnp.concatenate(gather(k, "ctx"))
    values = jnp.concatenate(gather(v, "ctx"))
    all_docs = jnp.concatenate(gather(docs, "ctx"))

    def masked():
        s = jnp.einsum("qhd,khd->hqk", q, keys, preferred_element_type=F32) * scale
        return jnp.where(docs[None, :, None] == all_docs[None, None, :], s, NEG_BIG)

    s = masked()
    top = jnp.max(s, axis=-1, keepdims=True)
    p = jnp.exp(s - top)
    total = jnp.sum(p, axis=-1)
    out = jnp.einsum("hqk,khd->qhd", p.astype(BF16), values, preferred_element_type=F32)
    out = out / total.T[..., None]
    log = top[..., 0] + jnp.log(total)

    def backward(grad):
        grad = grad.astype(BF16).reshape(rows, heads, HEAD)
        dot = jnp.sum(grad.astype(F32) * out, axis=-1).T
        p = jnp.exp(masked() - log[..., None])
        dv = jnp.einsum("hqk,qhd->khd", p.astype(BF16), grad, preferred_element_type=F32)
        dp = jnp.einsum("qhd,khd->hqk", grad, values, preferred_element_type=F32)
        ds = (p * (dp - dot[..., None])).astype(BF16)
        dq = jnp.einsum("hqk,khd->qhd", ds, keys, preferred_element_type=F32) * scale
        dk = jnp.einsum("hqk,qhd->khd", ds, q, preferred_element_type=F32) * scale

        def owned(value):
            half = value.shape[0] // 2
            keep, got = scatter(value[half:].astype(BF16), value[:half], "ctx", 0)
            return keep + got.astype(F32)

        dq = rotate_heads(dq, angles, -1.0)
        dk = rotate_heads(owned(dk), angles, -1.0)
        return jnp.concatenate([x.astype(BF16).reshape(rows, width) for x in (dq, dk, owned(dv))], axis=1)

    return out.astype(BF16).reshape(rows, width), backward


def body(
    layer_input,
    segments,
    positions,
    w_q,
    w_k,
    w_v,
    w_o,
    w_in,
    w_out,
    ln1_gain,
    ln1_bias,
    ln2_gain,
    ln2_bias,
    cotangent,
):
    LINE.clear()
    seqs, length, width = layer_input.shape
    assert seqs == 1
    tp, dp, ctx = lax.axis_size("tp"), lax.axis_size("dp"), lax.axis_size("ctx")
    lw, hidden = w_q.shape[1], w_in.shape[1]
    heads = lw // HEAD
    ids = jnp.stack([lax.axis_index("dp"), lax.axis_index("ctx"), lax.axis_index("tp")]).astype(jnp.int32)
    share = length // tp
    half = length // 2
    spread = heads == ctx and heads % 2 == 0 and half % BQ == 0 and tp % 2 == 0

    def exchange(parts, first=0):
        return [p if first + k == 0 else swap(p, "ctx", first + k) for k, p in enumerate(parts)]

    def exchange_tp(parts):
        return [p if d == 0 else swap(p, "tp", d) for d, p in zip(order(tp), parts)]

    def arrange_tokens(value):
        table = value.reshape(tp, share)
        picked = [lax.dynamic_index_in_dim(table, ids[2] ^ d, 0, keepdims=False) for d in order(tp)]
        return jnp.stack(picked).reshape(length)

    w_qkv = gather(jnp.concatenate([w_q, w_k, w_v], axis=1), "dp")
    vectors = jnp.stack([ln1_gain, ln1_bias, ln2_gain, ln2_bias])
    tall = jnp.concatenate([w_out, w_o, jnp.pad(vectors, ((0, 12), (0, 0)))])

    docs = arrange_tokens(segments.reshape(length))
    places = arrange_tokens(positions.reshape(length)).astype(F32)
    freq = 10000.0 ** (-(jnp.arange(LANES, dtype=jnp.int32) % (HEAD // 2)).astype(F32) * 2.0 / HEAD)
    angles = places[:, None] * freq[None, :]
    x = arrange(ids, layer_input.reshape(length, width), tp, dp, order(tp))

    if spread:
        side = jnp.where(jnp.arange(LANES) % HEAD < HEAD // 2, -1.0, 1.0)
        cosine, sine = step(lambda t: (jnp.cos(t), jnp.sin(t) * side[None, :]), angles)
        all_docs = jnp.concatenate([docs] + [swap(docs, "ctx", e) for e in range(1, ctx)])
        lane = jnp.arange(LANES)[None, :]
        in_docs = (lane >= HEAD) & (lane < HEAD + DOCS)
        folded = (lane >= HEAD + DOCS) & (lane < HEAD + DOCS + 3)

        kv = call(
            functools.partial(kv_body, dp=dp, n=heads),
            [shape((length, LANES), BF16)] * ctx,
            ids,
            x,
            *w_qkv,
            cosine,
            sine,
            in_specs=[SMEM] + [FULL] * (3 + dp),
            flops=4 * length * width * lw,
            name="project_kv",
        )
        wi, wod = gather_weight(after(w_in, kv[0])), gather_weight(after(tall, kv[0]))
        kv = exchange(kv)
        queries = call(
            functools.partial(q_body, dp=dp, n=heads),
            [shape((half, LANES), BF16)] * ctx,
            ids,
            x,
            *w_qkv,
            cosine,
            sine,
            in_specs=[SMEM] + [FULL] * (3 + dp),
            flops=2 * length * width * lw,
            name="project_q",
        )
        queries = exchange(queries)
        marks = step(lambda d: jnp.where(in_docs, lane - HEAD != d[:, None], folded).astype(BF16), all_docs)
        out_grad = arrange(ids, cotangent.reshape(length, width), tp, dp, [0])
        middle = ctx // 2
        groups = ((0, middle), (middle, ctx))
        outs, logs, mixed = [], [], []
        for lo, hi in groups:
            o, log = attend(queries[lo:hi], kv, marks, lo)
            outs.append(o)
            logs.append(log)
            mixed.extend(exchange(o, lo))
        attended = call(
            functools.partial(unpack_body, n=heads),
            [shape((share, lw), BF16)] * tp,
            ids,
            *mixed,
            in_specs=[SMEM] + [FULL] * ctx,
            name="unpack",
        )
    else:
        wi, wod = gather_weight(w_in), gather_weight(tall)
        out_grad = arrange(ids, cotangent.reshape(length, width), tp, dp, [0])
        joined = jnp.concatenate(w_qkv)
        mixed, attend_backward = gathered_attention(
            x, [joined[:, k * lw : (k + 1) * lw] for k in range(3)], angles, docs
        )
        attended = [mixed[j * share : (j + 1) * share] for j in range(tp)]

    received = exchange_tp(attended)
    forwarded, act = forward(received, out_grad, x, wod, wi, tp, dp)
    lows = gather(forwarded[0], "tp")
    act = exchange_tp(act)
    rows, first_grad, pre, grads = backward(forwarded, wod, wi, tp, dp, lw)
    grads = exchange_tp(grads)

    out_sum = GradSum(ids, 1, lambda start, size, *a: sum_over_rows(a[:tp], a[tp:], start, size))
    out_sum.operands = [*act, *[p[share:] for p in lows]]
    rows = gather(after(rows, grads[-1]), "tp")
    pre = exchange_tp([after(p, grads[-1]) for p in pre])

    filler = -(hidden + lw + 8) % (16 * ctx) + 8

    def product(start, size, *a):
        into = sum_over_rows(a[:tp], a[tp : 2 * tp], start, size)
        back = sum_over_rows(a[2 * tp : 3 * tp], a[3 * tp :], start, size)
        terms = sum(p[2 * share : 2 * share + 8, start : start + size].astype(F32) for p in a[3 * tp :])
        return jnp.concatenate([into, back, jnp.pad(terms, ((0, filler - 8), (0, 0)))])

    in_sum = GradSum(ids, 1, product)
    in_sum.operands = [*pre, *lows, *attended, *rows]

    if spread:
        out_sum.begin(width)
        packed = call(
            functools.partial(pack_body, tp=tp, n=heads),
            [shape((half, LANES), BF16)] * ctx,
            ids,
            *grads,
            in_specs=[SMEM] + [FULL] * tp,
            name="pack",
        )
        packed = exchange(packed)
        query_grads, carried = attend_back(
            queries[:middle], packed[:middle], outs[0], kv, logs[0], marks, None, None, 0, False
        )
        out_sum.over_dp()
        in_sum.begin(width)
        pieces = attend_back(
            queries[middle:], packed[middle:], outs[1], kv, logs[1], marks, carried, query_grads, middle, True
        )
        pieces = exchange(pieces)
        out_sum.over_ctx()
        in_sum.over_dp()
        output = place(ids, rows, tp, dp, length, share)
        whole, send, keep = call(
            functools.partial(input_grad_body, dp=dp, n=heads),
            [shape((length, 3 * lw), BF16), shape((half, width), BF16), shape((half, width), F32)],
            ids,
            *pieces,
            *w_qkv,
            cosine,
            sine,
            in_specs=[SMEM] + [FULL] * (ctx + dp + 2),
            flops=6 * length * width * lw,
            name="input_grad",
        )
    else:
        out_sum.begin(width)
        out_sum.over_dp()
        in_sum.begin(width)
        out_sum.over_ctx()
        in_sum.over_dp()
        output = place(ids, rows, tp, dp, length, share)
        whole = attend_backward(jnp.concatenate(grads))
        total = lax.dot_general(whole, joined, NT, preferred_element_type=F32)
        send, keep = total[half:].astype(BF16), total[:half]

    got = swap(send, "tp", 1)
    qkv_sum = GradSum(ids, 0, lambda start, size, l, r: over_rows(l[:, start : start + size], r))
    qkv_sum.operands = [x, whole]
    qkv_sum.begin(width)
    keep, got = scatter(None, keep, "tp", 0, got)
    in_sum.over_ctx()
    (w_out_grad,) = out_sum.columns([width // dp])
    low = step(lambda l, k, f: (f + k + l.astype(F32)).astype(BF16), got, keep, first_grad)
    low = gather(low, "tp")
    qkv_sum.over_dp()
    w_in_grad, w_o_grad, terms = in_sum.rows(hidden, lw)
    input_grad = place(ids, low, tp, dp, length)
    qkv_sum.over_ctx()
    w_q_grad, w_k_grad, w_v_grad = qkv_sum.columns([lw] * 3)
    return (
        output[None],
        input_grad[None],
        w_q_grad,
        w_k_grad,
        w_v_grad,
        w_o_grad,
        w_in_grad,
        w_out_grad,
        terms[0],
        terms[1],
        terms[2],
        terms[3],
    )


def solution(mesh):
    return jax.shard_map(
        body,
        mesh=mesh,
        in_specs=(
            P("dp", "ctx", None),
            P("dp", "ctx"),
            P("dp", "ctx"),
            P("dp", "tp"),
            P("dp", "tp"),
            P("dp", "tp"),
            P("tp", "dp"),
            P("dp", "tp"),
            P("tp", "dp"),
            P("dp"),
            P("dp"),
            P("dp"),
            P("dp"),
            P("dp", "ctx", None),
        ),
        out_specs=(
            P("dp", "ctx", None),
            P("dp", "ctx", None),
            P("dp", "tp"),
            P("dp", "tp"),
            P("dp", "tp"),
            P("tp", "dp"),
            P("dp", "tp"),
            P("tp", "dp"),
            P("dp"),
            P("dp"),
            P("dp"),
            P("dp"),
        ),
        check_vma=False,
    )
```

```python
import functools

import jax
import jax.numpy as jnp
from jax import lax
from jax.experimental import pallas as pl
from jax.experimental.pallas import tpu as pltpu
from jax.sharding import PartitionSpec as P

D = 1024
H = 16
HEAD = D // H
LANES = 128
DOCS = 17

NEG_BIG = -1e30
SQRT_HALF = 0.7071067811865476
INV_SQRT_TAU = 0.3989422804014327
LOG2E = 1.4426950408889634
LN2 = 0.6931471805599453
F32 = jnp.float32
BF16 = jnp.bfloat16
NT = (((1,), (1,)), ((), ()))
VMEM_LIMIT = 60 * 1024 * 1024


def order(n):
    found, bit = [0], n >> 1
    while bit:
        found = found + [d | bit for d in found]
        bit >>= 1
    return found


def swap(value, axis, bit):
    n = lax.axis_size(axis)
    return lax.ppermute(value, axis, [(i, i ^ bit) for i in range(n)])


def gather(value, axis):
    parts, bit = [value], lax.axis_size(axis) >> 1
    while bit:
        parts = parts + [swap(p, axis, bit) for p in parts]
        bit >>= 1
    return parts


def chips(value):
    parts, bit = [value], lax.axis_size("tp") >> 1
    while bit > 1:
        parts = parts + [swap(p, "tp", bit) for p in parts]
        bit >>= 1
    return parts


def cores(parts):
    return parts + [swap(p, "tp", 1) for p in parts]


def after(value, *others):
    return lax.optimization_barrier((value, *others))[0]


LINE = []


def in_line(value):
    return after(value, LINE[-1]) if LINE else value


def due(*values):
    LINE[:] = [after(LINE[-1], *jax.tree.leaves(values))]


def step(function, *args):
    result = function(in_line(args[0]), *args[1:])
    LINE[:] = [result[0] if isinstance(result, (list, tuple)) else result]
    return result


def part_of(value, dim, start, size):
    return lax.slice_in_dim(value, start, start + size, axis=dim)


def split_sum(got, keep, dim):
    half = keep.shape[dim] // 2
    upper = part_of(keep, dim, half, half) + part_of(got, dim, half, half).astype(F32)
    return upper.astype(BF16), part_of(keep, dim, 0, half) + part_of(got, dim, 0, half).astype(F32)


def scatter(send, keep, axis, dim, got=None):
    n, bit = lax.axis_size(axis), 1
    while True:
        got = swap(send, axis, bit) if got is None else got
        bit <<= 1
        if bit >= n:
            return keep, got
        send, keep = step(functools.partial(split_sum, dim=dim), got, keep)
        got = None


def call(body, out_shape, *args, grid=None, in_specs=None, out_specs=None, scratch=(), flops=0, trans=0, name=None):
    extra = {}
    if grid is not None:
        extra["grid"] = grid
    if in_specs is not None:
        extra["in_specs"] = in_specs
    if out_specs is not None:
        extra["out_specs"] = out_specs
    args = list(args)
    first = 1 if args[0].shape == (3,) else 0
    args[first] = in_line(args[first])
    result = pl.pallas_call(
        body,
        out_shape=out_shape,
        scratch_shapes=list(scratch),
        compiler_params=pltpu.CompilerParams(vmem_limit_bytes=VMEM_LIMIT),
        cost_estimate=pl.CostEstimate(flops=int(flops), bytes_accessed=1 << 24, transcendentals=int(trans)),
        name=name,
        **extra,
    )(*args)
    LINE[:] = [result[0] if isinstance(result, (list, tuple)) else result]
    return result


def shape(dims, dtype):
    return jax.ShapeDtypeStruct(dims, dtype)


SMEM = pl.BlockSpec(memory_space=pltpu.SMEM)
FULL = pl.BlockSpec(memory_space=pltpu.VMEM)


def whole_block(value):
    return pl.BlockSpec(value.shape, lambda i: (0,) * len(value.shape))


def arrange_body(ids, src, out, *, tp, dp, shares):
    rows, width = src.shape
    share, cols = rows // tp, width // dp
    for j, d in enumerate(shares):
        for e, f in enumerate(order(dp)):
            row = pl.multiple_of((ids[2] ^ d) * share, share)
            col = pl.multiple_of((ids[0] ^ f) * cols, cols)
            out[j * share : (j + 1) * share, e * cols : (e + 1) * cols] = src[pl.ds(row, share), pl.ds(col, cols)]


def arrange(ids, src, tp, dp, shares):
    rows = src.shape[0] // tp * len(shares)
    return call(
        functools.partial(arrange_body, tp=tp, dp=dp, shares=shares),
        shape((rows, src.shape[1]), src.dtype),
        ids,
        src,
        in_specs=[SMEM, FULL],
        name="arrange",
    )


def place_body(ids, *refs, tp, dp, first):
    *parts, out = refs
    rows, width = out.shape
    share, cols = rows // tp, width // dp
    for j, d in enumerate(order(tp)):
        for e, f in enumerate(order(dp)):
            row = pl.multiple_of((ids[2] ^ d) * share, share)
            col = pl.multiple_of((ids[0] ^ f) * cols, cols)
            block = parts[j][first : first + share, e * cols : (e + 1) * cols]
            out[pl.ds(row, share), pl.ds(col, cols)] = block.astype(F32)


def place(ids, parts, tp, dp, rows, first=0):
    return call(
        functools.partial(place_body, tp=tp, dp=dp, first=first),
        shape((rows, parts[0].shape[1]), F32),
        ids,
        *parts,
        in_specs=[SMEM] + [FULL] * len(parts),
        name="place",
    )


def halve_body(ids, got, keep, send, left, *, bit):
    rows = send.shape[0]
    mine = (ids[1] // bit) % 2
    at = pl.multiple_of((1 - mine) * rows, rows)
    send[...] = (keep[pl.ds(at, rows), :] + got[pl.ds(at, rows), :].astype(F32)).astype(BF16)
    at = pl.multiple_of(mine * rows, rows)
    left[...] = keep[pl.ds(at, rows), :] + got[pl.ds(at, rows), :].astype(F32)


def merge_body(got, keep, out):
    out[...] = (keep[...] + got[...].astype(F32)).astype(BF16)


def row_of(who, n, rows):
    at, bit, size = 0, 1, n * rows
    while bit < n:
        size //= 2
        at = at + ((who // bit) % 2) * size
        bit *= 2
    return pl.multiple_of(at, rows)


def product_body(*refs, tp):
    left, right = refs[:tp], refs[tp : 2 * tp]
    send, keep, tall, wide = refs[2 * tp :]
    share = left[0].shape[0]
    for j in range(tp):
        tall[j * share : (j + 1) * share, :] = left[j][...]
        wide[j * share : (j + 1) * share, :] = right[j][...]
    mid = send.shape[1]
    for c in spans(tall.shape[1], CB):
        total = over_rows(tall[:, c], wide[...])
        keep[c, :] = total[:, :mid]
        send[c, :] = total[:, mid:].astype(BF16)


def products_body(*refs, tp):
    pre, hidden, attended, rows = (refs[k * tp : (k + 1) * tp] for k in range(4))
    send, keep, tall, wide, thin, broad = refs[4 * tp :]
    share = pre[0].shape[0]
    mid = send.shape[1]
    terms = None
    for j in range(tp):
        there = slice(j * share, (j + 1) * share)
        tall[there, :] = pre[j][...]
        wide[there, :] = hidden[j][...]
        thin[there, :] = attended[j][...]
        broad[there, :] = rows[j][:share, :]
        term = rows[j][share:, :].astype(F32)
        terms = term if terms is None else terms + term
    at = 0
    for left, right in ((tall, wide), (thin, broad)):
        for c in spans(left.shape[1], CB):
            total = over_rows(left[:, c], right[...])
            size = total.shape[0]
            keep[at : at + size, :] = total[:, :mid]
            send[at : at + size, :] = total[:, mid:].astype(BF16)
            at += size
    keep[at : at + 16, :] = terms[:, :mid]
    send[at : at + 16, :] = terms[:, mid:].astype(BF16)
    at += 16
    if at < send.shape[0]:
        keep[at:, :] = jnp.zeros((send.shape[0] - at, mid), F32)
        send[at:, :] = jnp.zeros((send.shape[0] - at, mid), BF16)


def product(left, right):
    tp, (share, m), n = len(left), left[0].shape, right[0].shape[1]
    return call(
        functools.partial(product_body, tp=tp),
        [shape((m, n // 2), BF16), shape((m, n // 2), F32)],
        *left,
        *right,
        scratch=[pltpu.VMEM((tp * share, m), BF16), pltpu.VMEM((tp * share, n), BF16)],
        flops=2 * tp * share * m * n,
        name="product",
    )


def products(pre, hidden, attended, rows, ctx):
    tp, (share, m), n, lw = len(pre), pre[0].shape, hidden[0].shape[1], attended[0].shape[1]
    total = -(-(m + lw + 16) // (16 * ctx)) * 16 * ctx
    return call(
        functools.partial(products_body, tp=tp),
        [shape((total, n // 2), BF16), shape((total, n // 2), F32)],
        *pre,
        *hidden,
        *attended,
        *rows,
        scratch=[pltpu.VMEM((tp * share, w), BF16) for w in (m, n, lw, n)],
        flops=2 * tp * share * (m + lw) * n,
        name="products",
    )


def place_columns_body(ids, *refs, n, widths):
    parts, outs = refs[:n], refs[n:]
    rows = parts[0].shape[0]
    for e, part in zip(order(n), parts):
        at = row_of(ids[1] ^ e, n, rows)
        lane = 0
        for out, width in zip(outs, widths):
            out[pl.ds(at, rows), :] = part[:, lane : lane + width].astype(F32)
            lane += width


def place_rows_body(ids, *refs, n):
    parts, (first, second, terms, whole) = refs[:n], refs[n:]
    rows = parts[0].shape[0]
    for e, part in zip(order(n), parts):
        at = row_of(ids[1] ^ e, n, rows)
        whole[pl.ds(at, rows), :] = part[...].astype(F32)
    hidden, middle = first.shape[1], second.shape[0]
    first[...] = whole[:hidden, :].T
    second[...] = whole[hidden : hidden + middle, :]
    terms[...] = whole[hidden + middle : hidden + middle + 8, :]


class GradSum:
    def __init__(self, ids, dim, send, keep):
        self.ids, self.dim, self.keep = ids, dim, keep
        self.got = swap(send, "dp", 1)
        self.bit = 0

    def next(self):
        n = lax.axis_size("ctx")
        if self.bit == 0:
            self.keep, self.got = scatter(None, self.keep, "dp", self.dim, self.got)
        self.bit = max(1, 2 * self.bit)
        rows, cols = self.keep.shape
        if self.bit < n:
            send, self.keep = call(
                functools.partial(halve_body, bit=self.bit),
                [shape((rows // 2, cols), BF16), shape((rows // 2, cols), F32)],
                self.ids,
                self.got,
                self.keep,
                in_specs=[SMEM, FULL, FULL],
                name="halve",
            )
            self.got = swap(send, "ctx", self.bit)
        else:
            own = call(merge_body, shape((rows, cols), BF16), self.got, self.keep, name="merge")
            self.parts = gather(own, "ctx")

    def columns(self, widths):
        n = len(self.parts)
        rows = self.parts[0].shape[0] * n
        return call(
            functools.partial(place_columns_body, n=n, widths=widths),
            [shape((rows, w), F32) for w in widths],
            self.ids,
            *self.parts,
            in_specs=[SMEM] + [FULL] * n,
            name="place_columns",
        )

    def rows(self, hidden, middle):
        n = len(self.parts)
        rows, cols = self.parts[0].shape
        return call(
            functools.partial(place_rows_body, n=n),
            [shape((cols, hidden), F32), shape((middle, cols), F32), shape((8, cols), F32)],
            self.ids,
            *self.parts,
            in_specs=[SMEM] + [FULL] * n,
            scratch=[pltpu.VMEM((n * rows, cols), F32)],
            name="place_rows",
        )


def over_rows(left, right):
    return lax.dot_general(left, right, (((0,), (0,)), ((), ())), preferred_element_type=F32)


def swap_halves(tile, lane):
    return jnp.where(lane % HEAD < HEAD // 2, pltpu.roll(tile, LANES - HEAD // 2, 1), pltpu.roll(tile, HEAD // 2, 1))


def turn(tile):
    return pltpu.roll(tile, HEAD, 1)


def pick(me, values, index):
    chosen = values[index]
    for i in range(1, len(values)):
        chosen = jnp.where(me == i, values[i ^ index], chosen)
    return chosen


def rows_dot(x, pieces, start, size):
    total, at = None, 0
    for w in pieces:
        depth = w.shape[0]
        term = jnp.dot(x[:, at : at + depth], w[:, start : start + size], preferred_element_type=F32)
        total = term if total is None else total + term
        at += depth
    return total


def project_body(ids, x, *refs, dp, n):
    ws = refs[:dp]
    cosine, sine = refs[dp], refs[dp + 1]
    outs = refs[dp + 2 :]
    me = ids[1]
    step = 256
    length = x.shape[0]
    half = length // 2
    width = n * HEAD
    lane = lax.broadcasted_iota(jnp.int32, (step, LANES), 1)
    for i in range(half // step):
        sides = []
        for h in range(2):
            rows = slice(h * half + i * step, h * half + (i + 1) * step)
            total = rows_dot(x[rows, :], ws, 0, 3 * width)
            tiles = [total[:, t * LANES : (t + 1) * LANES] for t in range(3 * n // 2)]
            tiles = [
                tile * cosine[rows, :] + swap_halves(tile, lane) * sine[rows, :] if t < n else tile
                for t, tile in enumerate(tiles)
            ]
            heads, pairs = [], []
            for t in range(n // 2):
                qt, kt, vt = tiles[t] * (HEAD**-0.5 * LOG2E), tiles[n // 2 + t], tiles[n + t]
                pairs.append(jnp.where(lane < HEAD, kt, turn(vt)))
                pairs.append(jnp.where(lane < HEAD, turn(kt), vt))
                heads.extend([qt, turn(qt)] if h == 0 else [turn(qt), qt])
            sides.append(heads)
            for e in range(n):
                outs[e][rows, :] = pick(me, pairs, e).astype(BF16)
        packed = [jnp.where(lane < HEAD, lo, hi) for lo, hi in zip(*sides)]
        for e in range(n):
            outs[e][length + i * step : length + (i + 1) * step, :] = pick(me, packed, e).astype(BF16)


def unpack_pairs(me, packed, n, h, lane):
    tiles = []
    for t in range(n // 2):
        lo, hi = pick(me, packed, 2 * t), pick(me, packed, 2 * t + 1)
        if h == 0:
            tiles.append(jnp.where(lane < HEAD, lo, turn(hi)))
        else:
            tiles.append(jnp.where(lane < HEAD, turn(lo), hi))
    return tiles


def unpack_body(ids, *refs, n):
    packed, outs = refs[:n], refs[n:]
    half, share = packed[0].shape[0], outs[0].shape[0]
    lane = lax.broadcasted_iota(jnp.int32, (share, LANES), 1)
    for i in range(half // share):
        pieces = [p[i * share : (i + 1) * share, :].astype(F32) for p in packed]
        for h in range(2):
            tiles = unpack_pairs(ids[1], pieces, n, h, lane)
            out = outs[h * (half // share) + i]
            for t, tile in enumerate(tiles):
                out[:, t * LANES : (t + 1) * LANES] = tile.astype(BF16)


def pack_body(ids, *refs, tp, n):
    parts, outs = refs[:tp], refs[tp:]
    half, share = outs[0].shape[0], parts[0].shape[0]
    lane = lax.broadcasted_iota(jnp.int32, (share, LANES), 1)
    for i in range(half // share):
        sides = []
        for h in range(2):
            grad = parts[h * (half // share) + i]
            heads = []
            for t in range(n // 2):
                tile = grad[:, t * LANES : (t + 1) * LANES].astype(F32)
                heads.extend([tile, turn(tile)] if h == 0 else [turn(tile), tile])
            sides.append(heads)
        packed = [jnp.where(lane < HEAD, lo, hi) for lo, hi in zip(*sides)]
        for e in range(n):
            outs[e][i * share : (i + 1) * share, :] = pick(ids[1], packed, e).astype(BF16)


BQ = 256
KC = 1024


def fill_keys(kv, marks, ka, va):
    size = kv[0].shape[0] // 3 * 2
    lane = lax.broadcasted_iota(jnp.int32, (size, LANES), 1)
    ones = jnp.where(lane < 3, 1.0, 0.0).astype(BF16)
    for e, ref in enumerate(kv):
        rows = slice(e * size, (e + 1) * size)
        both = ref[:size, :]
        ka[rows, :] = jnp.where(lane < HEAD, both, marks[rows, :])
        va[rows, :] = jnp.where(lane < HEAD, ones, both)


def query_marks(marks, row, lane):
    there = (lane >= HEAD) & (lane < HEAD + DOCS)
    bias = (marks[pl.ds(row, BQ), :].astype(F32) - 1.0) * -NEG_BIG
    return jnp.where(there, bias, 0.0)


def block_of(i, half, length, first):
    block, h = i // 2, i % 2
    blocks = half // BQ
    token = (first + block // blocks) * length + h * half + (block % blocks) * BQ
    return pl.multiple_of(block * BQ, BQ), h, pl.multiple_of(token, BQ)


def attend_body(*refs, m, n, first):
    kv, marks = refs[:n], refs[n]
    outs, lse = refs[n + 1 : n + 1 + m], refs[n + 1 + m]
    qs, ka, va, os = refs[n + 2 + m :]
    half = kv[0].shape[0] // 3
    length = 2 * half
    i = pl.program_id(0)

    @pl.when(i == 0)
    def _():
        fill_keys(kv, marks, ka, va)
        for e in range(m):
            qs[e * half : (e + 1) * half, :] = kv[first + e][length:, :]

    at, h, token = block_of(i, half, length, first)
    lane = lax.broadcasted_iota(jnp.int32, (BQ, LANES), 1)
    q = qs[pl.ds(at, BQ), :].astype(F32)
    q = jnp.where(h == 1, turn(q), q)
    q = jnp.where(lane < HEAD, q, query_marks(marks, token, lane)).astype(BF16)
    scores, top = [], None
    for j in range(n * length // KC):
        s = lax.dot_general(q, ka[j * KC : (j + 1) * KC, :], NT, preferred_element_type=F32)
        scores.append(s)
        for t in range(KC // LANES):
            tile = s[:, t * LANES : (t + 1) * LANES]
            top = tile if top is None else jnp.maximum(top, tile)
    top = jnp.max(top, axis=1, keepdims=True)
    total = jnp.zeros((BQ, LANES), F32)
    for j, s in enumerate(scores):
        p = jnp.exp2(s - top).astype(BF16)
        total += jnp.dot(p, va[j * KC : (j + 1) * KC, :], preferred_element_type=F32)
    weight = total[:, :1]
    o = total / weight
    o = jnp.where(h == 0, turn(o), o)
    log = jnp.broadcast_to(top + jnp.log2(weight), (BQ, LANES))
    other = (lane < HEAD) & (h == 1)
    os[pl.ds(at, BQ), :] = jnp.where(other, os[pl.ds(at, BQ), :], o)
    lse[pl.ds(at, BQ), :] = jnp.where(other, lse[pl.ds(at, BQ), :], log)

    @pl.when(i == pl.num_programs(0) - 1)
    def _():
        for e in range(m):
            outs[e][...] = os[e * half : (e + 1) * half, :].astype(BF16)


def attend(kv, marks, first, m):
    n, half = len(kv), kv[0].shape[0] // 3
    length = 2 * half
    steps = m * 2 * half // BQ
    args = [*kv, marks]
    outs = [shape((half, LANES), BF16)] * m + [shape((m * half, LANES), F32)]
    out = call(
        functools.partial(attend_body, m=m, n=n, first=first),
        outs,
        *args,
        grid=(steps,),
        in_specs=[whole_block(a) for a in args],
        out_specs=[whole_block(o) for o in outs],
        scratch=[
            pltpu.VMEM((m * half, LANES), BF16),
            pltpu.VMEM((n * length, LANES), BF16),
            pltpu.VMEM((n * length, LANES), BF16),
            pltpu.VMEM((m * half, LANES), F32),
        ],
        flops=4 * steps * BQ * n * length * 256,
        trans=steps * BQ * n * length,
        name="attend",
    )
    return out[:m], out[m]


def split3(value):
    high = value.astype(BF16).astype(F32)
    rest = value - high
    middle = rest.astype(BF16).astype(F32)
    return high, middle, rest - middle


def attend_back_body(*refs, m, n, first, start, end):
    grads, outs = (refs[k * m : (k + 1) * m] for k in range(2))
    kv, lse, marks = refs[2 * m : 2 * m + n], refs[2 * m + n], refs[2 * m + n + 1]
    at = 2 * m + n + 2
    before = None
    if not start:
        before, at = refs[at], at + 1
    if end:
        earlier, at = refs[at : at + n - m], at + n - m
        results, at = refs[at : at + n], at + n
        qs, gs, os, ds_, ka, va, acc = refs[at:]
    else:
        dqs, at = refs[at : at + m], at + m
        acc, at = refs[at], at + 1
        qs, gs, os, ds_, ka, va = refs[at:]
    half = kv[0].shape[0] // 3
    length = 2 * half
    i = pl.program_id(0)

    @pl.when(i == 0)
    def _():
        fill_keys(kv, marks, ka, va)
        for e in range(m):
            rows = slice(e * half, (e + 1) * half)
            qs[rows, :] = kv[first + e][length:, :]
            gs[rows, :] = grads[e][...]
            os[rows, :] = outs[e][...]
        acc[...] = jnp.zeros_like(acc) if start else before[...]

    row, h, token = block_of(i, half, length, first)
    lane = lax.broadcasted_iota(jnp.int32, (BQ, LANES), 1)
    here = pl.ds(row, BQ)
    q = qs[here, :].astype(F32)
    g = gs[here, :].astype(F32)
    o = os[here, :].astype(F32)
    log = lse[here, :]
    q = jnp.where(h == 1, turn(q), q)
    g = jnp.where(h == 0, turn(g), g)
    o = jnp.where(h == 0, turn(o), o)
    log = jnp.where(h == 1, turn(log), log)[:, :1]
    dot = jnp.sum(jnp.where(lane >= HEAD, g * o, 0.0), axis=1, keepdims=True)
    b0, b1, b2 = split3(-log)
    q_marks = query_marks(marks, token, lane)
    first_lane = HEAD + DOCS
    qa = jnp.where(lane == first_lane, b0, q_marks)
    qa = jnp.where(lane == first_lane + 1, b1, qa)
    qa = jnp.where(lane == first_lane + 2, b2, qa)
    qa = jnp.where(lane < HEAD, q, qa).astype(BF16)
    b0, b1, b2 = split3(-dot)
    ga = jnp.where(lane == 0, b0, jnp.where(lane == 1, b1, jnp.where(lane == 2, b2, 0.0)))
    ga = jnp.where(lane >= HEAD, g, ga).astype(BF16)
    q_t = q.T[:HEAD].astype(BF16)
    g_t = g.T[HEAD:].astype(BF16)
    total = jnp.zeros((BQ, LANES), F32)
    for j in range(n * length // KC):
        cols = slice(j * KC, (j + 1) * KC)
        s = lax.dot_general(qa, ka[cols, :], NT, preferred_element_type=F32)
        t = lax.dot_general(ga, va[cols, :], NT, preferred_element_type=F32)
        p = jnp.exp2(s)
        ds = (p * t).astype(BF16)
        p = p.astype(BF16)
        acc[HEAD:, cols] += jnp.dot(g_t, p, preferred_element_type=F32)
        acc[:HEAD, cols] += jnp.dot(q_t, ds, preferred_element_type=F32)
        total += jnp.dot(ds, ka[cols, :], preferred_element_type=F32)
    total = total * (HEAD**-0.5)
    total = jnp.where(h == 1, turn(total), total)
    other = (lane < HEAD) & (h == 1)
    ds_[here, :] = jnp.where(other, ds_[here, :], total)

    @pl.when(i == pl.num_programs(0) - 1)
    def _():
        if not end:
            for e in range(m):
                dqs[e][...] = ds_[e * half : (e + 1) * half, :].astype(BF16)
        else:
            for e in range(n):
                if e < n - m:
                    results[e][:half, :] = earlier[e][...]
                else:
                    at = (e - n + m) * half
                    results[e][:half, :] = ds_[at : at + half, :].astype(BF16)
                cols = slice(e * length, (e + 1) * length)
                turned = acc[:, cols].T
                key_lane = lax.broadcasted_iota(jnp.int32, (length, LANES), 1)
                results[e][half:, :] = jnp.where(key_lane < HEAD, turned * LN2, turned).astype(BF16)


def attend_back(grads, outs, kv, lse, marks, before, earlier, first, end):
    m, n, half = len(grads), len(kv), kv[0].shape[0] // 3
    length = 2 * half
    steps = m * 2 * half // BQ
    start = before is None
    args = [*grads, *outs, *kv, lse, marks] + ([] if start else [before]) + (list(earlier) if end else [])
    if end:
        results = [shape((half + length, LANES), BF16)] * n
    else:
        results = [shape((half, LANES), BF16)] * m + [shape((LANES, n * length), F32)]
    out = call(
        functools.partial(attend_back_body, m=m, n=n, first=first, start=start, end=end),
        results,
        *args,
        grid=(steps,),
        in_specs=[whole_block(a) for a in args],
        out_specs=[whole_block(o) for o in results],
        scratch=[pltpu.VMEM((m * half, LANES), BF16)] * 3
        + [pltpu.VMEM((m * half, LANES), F32)]
        + [pltpu.VMEM((n * length, LANES), BF16)] * 2
        + ([pltpu.VMEM((LANES, n * length), F32)] if end else []),
        flops=10 * steps * BQ * n * length * 256,
        trans=steps * BQ * n * length,
        name="attend_back",
    )
    return out if end else (out[:m], out[m])


def input_grad_body(ids, *refs, dp, n):
    pieces, ws = refs[:n], refs[n : n + dp]
    cosine, sine, whole, send, keep = refs[n + dp :]
    me = ids[1]
    half = send.shape[0]
    step = 256
    lane = lax.broadcasted_iota(jnp.int32, (step, LANES), 1)
    for h, target in ((1, send), (0, keep)):
        for i in range(half // step):
            rows = slice(h * half + i * step, h * half + (i + 1) * step)
            there = slice(i * step, (i + 1) * step)
            dq = [p[there, :].astype(F32) for p in pieces]
            kv = [p[half + rows.start : half + rows.stop, :].astype(F32) for p in pieces]
            qt = unpack_pairs(me, dq, n, h, lane)
            kt = unpack_pairs(me, kv, n, 0, lane)
            vt = unpack_pairs(me, kv, n, 1, lane)
            back = [x * cosine[rows, :] - swap_halves(x, lane) * sine[rows, :] for x in qt + kt]
            low = jnp.concatenate(back + vt, axis=1).astype(BF16)
            whole[rows, :] = low
            col = 0
            for w in ws:
                size = w.shape[0]
                total = lax.dot_general(low, w[...], NT, preferred_element_type=F32)
                target[there, col : col + size] = total.astype(target.dtype)
                col += size


def normed_of(value):
    centered = value - jnp.mean(value, axis=-1, keepdims=True)
    inverse = lax.rsqrt(jnp.mean(centered * centered, axis=-1, keepdims=True) + 1e-05)
    return centered * inverse, inverse


def back_of(grad, normed, inverse, gain):
    scaled = grad * gain
    inner = (
        scaled
        - jnp.mean(scaled, axis=-1, keepdims=True)
        - normed * jnp.mean(scaled * normed, axis=-1, keepdims=True)
    )
    return inverse * inner


RB = 64
CB = 512


def spans(total, size):
    size = min(size, total)
    return [slice(i, i + size) for i in range(0, total, size)]


class Copies:
    def __init__(self, sems):
        self.sems, self.count, self.groups = sems, 0, {}

    def start(self, group, src, dst):
        copy = pltpu.make_async_copy(src, dst, self.sems.at[self.count])
        copy.start()
        self.count += 1
        self.groups.setdefault(group, []).append(copy)

    def wait(self, group):
        for copy in self.groups[group]:
            copy.wait()


def weight_copies(copies, wod, wi, tp, dp, heads, gains, wi_all, wd_all, x=None, tokens=None):
    hidden = wi[0].shape[1]
    cols = wi[0].shape[0]
    lw = wod[0].shape[0] - hidden - 16

    def small():
        for f in range(dp):
            src = wod[f].at[pl.ds(hidden + lw, 16), :]
            copies.start("small", src, gains.at[:, pl.ds(f * cols, cols)])
        for d in range(tp):
            for f in range(dp):
                src = wod[d * dp + f].at[pl.ds(hidden, lw), :]
                copies.start("small", src, heads.at[pl.ds(d * lw, lw), pl.ds(f * cols, cols)])
        if x is not None:
            copies.start("small", x.at[pl.ds(0, tokens.shape[0]), :], tokens)

    def large():
        for d in range(tp):
            for f in range(dp):
                copies.start(d, wi[d * dp + f], wi_all.at[d, pl.ds(f * cols, cols), :])
                src = wod[d * dp + f].at[pl.ds(0, hidden), :]
                copies.start(d, src, wd_all.at[d, :, pl.ds(f * cols, cols)])

    return small, large


def forward_body(*refs, tp, dp):
    received, cotangent, x = refs[:tp], refs[tp], refs[tp + 1]
    at = tp + 2
    wod, wi = refs[at : at + tp * dp], refs[at + tp * dp : at + 2 * tp * dp]
    at += 2 * tp * dp
    second_low, out_low, slope, normed, inverse, second, terms, lows = refs[at : at + 8]
    act = refs[at + 8 : at + 8 + tp]
    heads, gains, wi_all, wd_all, tokens, attended, acc, sems = refs[at + 8 + tp :]
    share, width = tokens.shape
    hidden = wi[0].shape[1]
    lw = received[0].shape[1]
    copies = Copies(sems)
    small, large = weight_copies(copies, wod, wi, tp, dp, heads, gains, wi_all, wd_all, x, tokens)
    small()
    large()
    for j in range(tp):
        attended[:, j * lw : (j + 1) * lw] = received[j][...]
    copies.wait("small")
    for c in spans(width, CB):
        mixed = jnp.dot(attended[...], heads[:, c], preferred_element_type=F32)
        acc[:, c] = mixed + tokens[:, c].astype(F32)
    gain = gains[...].astype(F32)
    for b in spans(share, RB):
        n, r = normed_of(acc[b, :])
        out = n * gain[0:1, :] + gain[1:2, :]
        acc[b, :] = out
        lows[b, :] = out.astype(BF16)
        normed[b, :] = n
        inverse[b, :] = jnp.broadcast_to(r, (r.shape[0], LANES))
    for d in range(tp):
        copies.wait(d)
        for c in spans(hidden, CB):
            h = jnp.dot(lows[...], wi_all[d, :, c], preferred_element_type=F32)
            phi = 0.5 * (1.0 + lax.erf(h * SQRT_HALF))
            act[d][:, c] = (h * phi).astype(BF16)
            there = slice(d * hidden + c.start, d * hidden + c.stop)
            slope[:, there] = (phi + h * jnp.exp(-0.5 * h * h) * INV_SQRT_TAU).astype(BF16)
        for c in spans(width, CB):
            acc[:, c] += jnp.dot(act[d][...], wd_all[d, :, c], preferred_element_type=F32)
    sums = [jnp.zeros((1, width), F32)] * 2
    for b in spans(share, RB):
        n, r = normed_of(acc[b, :])
        out_low[b, :] = (n * gain[2:3, :] + gain[3:4, :]).astype(BF16)
        grad = cotangent[b, :].astype(F32)
        result = back_of(grad, n, r, gain[2:3, :])
        second[b, :] = result
        second_low[b, :] = result.astype(BF16)
        sums = [sums[0] + jnp.sum(grad * n, axis=0, keepdims=True), sums[1] + jnp.sum(grad, axis=0, keepdims=True)]
    terms[0:1, :], terms[1:2, :] = sums


def middle_scratch(tp, dp, lw, hidden, width, share):
    return [
        pltpu.VMEM((tp * lw, width), BF16),
        pltpu.VMEM((16, width), BF16),
        pltpu.VMEM((tp, width, hidden), BF16),
        pltpu.VMEM((tp, hidden, width), BF16),
    ]


ANY = pl.BlockSpec(memory_space=pl.ANY)


def forward(received, cotangent, x, wod, wi, tp, dp):
    (share, lw), (cols, hidden) = received[0].shape, wi[0].shape
    width = cols * dp
    outs = [
        shape((share, width), BF16),
        shape((share, width), BF16),
        shape((share, tp * hidden), BF16),
        shape((share, width), F32),
        shape((share, LANES), F32),
        shape((share, width), F32),
        shape((2, width), F32),
        shape((share, width), BF16),
    ]
    out = call(
        functools.partial(forward_body, tp=tp, dp=dp),
        outs + [shape((share, hidden), BF16)] * tp,
        *received,
        cotangent,
        x,
        *wod,
        *wi,
        in_specs=[FULL] * (tp + 1) + [ANY] * (1 + 2 * tp * dp),
        scratch=middle_scratch(tp, dp, lw, hidden, width, share)
        + [
            pltpu.VMEM((share, width), BF16),
            pltpu.VMEM((share, tp * lw), BF16),
            pltpu.VMEM((share, width), F32),
            pltpu.SemaphoreType.DMA((dp + tp * dp * 3 + 1,)),
        ],
        flops=2 * share * width * (tp * lw + 2 * tp * hidden),
        trans=3 * share * tp * hidden,
        name="forward",
    )
    return out[:7], out[7], out[8:]


def backward_body(*refs, tp, dp):
    second_low, slope, normed, inverse, second, terms = refs[:6]
    wod, wi = refs[6 : 6 + tp * dp], refs[6 + tp * dp : 6 + 2 * tp * dp]
    at = 6 + 2 * tp * dp
    rows, first = refs[at], refs[at + 1]
    pre, grads = refs[at + 2 : at + 2 + tp], refs[at + 2 + tp : at + 2 + 2 * tp]
    heads, gains, wi_all, wd_all, acc, edge, sems = refs[at + 2 + 2 * tp :]
    share, width = second_low.shape
    hidden, lw = pre[0].shape[1], grads[0].shape[1]
    copies = Copies(sems)
    small, large = weight_copies(copies, wod, wi, tp, dp, heads, gains, wi_all, wd_all)
    large()
    small()
    acc[...] = second[...]
    for d in range(tp):
        copies.wait(d)
        for c in spans(hidden, CB):
            grad = lax.dot_general(second_low[...], wd_all[d, c, :], NT, preferred_element_type=F32)
            there = slice(d * hidden + c.start, d * hidden + c.stop)
            pre[d][:, c] = (grad * slope[:, there].astype(F32)).astype(BF16)
        for c in spans(width, CB):
            acc[:, c] += lax.dot_general(pre[d][...], wi_all[d, c, :], NT, preferred_element_type=F32)
    copies.wait("small")
    gain = gains[...].astype(F32)
    sums = [jnp.zeros((1, width), F32)] * 2
    for b in spans(share, RB):
        grad, n = acc[b, :], normed[b, :]
        result = back_of(grad, n, inverse[b, :1], gain[0:1, :])
        first[b, :] = result
        rows[b, :] = result.astype(BF16)
        sums = [sums[0] + jnp.sum(grad * n, axis=0, keepdims=True), sums[1] + jnp.sum(grad, axis=0, keepdims=True)]
    for j in range(tp):
        part = lax.dot_general(rows[:share, :], heads[j * lw : (j + 1) * lw, :], NT, preferred_element_type=F32)
        grads[j][...] = part.astype(BF16)
    edge[...] = jnp.zeros_like(edge)
    edge[0:1, :], edge[1:2, :] = sums
    edge[2:4, :] = terms[...]
    rows[share:, :] = edge[...].astype(BF16)


def backward(forwarded, wod, wi, tp, dp, lw):
    cols, hidden = wi[0].shape
    share, width = forwarded[0].shape
    out = call(
        functools.partial(backward_body, tp=tp, dp=dp),
        [shape((share + 16, width), BF16), shape((share, width), F32)]
        + [shape((share, hidden), BF16)] * tp
        + [shape((share, lw), BF16)] * tp,
        *forwarded,
        *wod,
        *wi,
        in_specs=[FULL] * 6 + [ANY] * (2 * tp * dp),
        scratch=middle_scratch(tp, dp, lw, hidden, width, share)
        + [
            pltpu.VMEM((share, width), F32),
            pltpu.VMEM((16, width), F32),
            pltpu.SemaphoreType.DMA((dp + tp * dp * 3,)),
        ],
        flops=2 * share * width * (tp * lw + 2 * tp * hidden),
        name="backward",
    )
    return out[0], out[1], out[2 : 2 + tp], out[2 + tp :]


def rotate_heads(values, angles, sign):
    half = HEAD // 2
    cosine = jnp.cos(angles)[:, None, :half]
    sine = sign * jnp.sin(angles)[:, None, :half]
    first, second = values[..., :half], values[..., half:]
    return jnp.concatenate([first * cosine - second * sine, second * cosine + first * sine], axis=-1)


def gathered_attention(tokens, weights, angles, docs):
    rows, width = tokens.shape[0], weights[0].shape[1]
    heads = width // HEAD
    scale = HEAD**-0.5

    def project(w):
        return jnp.dot(tokens, w, preferred_element_type=F32).reshape(rows, heads, HEAD)

    q = rotate_heads(project(weights[0]), angles, 1.0).astype(BF16)
    k = rotate_heads(project(weights[1]), angles, 1.0).astype(BF16)
    v = project(weights[2]).astype(BF16)
    keys = jnp.concatenate(gather(k, "ctx"))
    values = jnp.concatenate(gather(v, "ctx"))
    all_docs = jnp.concatenate(gather(docs, "ctx"))

    def masked():
        s = jnp.einsum("qhd,khd->hqk", q, keys, preferred_element_type=F32) * scale
        return jnp.where(docs[None, :, None] == all_docs[None, None, :], s, NEG_BIG)

    s = masked()
    top = jnp.max(s, axis=-1, keepdims=True)
    p = jnp.exp(s - top)
    total = jnp.sum(p, axis=-1)
    out = jnp.einsum("hqk,khd->qhd", p.astype(BF16), values, preferred_element_type=F32)
    out = out / total.T[..., None]
    log = top[..., 0] + jnp.log(total)

    def backward(grad):
        grad = grad.astype(BF16).reshape(rows, heads, HEAD)
        dot = jnp.sum(grad.astype(F32) * out, axis=-1).T
        p = jnp.exp(masked() - log[..., None])
        dv = jnp.einsum("hqk,qhd->khd", p.astype(BF16), grad, preferred_element_type=F32)
        dp = jnp.einsum("qhd,khd->hqk", grad, values, preferred_element_type=F32)
        ds = (p * (dp - dot[..., None])).astype(BF16)
        dq = jnp.einsum("hqk,khd->qhd", ds, keys, preferred_element_type=F32) * scale
        dk = jnp.einsum("hqk,qhd->khd", ds, q, preferred_element_type=F32) * scale

        def owned(value):
            half = value.shape[0] // 2
            keep, got = scatter(value[half:].astype(BF16), value[:half], "ctx", 0)
            return keep + got.astype(F32)

        dq = rotate_heads(dq, angles, -1.0)
        dk = rotate_heads(owned(dk), angles, -1.0)
        return jnp.concatenate([x.astype(BF16).reshape(rows, width) for x in (dq, dk, owned(dv))], axis=1)

    return out.astype(BF16).reshape(rows, width), backward


def body(
    layer_input,
    segments,
    positions,
    w_q,
    w_k,
    w_v,
    w_o,
    w_in,
    w_out,
    ln1_gain,
    ln1_bias,
    ln2_gain,
    ln2_bias,
    cotangent,
):
    LINE.clear()
    seqs, length, width = layer_input.shape
    assert seqs == 1
    tp, dp, ctx = lax.axis_size("tp"), lax.axis_size("dp"), lax.axis_size("ctx")
    lw, hidden = w_q.shape[1], w_in.shape[1]
    heads = lw // HEAD
    ids = jnp.stack([lax.axis_index("dp"), lax.axis_index("ctx"), lax.axis_index("tp")]).astype(jnp.int32)
    share = length // tp
    half = length // 2
    spread = heads == ctx and heads % 2 == 0 and half % BQ == 0 and tp % 2 == 0

    def exchange(parts, first=0):
        return [p if first + k == 0 else swap(p, "ctx", first + k) for k, p in enumerate(parts)]

    def exchange_tp(parts):
        return [p if d == 0 else swap(p, "tp", d) for d, p in zip(order(tp), parts)]

    def over_dp(parts):
        return [gather(p, "dp") for p in parts]

    def arrange_tokens(value):
        table = value.reshape(tp, share)
        picked = [lax.dynamic_index_in_dim(table, ids[2] ^ d, 0, keepdims=False) for d in order(tp)]
        return jnp.stack(picked).reshape(length)

    w_qkv = gather(step(lambda *w: jnp.concatenate(w, axis=1), w_q, w_k, w_v), "dp")
    vectors = jnp.stack([ln1_gain, ln1_bias, ln2_gain, ln2_bias])
    tall = chips(jnp.concatenate([w_out, w_o, jnp.pad(vectors, ((0, 12), (0, 0)))]))
    docs = arrange_tokens(segments.reshape(length))
    places = arrange_tokens(positions.reshape(length)).astype(F32)
    freq = 10000.0 ** (-(jnp.arange(LANES, dtype=jnp.int32) % (HEAD // 2)).astype(F32) * 2.0 / HEAD)
    angles = places[:, None] * freq[None, :]
    x = arrange(ids, layer_input.reshape(length, width), tp, dp, order(tp))

    if spread:
        all_docs = jnp.concatenate([docs] + [swap(docs, "ctx", e) for e in range(1, ctx)])
        side = jnp.where(jnp.arange(LANES) % HEAD < HEAD // 2, -1.0, 1.0)
        cosine, sine = step(lambda t: (jnp.cos(t), jnp.sin(t) * side[None, :]), angles)
        lane = jnp.arange(LANES)[None, :]
        in_docs = (lane >= HEAD) & (lane < HEAD + DOCS)
        folded = (lane >= HEAD + DOCS) & (lane < HEAD + DOCS + 3)
        marks = step(lambda d: jnp.where(in_docs, lane - HEAD != d[:, None], folded).astype(BF16), all_docs)
        due(w_qkv)
        wi = gather(in_line(w_in), "dp")
        kv = call(
            functools.partial(project_body, dp=dp, n=heads),
            [shape((length + half, LANES), BF16)] * ctx,
            ids,
            x,
            *w_qkv,
            cosine,
            sine,
            in_specs=[SMEM] + [FULL] * (3 + dp),
            flops=6 * length * width * lw,
            name="project",
        )
        kv = exchange(kv)
        out_grad = arrange(ids, cotangent.reshape(length, width), tp, dp, [0])
        due(tall, wi)
        out_grad = step(lambda v: v, out_grad)
        tall = over_dp([in_line(p) for p in tall])
        wi = [chips(in_line(p)) for p in wi]
        due(kv)
        middle = ctx // 2
        o, log = attend(kv, marks, 0, middle)
        outs, logs = [o], [log]
        mixed = exchange(o)
        due(wi, tall[: max(1, tp // 4)])
        wi = [list(p) for p in zip(*wi)]
        first_cores = [[swap(in_line(p), "tp", 1) for p in wi[k]] for k in range(len(wi))]
        o, log = attend(kv, marks, middle, ctx - middle)
        outs.append(o)
        logs.append(log)
        mixed.extend(exchange(o, middle))
        due(mixed, first_cores)
        wi = [q for p in wi + first_cores for q in p]
        attended = call(
            functools.partial(unpack_body, n=heads),
            [shape((share, lw), BF16)] * tp,
            ids,
            *mixed,
            in_specs=[SMEM] + [FULL] * ctx,
            name="unpack",
        )
        tall = [in_line(q) for p in tall for q in p]
    else:
        wi = [list(p) for p in zip(*[chips(p) for p in gather(w_in, "dp")])]
        wi = cores([q for p in wi for q in p])
        tall = [q for p in over_dp(tall) for q in p]
        out_grad = arrange(ids, cotangent.reshape(length, width), tp, dp, [0])
        joined = jnp.concatenate(w_qkv)
        mixed, attend_backward = gathered_attention(
            x, [joined[:, k * lw : (k + 1) * lw] for k in range(3)], angles, docs
        )
        attended = [mixed[j * share : (j + 1) * share] for j in range(tp)]

    received = exchange_tp(attended)
    tall = cores(tall)
    forwarded, hidden_low, act = forward(received, out_grad, x, tall, wi, tp, dp)
    second_low, out_low, *forwarded = forwarded
    act = list(act)
    for j, d in enumerate(order(tp)):
        if d in (1, tp // 2):
            act[j] = swap(act[j], "tp", d)
    rows, first_grad, pre, grads = backward([second_low, *forwarded], tall, wi, tp, dp, lw)
    due([act[j] for j, d in enumerate(order(tp)) if d in (1, tp // 2)])
    grads = exchange_tp([in_line(g) for g in grads])

    if spread:
        packed = call(
            functools.partial(pack_body, tp=tp, n=heads),
            [shape((half, LANES), BF16)] * ctx,
            ids,
            *grads,
            in_specs=[SMEM] + [FULL] * tp,
            name="pack",
        )
        packed = exchange(packed)
        due(packed[:middle])

    second_low = chips(in_line(second_low))
    for j, d in enumerate(order(tp)):
        if d not in (0, 1, tp // 2):
            act[j] = swap(in_line(act[j]), "tp", d)
    hidden_low = chips(in_line(hidden_low))
    if spread:
        query_grads, carried = attend_back(
            packed[:middle], outs[0], kv, logs[0], marks, None, None, 0, False
        )
        due(packed, second_low, act)
    second_low = cores(second_low)
    out_sum = GradSum(ids, 1, *product(act, second_low))
    rows = chips(in_line(rows))
    pre = list(pre)
    for j, d in enumerate(order(tp)):
        if d > 1:
            pre[j] = swap(in_line(pre[j]), "tp", d)
    if spread:
        due(hidden_low)
        pieces = attend_back(
            packed[middle:], outs[1], kv, logs[1], marks, carried, query_grads, middle, True
        )
        due(rows, pre, out_sum.got)
        pieces = exchange(pieces)
    hidden_low = cores(hidden_low)
    rows = cores(rows)
    pre[order(tp).index(1)] = swap(pre[order(tp).index(1)], "tp", 1)
    in_sum = GradSum(ids, 1, *products(pre, hidden_low, attended, rows, ctx))
    out_low = chips(in_line(out_low))
    out_sum.next()
    if spread:
        due(pieces)
        whole, send, keep = call(
            functools.partial(input_grad_body, dp=dp, n=heads),
            [shape((length, 3 * lw), BF16), shape((half, width), BF16), shape((half, width), F32)],
            ids,
            *pieces,
            *w_qkv,
            cosine,
            sine,
            in_specs=[SMEM] + [FULL] * (ctx + dp + 2),
            flops=6 * length * width * lw,
            name="input_grad",
        )
    else:
        whole = attend_backward(jnp.concatenate(grads))
        total = lax.dot_general(whole, joined, NT, preferred_element_type=F32)
        send, keep = total[half:].astype(BF16), total[:half]
    got = swap(send, "tp", 1)
    mid = width // 2
    send = step(lambda l, r: over_rows(l[:, mid:], r).astype(BF16), x, whole)
    qkv_sum = GradSum(ids, 0, send, step(lambda l, r: over_rows(l[:, :mid], r), x, whole))
    keep, got = scatter(None, keep, "tp", 0, got)
    in_sum.next()
    out_sum.next()
    output = place(ids, cores(out_low), tp, dp, length)
    low = step(lambda l, k, f: (f + k + l.astype(F32)).astype(BF16), got, keep, first_grad)
    low = chips(low)
    qkv_sum.next()
    in_sum.next()
    out_sum.next()
    qkv_sum.next()
    in_sum.next()
    input_grad = place(ids, cores(low), tp, dp, length)
    qkv_sum.next()
    (w_out_grad,) = out_sum.columns([width // dp])
    w_in_grad, w_o_grad, terms = in_sum.rows(hidden, lw)
    w_q_grad, w_k_grad, w_v_grad = qkv_sum.columns([lw] * 3)
    return (
        output[None],
        input_grad[None],
        w_q_grad,
        w_k_grad,
        w_v_grad,
        w_o_grad,
        w_in_grad,
        w_out_grad,
        terms[0],
        terms[1],
        terms[2],
        terms[3],
    )


def solution(mesh):
    return jax.shard_map(
        body,
        mesh=mesh,
        in_specs=(
            P("dp", "ctx", None),
            P("dp", "ctx"),
            P("dp", "ctx"),
            P("dp", "tp"),
            P("dp", "tp"),
            P("dp", "tp"),
            P("tp", "dp"),
            P("dp", "tp"),
            P("tp", "dp"),
            P("dp"),
            P("dp"),
            P("dp"),
            P("dp"),
            P("dp", "ctx", None),
        ),
        out_specs=(
            P("dp", "ctx", None),
            P("dp", "ctx", None),
            P("dp", "tp"),
            P("dp", "tp"),
            P("dp", "tp"),
            P("tp", "dp"),
            P("dp", "tp"),
            P("tp", "dp"),
            P("dp"),
            P("dp"),
            P("dp"),
            P("dp"),
        ),
        check_vma=False,
    )
```

```python
import functools

import jax
import jax.numpy as jnp
from jax import lax
from jax.experimental import pallas as pl
from jax.experimental.pallas import tpu as pltpu
from jax.sharding import PartitionSpec as P

D = 1024
H = 16
HEAD = D // H
LANES = 128
DOCS = 17

NEG_BIG = -1e30
SQRT_HALF = 0.7071067811865476
INV_SQRT_TAU = 0.3989422804014327
LOG2E = 1.4426950408889634
LN2 = 0.6931471805599453
F32 = jnp.float32
BF16 = jnp.bfloat16
NT = (((1,), (1,)), ((), ()))
VMEM_LIMIT = 60 * 1024 * 1024


def order(n):
    found, bit = [0], n >> 1
    while bit:
        found = found + [d | bit for d in found]
        bit >>= 1
    return found


def swap(value, axis, bit):
    n = lax.axis_size(axis)
    return lax.ppermute(value, axis, [(i, i ^ bit) for i in range(n)])


def gather(value, axis):
    parts, bit = [value], lax.axis_size(axis) >> 1
    while bit:
        parts = parts + [swap(p, axis, bit) for p in parts]
        bit >>= 1
    return parts


def chips(value):
    parts, bit = [value], lax.axis_size("tp") >> 1
    while bit > 1:
        parts = parts + [swap(p, "tp", bit) for p in parts]
        bit >>= 1
    return parts


def cores(parts):
    return parts + [swap(p, "tp", 1) for p in parts]


def after(value, *others):
    return lax.optimization_barrier((value, *others))[0]


LINE = []


def in_line(value):
    return after(value, *LINE) if LINE else value


def due(*values):
    LINE.extend(jax.tree.leaves(values))


def step(function, *args):
    result = function(in_line(args[0]), *args[1:])
    LINE[:] = [result[0] if isinstance(result, (list, tuple)) else result]
    return result


def part_of(value, dim, start, size):
    return lax.slice_in_dim(value, start, start + size, axis=dim)


def split_sum(got, keep, dim):
    half = keep.shape[dim] // 2
    upper = part_of(keep, dim, half, half) + part_of(got, dim, half, half).astype(F32)
    return upper.astype(BF16), part_of(keep, dim, 0, half) + part_of(got, dim, 0, half).astype(F32)


def scatter(send, keep, axis, dim, got=None):
    n, bit = lax.axis_size(axis), 1
    while True:
        got = swap(send, axis, bit) if got is None else got
        bit <<= 1
        if bit >= n:
            return keep, got
        send, keep = step(functools.partial(split_sum, dim=dim), got, keep)
        got = None


def call(body, out_shape, *args, grid=None, in_specs=None, out_specs=None, scratch=(), flops=0, trans=0, name=None):
    extra = {}
    if grid is not None:
        extra["grid"] = grid
    if in_specs is not None:
        extra["in_specs"] = in_specs
    if out_specs is not None:
        extra["out_specs"] = out_specs
    args = list(args)
    first = 1 if args[0].shape == (3,) else 0
    args[first] = in_line(args[first])
    result = pl.pallas_call(
        body,
        out_shape=out_shape,
        scratch_shapes=list(scratch),
        compiler_params=pltpu.CompilerParams(vmem_limit_bytes=VMEM_LIMIT),
        cost_estimate=pl.CostEstimate(flops=1, bytes_accessed=1, transcendentals=0),
        name=name,
        **extra,
    )(*args)
    LINE[:] = [result[0] if isinstance(result, (list, tuple)) else result]
    return result


def shape(dims, dtype):
    return jax.ShapeDtypeStruct(dims, dtype)


SMEM = pl.BlockSpec(memory_space=pltpu.SMEM)
FULL = pl.BlockSpec(memory_space=pltpu.VMEM)


def whole_block(value):
    return pl.BlockSpec(value.shape, lambda i: (0,) * len(value.shape))


def arrange_body(ids, src, out, *, tp, dp, shares):
    rows, width = src.shape
    share, cols = rows // tp, width // dp
    for j, d in enumerate(shares):
        for e, f in enumerate(order(dp)):
            row = pl.multiple_of((ids[2] ^ d) * share, share)
            col = pl.multiple_of((ids[0] ^ f) * cols, cols)
            out[j * share : (j + 1) * share, e * cols : (e + 1) * cols] = src[pl.ds(row, share), pl.ds(col, cols)]


def arrange(ids, src, tp, dp, shares):
    rows = src.shape[0] // tp * len(shares)
    return call(
        functools.partial(arrange_body, tp=tp, dp=dp, shares=shares),
        shape((rows, src.shape[1]), src.dtype),
        ids,
        src,
        in_specs=[SMEM, FULL],
        name="arrange",
    )


def place_body(ids, *refs, tp, dp, first):
    *parts, out = refs
    rows, width = out.shape
    share, cols = rows // tp, width // dp
    for j, d in enumerate(order(tp)):
        for e, f in enumerate(order(dp)):
            row = pl.multiple_of((ids[2] ^ d) * share, share)
            col = pl.multiple_of((ids[0] ^ f) * cols, cols)
            block = parts[j][first : first + share, e * cols : (e + 1) * cols]
            out[pl.ds(row, share), pl.ds(col, cols)] = block.astype(F32)


def place(ids, parts, tp, dp, rows, first=0):
    return call(
        functools.partial(place_body, tp=tp, dp=dp, first=first),
        shape((rows, parts[0].shape[1]), F32),
        ids,
        *parts,
        in_specs=[SMEM] + [FULL] * len(parts),
        name="place",
    )


def halve_body(ids, got, keep, send, left, *, bit):
    rows = send.shape[0]
    mine = (ids[1] // bit) % 2
    at = pl.multiple_of((1 - mine) * rows, rows)
    send[...] = (keep[pl.ds(at, rows), :] + got[pl.ds(at, rows), :].astype(F32)).astype(BF16)
    at = pl.multiple_of(mine * rows, rows)
    left[...] = keep[pl.ds(at, rows), :] + got[pl.ds(at, rows), :].astype(F32)


def merge_body(got, keep, out):
    out[...] = (keep[...] + got[...].astype(F32)).astype(BF16)


def row_of(who, n, rows):
    at, bit, size = 0, 1, n * rows
    while bit < n:
        size //= 2
        at = at + ((who // bit) % 2) * size
        bit *= 2
    return pl.multiple_of(at, rows)


def product_body(*refs, tp):
    left, right = refs[:tp], refs[tp : 2 * tp]
    send, keep, tall, wide = refs[2 * tp :]
    share = left[0].shape[0]
    for j in range(tp):
        tall[j * share : (j + 1) * share, :] = left[j][...]
        wide[j * share : (j + 1) * share, :] = right[j][...]
    mid = send.shape[1]
    for c in spans(tall.shape[1], CB):
        total = over_rows(tall[:, c], wide[...])
        keep[c, :] = total[:, :mid]
        send[c, :] = total[:, mid:].astype(BF16)


def products_body(*refs, tp):
    pre, hidden, attended, rows = (refs[k * tp : (k + 1) * tp] for k in range(4))
    send, keep, tall, wide, thin, broad = refs[4 * tp :]
    share = pre[0].shape[0]
    mid = send.shape[1]
    terms = None
    for j in range(tp):
        there = slice(j * share, (j + 1) * share)
        tall[there, :] = pre[j][...]
        wide[there, :] = hidden[j][...]
        thin[there, :] = attended[j][...]
        broad[there, :] = rows[j][:share, :]
        term = rows[j][share:, :].astype(F32)
        terms = term if terms is None else terms + term
    at = 0
    for left, right in ((tall, wide), (thin, broad)):
        for c in spans(left.shape[1], CB):
            total = over_rows(left[:, c], right[...])
            size = total.shape[0]
            keep[at : at + size, :] = total[:, :mid]
            send[at : at + size, :] = total[:, mid:].astype(BF16)
            at += size
    keep[at : at + 16, :] = terms[:, :mid]
    send[at : at + 16, :] = terms[:, mid:].astype(BF16)
    at += 16
    if at < send.shape[0]:
        keep[at:, :] = jnp.zeros((send.shape[0] - at, mid), F32)
        send[at:, :] = jnp.zeros((send.shape[0] - at, mid), BF16)


def product(left, right):
    tp, (share, m), n = len(left), left[0].shape, right[0].shape[1]
    return call(
        functools.partial(product_body, tp=tp),
        [shape((m, n // 2), BF16), shape((m, n // 2), F32)],
        *left,
        *right,
        scratch=[pltpu.VMEM((tp * share, m), BF16), pltpu.VMEM((tp * share, n), BF16)],
        flops=2 * tp * share * m * n,
        name="product",
    )


def products(pre, hidden, attended, rows, ctx):
    tp, (share, m), n, lw = len(pre), pre[0].shape, hidden[0].shape[1], attended[0].shape[1]
    total = -(-(m + lw + 16) // (16 * ctx)) * 16 * ctx
    return call(
        functools.partial(products_body, tp=tp),
        [shape((total, n // 2), BF16), shape((total, n // 2), F32)],
        *pre,
        *hidden,
        *attended,
        *rows,
        scratch=[pltpu.VMEM((tp * share, w), BF16) for w in (m, n, lw, n)],
        flops=2 * tp * share * (m + lw) * n,
        name="products",
    )


def place_columns_body(ids, *refs, n, widths):
    parts, outs = refs[:n], refs[n:]
    rows = parts[0].shape[0]
    for e, part in zip(order(n), parts):
        at = row_of(ids[1] ^ e, n, rows)
        lane = 0
        for out, width in zip(outs, widths):
            out[pl.ds(at, rows), :] = part[:, lane : lane + width].astype(F32)
            lane += width


def place_rows_body(ids, *refs, n):
    parts, (first, second, terms, whole) = refs[:n], refs[n:]
    rows = parts[0].shape[0]
    for e, part in zip(order(n), parts):
        at = row_of(ids[1] ^ e, n, rows)
        whole[pl.ds(at, rows), :] = part[...].astype(F32)
    hidden, middle = first.shape[1], second.shape[0]
    first[...] = whole[:hidden, :].T
    second[...] = whole[hidden : hidden + middle, :]
    terms[...] = whole[hidden + middle : hidden + middle + 8, :]


class GradSum:
    def __init__(self, ids, dim, send, keep):
        self.ids, self.dim, self.keep = ids, dim, keep
        self.got = swap(send, "dp", 1)
        self.bit = 0

    def halve(self):
        if self.bit == 0:
            self.keep, self.got = scatter(None, self.keep, "dp", self.dim, self.got)
        self.bit = max(1, 2 * self.bit)
        rows, cols = self.keep.shape
        send, self.keep = call(
            functools.partial(halve_body, bit=self.bit),
            [shape((rows // 2, cols), BF16), shape((rows // 2, cols), F32)],
            self.ids,
            self.got,
            self.keep,
            in_specs=[SMEM, FULL, FULL],
            name="halve",
        )
        self.got = swap(send, "ctx", self.bit)

    def merge(self):
        while 2 * self.bit < lax.axis_size("ctx"):
            self.halve()
        self.parts = [call(merge_body, shape(self.keep.shape, BF16), self.got, self.keep, name="merge")]
        bit = self.bit
        while bit > 1:
            self.parts = self.parts + [swap(p, "ctx", bit) for p in self.parts]
            bit >>= 1

    def last(self):
        due(self.parts)
        self.parts = self.parts + [swap(p, "ctx", 1) for p in [in_line(p) for p in self.parts]]

    def columns(self, widths):
        n = len(self.parts)
        rows = self.parts[0].shape[0] * n
        return call(
            functools.partial(place_columns_body, n=n, widths=widths),
            [shape((rows, w), F32) for w in widths],
            self.ids,
            *self.parts,
            in_specs=[SMEM] + [FULL] * n,
            name="place_columns",
        )

    def rows(self, hidden, middle):
        n = len(self.parts)
        rows, cols = self.parts[0].shape
        return call(
            functools.partial(place_rows_body, n=n),
            [shape((cols, hidden), F32), shape((middle, cols), F32), shape((8, cols), F32)],
            self.ids,
            *self.parts,
            in_specs=[SMEM] + [FULL] * n,
            scratch=[pltpu.VMEM((n * rows, cols), F32)],
            name="place_rows",
        )


def over_rows(left, right):
    return lax.dot_general(left, right, (((0,), (0,)), ((), ())), preferred_element_type=F32)


def swap_halves(tile, lane):
    return jnp.where(lane % HEAD < HEAD // 2, pltpu.roll(tile, LANES - HEAD // 2, 1), pltpu.roll(tile, HEAD // 2, 1))


def turn(tile):
    return pltpu.roll(tile, HEAD, 1)


def pick(me, values, index):
    chosen = values[index]
    for i in range(1, len(values)):
        chosen = jnp.where(me == i, values[i ^ index], chosen)
    return chosen


def rows_dot(x, pieces, start, size):
    total, at = None, 0
    for w in pieces:
        depth = w.shape[0]
        term = jnp.dot(x[:, at : at + depth], w[:, start : start + size], preferred_element_type=F32)
        total = term if total is None else total + term
        at += depth
    return total


def project_body(ids, x, *refs, dp, n):
    ws = refs[:dp]
    cosine, sine = refs[dp], refs[dp + 1]
    outs = refs[dp + 2 :]
    me = ids[1]
    step = 256
    length = x.shape[0]
    half = length // 2
    width = n * HEAD
    lane = lax.broadcasted_iota(jnp.int32, (step, LANES), 1)
    for i in range(half // step):
        sides = []
        for h in range(2):
            rows = slice(h * half + i * step, h * half + (i + 1) * step)
            total = rows_dot(x[rows, :], ws, 0, 3 * width)
            tiles = [total[:, t * LANES : (t + 1) * LANES] for t in range(3 * n // 2)]
            tiles = [
                tile * cosine[rows, :] + swap_halves(tile, lane) * sine[rows, :] if t < n else tile
                for t, tile in enumerate(tiles)
            ]
            heads, pairs = [], []
            for t in range(n // 2):
                qt, kt, vt = tiles[t] * (HEAD**-0.5 * LOG2E), tiles[n // 2 + t], tiles[n + t]
                pairs.append(jnp.where(lane < HEAD, kt, turn(vt)))
                pairs.append(jnp.where(lane < HEAD, turn(kt), vt))
                heads.extend([qt, turn(qt)] if h == 0 else [turn(qt), qt])
            sides.append(heads)
            for e in range(n):
                outs[e][rows, :] = pick(me, pairs, e).astype(BF16)
        packed = [jnp.where(lane < HEAD, lo, hi) for lo, hi in zip(*sides)]
        for e in range(n):
            outs[e][length + i * step : length + (i + 1) * step, :] = pick(me, packed, e).astype(BF16)


def unpack_pairs(me, packed, n, h, lane):
    tiles = []
    for t in range(n // 2):
        lo, hi = pick(me, packed, 2 * t), pick(me, packed, 2 * t + 1)
        if h == 0:
            tiles.append(jnp.where(lane < HEAD, lo, turn(hi)))
        else:
            tiles.append(jnp.where(lane < HEAD, turn(lo), hi))
    return tiles


def unpack_body(ids, *refs, n):
    packed, outs = refs[:n], refs[n:]
    half, share = packed[0].shape[0], outs[0].shape[0]
    lane = lax.broadcasted_iota(jnp.int32, (share, LANES), 1)
    for i in range(half // share):
        pieces = [p[i * share : (i + 1) * share, :].astype(F32) for p in packed]
        for h in range(2):
            tiles = unpack_pairs(ids[1], pieces, n, h, lane)
            out = outs[h * (half // share) + i]
            for t, tile in enumerate(tiles):
                out[:, t * LANES : (t + 1) * LANES] = tile.astype(BF16)


def pack_body(ids, *refs, tp, n):
    parts, outs = refs[:tp], refs[tp:]
    half, share = outs[0].shape[0], parts[0].shape[0]
    lane = lax.broadcasted_iota(jnp.int32, (share, LANES), 1)
    for i in range(half // share):
        sides = []
        for h in range(2):
            grad = parts[h * (half // share) + i]
            heads = []
            for t in range(n // 2):
                tile = grad[:, t * LANES : (t + 1) * LANES].astype(F32)
                heads.extend([tile, turn(tile)] if h == 0 else [turn(tile), tile])
            sides.append(heads)
        packed = [jnp.where(lane < HEAD, lo, hi) for lo, hi in zip(*sides)]
        for e in range(n):
            outs[e][i * share : (i + 1) * share, :] = pick(ids[1], packed, e).astype(BF16)


BQ = 256
KC = 1024


def fill_keys(kv, marks, ka, va):
    size = kv[0].shape[0] // 3 * 2
    lane = lax.broadcasted_iota(jnp.int32, (size, LANES), 1)
    ones = jnp.where(lane < 3, 1.0, 0.0).astype(BF16)
    for e, ref in enumerate(kv):
        rows = slice(e * size, (e + 1) * size)
        both = ref[:size, :]
        ka[rows, :] = jnp.where(lane < HEAD, both, marks[rows, :])
        va[rows, :] = jnp.where(lane < HEAD, ones, both)


def query_marks(marks, row, lane):
    there = (lane >= HEAD) & (lane < HEAD + DOCS)
    bias = (marks[pl.ds(row, BQ), :].astype(F32) - 1.0) * -NEG_BIG
    return jnp.where(there, bias, 0.0)


def block_of(i, half, length, first):
    block, h = i // 2, i % 2
    blocks = half // BQ
    token = (first + block // blocks) * length + h * half + (block % blocks) * BQ
    return pl.multiple_of(block * BQ, BQ), h, pl.multiple_of(token, BQ)


def attend_body(*refs, m, n, first):
    kv, marks = refs[:n], refs[n]
    outs, lse = refs[n + 1 : n + 1 + m], refs[n + 1 + m]
    qs, ka, va, os = refs[n + 2 + m :]
    half = kv[0].shape[0] // 3
    length = 2 * half
    i = pl.program_id(0)

    @pl.when(i == 0)
    def _():
        fill_keys(kv, marks, ka, va)
        for e in range(m):
            qs[e * half : (e + 1) * half, :] = kv[first + e][length:, :]

    at, h, token = block_of(i, half, length, first)
    lane = lax.broadcasted_iota(jnp.int32, (BQ, LANES), 1)
    q = qs[pl.ds(at, BQ), :].astype(F32)
    q = jnp.where(h == 1, turn(q), q)
    q = jnp.where(lane < HEAD, q, query_marks(marks, token, lane)).astype(BF16)
    scores, top = [], None
    for j in range(n * length // KC):
        s = lax.dot_general(q, ka[j * KC : (j + 1) * KC, :], NT, preferred_element_type=F32)
        scores.append(s)
        for t in range(KC // LANES):
            tile = s[:, t * LANES : (t + 1) * LANES]
            top = tile if top is None else jnp.maximum(top, tile)
    top = jnp.max(top, axis=1, keepdims=True)
    total = jnp.zeros((BQ, LANES), F32)
    for j, s in enumerate(scores):
        p = jnp.exp2(s - top).astype(BF16)
        total += jnp.dot(p, va[j * KC : (j + 1) * KC, :], preferred_element_type=F32)
    weight = total[:, :1]
    o = total / weight
    o = jnp.where(h == 0, turn(o), o)
    log = jnp.broadcast_to(top + jnp.log2(weight), (BQ, LANES))
    other = (lane < HEAD) & (h == 1)
    os[pl.ds(at, BQ), :] = jnp.where(other, os[pl.ds(at, BQ), :], o)
    lse[pl.ds(at, BQ), :] = jnp.where(other, lse[pl.ds(at, BQ), :], log)

    @pl.when(i == pl.num_programs(0) - 1)
    def _():
        for e in range(m):
            outs[e][...] = os[e * half : (e + 1) * half, :].astype(BF16)


def attend(kv, marks, first, m):
    n, half = len(kv), kv[0].shape[0] // 3
    length = 2 * half
    steps = m * 2 * half // BQ
    args = [*kv, marks]
    outs = [shape((half, LANES), BF16)] * m + [shape((m * half, LANES), F32)]
    out = call(
        functools.partial(attend_body, m=m, n=n, first=first),
        outs,
        *args,
        grid=(steps,),
        in_specs=[whole_block(a) for a in args],
        out_specs=[whole_block(o) for o in outs],
        scratch=[
            pltpu.VMEM((m * half, LANES), BF16),
            pltpu.VMEM((n * length, LANES), BF16),
            pltpu.VMEM((n * length, LANES), BF16),
            pltpu.VMEM((m * half, LANES), F32),
        ],
        flops=4 * steps * BQ * n * length * 256,
        trans=steps * BQ * n * length,
        name="attend",
    )
    return out[:m], out[m]


def split3(value):
    high = value.astype(BF16).astype(F32)
    rest = value - high
    middle = rest.astype(BF16).astype(F32)
    return high, middle, rest - middle


def attend_back_body(*refs, m, n, first, start, end):
    grads, outs = (refs[k * m : (k + 1) * m] for k in range(2))
    kv, lse, marks = refs[2 * m : 2 * m + n], refs[2 * m + n], refs[2 * m + n + 1]
    at = 2 * m + n + 2
    before = None
    if not start:
        before, at = refs[at], at + 1
    if end:
        earlier, at = refs[at : at + n - m], at + n - m
        results, at = refs[at : at + n], at + n
        qs, gs, os, ds_, ka, va, acc = refs[at:]
    else:
        dqs, at = refs[at : at + m], at + m
        acc, at = refs[at], at + 1
        qs, gs, os, ds_, ka, va = refs[at:]
    half = kv[0].shape[0] // 3
    length = 2 * half
    i = pl.program_id(0)

    @pl.when(i == 0)
    def _():
        fill_keys(kv, marks, ka, va)
        for e in range(m):
            rows = slice(e * half, (e + 1) * half)
            qs[rows, :] = kv[first + e][length:, :]
            gs[rows, :] = grads[e][...]
            os[rows, :] = outs[e][...]
        acc[...] = jnp.zeros_like(acc) if start else before[...]

    row, h, token = block_of(i, half, length, first)
    lane = lax.broadcasted_iota(jnp.int32, (BQ, LANES), 1)
    here = pl.ds(row, BQ)
    q = qs[here, :].astype(F32)
    g = gs[here, :].astype(F32)
    o = os[here, :].astype(F32)
    log = lse[here, :]
    q = jnp.where(h == 1, turn(q), q)
    g = jnp.where(h == 0, turn(g), g)
    o = jnp.where(h == 0, turn(o), o)
    log = jnp.where(h == 1, turn(log), log)[:, :1]
    dot = jnp.sum(jnp.where(lane >= HEAD, g * o, 0.0), axis=1, keepdims=True)
    b0, b1, b2 = split3(-log)
    q_marks = query_marks(marks, token, lane)
    first_lane = HEAD + DOCS
    qa = jnp.where(lane == first_lane, b0, q_marks)
    qa = jnp.where(lane == first_lane + 1, b1, qa)
    qa = jnp.where(lane == first_lane + 2, b2, qa)
    qa = jnp.where(lane < HEAD, q, qa).astype(BF16)
    b0, b1, b2 = split3(-dot)
    ga = jnp.where(lane == 0, b0, jnp.where(lane == 1, b1, jnp.where(lane == 2, b2, 0.0)))
    ga = jnp.where(lane >= HEAD, g, ga).astype(BF16)
    q_t = q.T[:HEAD].astype(BF16)
    g_t = g.T[HEAD:].astype(BF16)
    total = jnp.zeros((BQ, LANES), F32)
    for j in range(n * length // KC):
        cols = slice(j * KC, (j + 1) * KC)
        s = lax.dot_general(qa, ka[cols, :], NT, preferred_element_type=F32)
        t = lax.dot_general(ga, va[cols, :], NT, preferred_element_type=F32)
        p = jnp.exp2(s)
        ds = (p * t).astype(BF16)
        p = p.astype(BF16)
        acc[HEAD:, cols] += jnp.dot(g_t, p, preferred_element_type=F32)
        acc[:HEAD, cols] += jnp.dot(q_t, ds, preferred_element_type=F32)
        total += jnp.dot(ds, ka[cols, :], preferred_element_type=F32)
    total = total * (HEAD**-0.5)
    total = jnp.where(h == 1, turn(total), total)
    other = (lane < HEAD) & (h == 1)
    ds_[here, :] = jnp.where(other, ds_[here, :], total)

    @pl.when(i == pl.num_programs(0) - 1)
    def _():
        if not end:
            for e in range(m):
                dqs[e][...] = ds_[e * half : (e + 1) * half, :].astype(BF16)
        else:
            for e in range(n):
                if e < n - m:
                    results[e][:half, :] = earlier[e][...]
                else:
                    at = (e - n + m) * half
                    results[e][:half, :] = ds_[at : at + half, :].astype(BF16)
                cols = slice(e * length, (e + 1) * length)
                turned = acc[:, cols].T
                key_lane = lax.broadcasted_iota(jnp.int32, (length, LANES), 1)
                results[e][half:, :] = jnp.where(key_lane < HEAD, turned * LN2, turned).astype(BF16)


def attend_back(grads, outs, kv, lse, marks, before, earlier, first, end):
    m, n, half = len(grads), len(kv), kv[0].shape[0] // 3
    length = 2 * half
    steps = m * 2 * half // BQ
    start = before is None
    args = [*grads, *outs, *kv, lse, marks] + ([] if start else [before]) + (list(earlier) if end else [])
    if end:
        results = [shape((half + length, LANES), BF16)] * n
    else:
        results = [shape((half, LANES), BF16)] * m + [shape((LANES, n * length), F32)]
    out = call(
        functools.partial(attend_back_body, m=m, n=n, first=first, start=start, end=end),
        results,
        *args,
        grid=(steps,),
        in_specs=[whole_block(a) for a in args],
        out_specs=[whole_block(o) for o in results],
        scratch=[pltpu.VMEM((m * half, LANES), BF16)] * 3
        + [pltpu.VMEM((m * half, LANES), F32)]
        + [pltpu.VMEM((n * length, LANES), BF16)] * 2
        + ([pltpu.VMEM((LANES, n * length), F32)] if end else []),
        flops=10 * steps * BQ * n * length * 256,
        trans=steps * BQ * n * length,
        name="attend_back",
    )
    return out if end else (out[:m], out[m])


def input_grad_body(ids, *refs, dp, n):
    pieces, ws = refs[:n], refs[n : n + dp]
    cosine, sine, whole, send, keep = refs[n + dp :]
    me = ids[1]
    half = send.shape[0]
    step = 256
    lane = lax.broadcasted_iota(jnp.int32, (step, LANES), 1)
    for h, target in ((1, send), (0, keep)):
        for i in range(half // step):
            rows = slice(h * half + i * step, h * half + (i + 1) * step)
            there = slice(i * step, (i + 1) * step)
            dq = [p[there, :].astype(F32) for p in pieces]
            kv = [p[half + rows.start : half + rows.stop, :].astype(F32) for p in pieces]
            qt = unpack_pairs(me, dq, n, h, lane)
            kt = unpack_pairs(me, kv, n, 0, lane)
            vt = unpack_pairs(me, kv, n, 1, lane)
            back = [x * cosine[rows, :] - swap_halves(x, lane) * sine[rows, :] for x in qt + kt]
            low = jnp.concatenate(back + vt, axis=1).astype(BF16)
            whole[rows, :] = low
            col = 0
            for w in ws:
                size = w.shape[0]
                total = lax.dot_general(low, w[...], NT, preferred_element_type=F32)
                target[there, col : col + size] = total.astype(target.dtype)
                col += size


def normed_of(value):
    centered = value - jnp.mean(value, axis=-1, keepdims=True)
    inverse = lax.rsqrt(jnp.mean(centered * centered, axis=-1, keepdims=True) + 1e-05)
    return centered * inverse, inverse


def back_of(grad, normed, inverse, gain):
    scaled = grad * gain
    inner = (
        scaled
        - jnp.mean(scaled, axis=-1, keepdims=True)
        - normed * jnp.mean(scaled * normed, axis=-1, keepdims=True)
    )
    return inverse * inner


RB = 64
CB = 512


def spans(total, size):
    size = min(size, total)
    return [slice(i, i + size) for i in range(0, total, size)]


class Copies:
    def __init__(self, sems):
        self.sems, self.count, self.groups = sems, 0, {}

    def start(self, group, src, dst):
        copy = pltpu.make_async_copy(src, dst, self.sems.at[self.count])
        copy.start()
        self.count += 1
        self.groups.setdefault(group, []).append(copy)

    def wait(self, group):
        for copy in self.groups[group]:
            copy.wait()


def weight_copies(copies, wod, wi, tp, dp, heads, gains, wi_all, wd_all, x=None, tokens=None):
    hidden = wi[0].shape[1]
    cols = wi[0].shape[0]
    lw = wod[0].shape[0] - hidden - 16

    def small():
        for f in range(dp):
            src = wod[f].at[pl.ds(hidden + lw, 16), :]
            copies.start("small", src, gains.at[:, pl.ds(f * cols, cols)])
        for d in range(tp):
            for f in range(dp):
                src = wod[d * dp + f].at[pl.ds(hidden, lw), :]
                copies.start("small", src, heads.at[pl.ds(d * lw, lw), pl.ds(f * cols, cols)])
        if x is not None:
            copies.start("small", x.at[pl.ds(0, tokens.shape[0]), :], tokens)

    def large():
        for d in range(tp):
            for f in range(dp):
                copies.start(d, wi[d * dp + f], wi_all.at[d, pl.ds(f * cols, cols), :])
                src = wod[d * dp + f].at[pl.ds(0, hidden), :]
                copies.start(d, src, wd_all.at[d, :, pl.ds(f * cols, cols)])

    return small, large


def forward_body(*refs, tp, dp):
    received, cotangent, x = refs[:tp], refs[tp], refs[tp + 1]
    at = tp + 2
    wod, wi = refs[at : at + tp * dp], refs[at + tp * dp : at + 2 * tp * dp]
    at += 2 * tp * dp
    second_low, out_low, slope, normed, inverse, second, terms, lows = refs[at : at + 8]
    act = refs[at + 8 : at + 8 + tp]
    heads, gains, wi_all, wd_all, tokens, attended, acc, sems = refs[at + 8 + tp :]
    share, width = tokens.shape
    hidden = wi[0].shape[1]
    lw = received[0].shape[1]
    copies = Copies(sems)
    small, large = weight_copies(copies, wod, wi, tp, dp, heads, gains, wi_all, wd_all, x, tokens)
    small()
    large()
    for j in range(tp):
        attended[:, j * lw : (j + 1) * lw] = received[j][...]
    copies.wait("small")
    for c in spans(width, CB):
        mixed = jnp.dot(attended[...], heads[:, c], preferred_element_type=F32)
        acc[:, c] = mixed + tokens[:, c].astype(F32)
    gain = gains[...].astype(F32)
    for b in spans(share, RB):
        n, r = normed_of(acc[b, :])
        out = n * gain[0:1, :] + gain[1:2, :]
        acc[b, :] = out
        lows[b, :] = out.astype(BF16)
        normed[b, :] = n
        inverse[b, :] = jnp.broadcast_to(r, (r.shape[0], LANES))
    for d in range(tp):
        copies.wait(d)
        for c in spans(hidden, CB):
            h = jnp.dot(lows[...], wi_all[d, :, c], preferred_element_type=F32)
            phi = 0.5 * (1.0 + lax.erf(h * SQRT_HALF))
            act[d][:, c] = (h * phi).astype(BF16)
            there = slice(d * hidden + c.start, d * hidden + c.stop)
            slope[:, there] = (phi + h * jnp.exp(-0.5 * h * h) * INV_SQRT_TAU).astype(BF16)
        for c in spans(width, CB):
            acc[:, c] += jnp.dot(act[d][...], wd_all[d, :, c], preferred_element_type=F32)
    sums = [jnp.zeros((1, width), F32)] * 2
    for b in spans(share, RB):
        n, r = normed_of(acc[b, :])
        out_low[b, :] = (n * gain[2:3, :] + gain[3:4, :]).astype(BF16)
        grad = cotangent[b, :].astype(F32)
        result = back_of(grad, n, r, gain[2:3, :])
        second[b, :] = result
        second_low[b, :] = result.astype(BF16)
        sums = [sums[0] + jnp.sum(grad * n, axis=0, keepdims=True), sums[1] + jnp.sum(grad, axis=0, keepdims=True)]
    terms[0:1, :], terms[1:2, :] = sums


def middle_scratch(tp, dp, lw, hidden, width, share):
    return [
        pltpu.VMEM((tp * lw, width), BF16),
        pltpu.VMEM((16, width), BF16),
        pltpu.VMEM((tp, width, hidden), BF16),
        pltpu.VMEM((tp, hidden, width), BF16),
    ]


ANY = pl.BlockSpec(memory_space=pl.ANY)


def forward(received, cotangent, x, wod, wi, tp, dp):
    (share, lw), (cols, hidden) = received[0].shape, wi[0].shape
    width = cols * dp
    outs = [
        shape((share, width), BF16),
        shape((share, width), BF16),
        shape((share, tp * hidden), BF16),
        shape((share, width), F32),
        shape((share, LANES), F32),
        shape((share, width), F32),
        shape((2, width), F32),
        shape((share, width), BF16),
    ]
    out = call(
        functools.partial(forward_body, tp=tp, dp=dp),
        outs + [shape((share, hidden), BF16)] * tp,
        *received,
        cotangent,
        x,
        *wod,
        *wi,
        in_specs=[FULL] * (tp + 1) + [ANY] * (1 + 2 * tp * dp),
        scratch=middle_scratch(tp, dp, lw, hidden, width, share)
        + [
            pltpu.VMEM((share, width), BF16),
            pltpu.VMEM((share, tp * lw), BF16),
            pltpu.VMEM((share, width), F32),
            pltpu.SemaphoreType.DMA((dp + tp * dp * 3 + 1,)),
        ],
        flops=2 * share * width * (tp * lw + 2 * tp * hidden),
        trans=3 * share * tp * hidden,
        name="forward",
    )
    return out[:7], out[7], out[8:]


def backward_body(*refs, tp, dp):
    second_low, slope, normed, inverse, second, terms = refs[:6]
    wod, wi = refs[6 : 6 + tp * dp], refs[6 + tp * dp : 6 + 2 * tp * dp]
    at = 6 + 2 * tp * dp
    rows, first = refs[at], refs[at + 1]
    pre, grads = refs[at + 2 : at + 2 + tp], refs[at + 2 + tp : at + 2 + 2 * tp]
    heads, gains, wi_all, wd_all, acc, edge, sems = refs[at + 2 + 2 * tp :]
    share, width = second_low.shape
    hidden, lw = pre[0].shape[1], grads[0].shape[1]
    copies = Copies(sems)
    small, large = weight_copies(copies, wod, wi, tp, dp, heads, gains, wi_all, wd_all)
    large()
    small()
    acc[...] = second[...]
    for d in range(tp):
        copies.wait(d)
        for c in spans(hidden, CB):
            grad = lax.dot_general(second_low[...], wd_all[d, c, :], NT, preferred_element_type=F32)
            there = slice(d * hidden + c.start, d * hidden + c.stop)
            pre[d][:, c] = (grad * slope[:, there].astype(F32)).astype(BF16)
        for c in spans(width, CB):
            acc[:, c] += lax.dot_general(pre[d][...], wi_all[d, c, :], NT, preferred_element_type=F32)
    copies.wait("small")
    gain = gains[...].astype(F32)
    sums = [jnp.zeros((1, width), F32)] * 2
    for b in spans(share, RB):
        grad, n = acc[b, :], normed[b, :]
        result = back_of(grad, n, inverse[b, :1], gain[0:1, :])
        first[b, :] = result
        rows[b, :] = result.astype(BF16)
        sums = [sums[0] + jnp.sum(grad * n, axis=0, keepdims=True), sums[1] + jnp.sum(grad, axis=0, keepdims=True)]
    for j in range(tp):
        part = lax.dot_general(rows[:share, :], heads[j * lw : (j + 1) * lw, :], NT, preferred_element_type=F32)
        grads[j][...] = part.astype(BF16)
    edge[...] = jnp.zeros_like(edge)
    edge[0:1, :], edge[1:2, :] = sums
    edge[2:4, :] = terms[...]
    rows[share:, :] = edge[...].astype(BF16)


def backward(forwarded, wod, wi, tp, dp, lw):
    cols, hidden = wi[0].shape
    share, width = forwarded[0].shape
    out = call(
        functools.partial(backward_body, tp=tp, dp=dp),
        [shape((share + 16, width), BF16), shape((share, width), F32)]
        + [shape((share, hidden), BF16)] * tp
        + [shape((share, lw), BF16)] * tp,
        *forwarded,
        *wod,
        *wi,
        in_specs=[FULL] * 6 + [ANY] * (2 * tp * dp),
        scratch=middle_scratch(tp, dp, lw, hidden, width, share)
        + [
            pltpu.VMEM((share, width), F32),
            pltpu.VMEM((16, width), F32),
            pltpu.SemaphoreType.DMA((dp + tp * dp * 3,)),
        ],
        flops=2 * share * width * (tp * lw + 2 * tp * hidden),
        name="backward",
    )
    return out[0], out[1], out[2 : 2 + tp], out[2 + tp :]


def rotate_heads(values, angles, sign):
    half = HEAD // 2
    cosine = jnp.cos(angles)[:, None, :half]
    sine = sign * jnp.sin(angles)[:, None, :half]
    first, second = values[..., :half], values[..., half:]
    return jnp.concatenate([first * cosine - second * sine, second * cosine + first * sine], axis=-1)


def gathered_attention(tokens, weights, angles, docs):
    rows, width = tokens.shape[0], weights[0].shape[1]
    heads = width // HEAD
    scale = HEAD**-0.5

    def project(w):
        return jnp.dot(tokens, w, preferred_element_type=F32).reshape(rows, heads, HEAD)

    q = rotate_heads(project(weights[0]), angles, 1.0).astype(BF16)
    k = rotate_heads(project(weights[1]), angles, 1.0).astype(BF16)
    v = project(weights[2]).astype(BF16)
    keys = jnp.concatenate(gather(k, "ctx"))
    values = jnp.concatenate(gather(v, "ctx"))
    all_docs = jnp.concatenate(gather(docs, "ctx"))

    def masked():
        s = jnp.einsum("qhd,khd->hqk", q, keys, preferred_element_type=F32) * scale
        return jnp.where(docs[None, :, None] == all_docs[None, None, :], s, NEG_BIG)

    s = masked()
    top = jnp.max(s, axis=-1, keepdims=True)
    p = jnp.exp(s - top)
    total = jnp.sum(p, axis=-1)
    out = jnp.einsum("hqk,khd->qhd", p.astype(BF16), values, preferred_element_type=F32)
    out = out / total.T[..., None]
    log = top[..., 0] + jnp.log(total)

    def backward(grad):
        grad = grad.astype(BF16).reshape(rows, heads, HEAD)
        dot = jnp.sum(grad.astype(F32) * out, axis=-1).T
        p = jnp.exp(masked() - log[..., None])
        dv = jnp.einsum("hqk,qhd->khd", p.astype(BF16), grad, preferred_element_type=F32)
        dp = jnp.einsum("qhd,khd->hqk", grad, values, preferred_element_type=F32)
        ds = (p * (dp - dot[..., None])).astype(BF16)
        dq = jnp.einsum("hqk,khd->qhd", ds, keys, preferred_element_type=F32) * scale
        dk = jnp.einsum("hqk,qhd->khd", ds, q, preferred_element_type=F32) * scale

        def owned(value):
            half = value.shape[0] // 2
            keep, got = scatter(value[half:].astype(BF16), value[:half], "ctx", 0)
            return keep + got.astype(F32)

        dq = rotate_heads(dq, angles, -1.0)
        dk = rotate_heads(owned(dk), angles, -1.0)
        return jnp.concatenate([x.astype(BF16).reshape(rows, width) for x in (dq, dk, owned(dv))], axis=1)

    return out.astype(BF16).reshape(rows, width), backward


def body(
    layer_input,
    segments,
    positions,
    w_q,
    w_k,
    w_v,
    w_o,
    w_in,
    w_out,
    ln1_gain,
    ln1_bias,
    ln2_gain,
    ln2_bias,
    cotangent,
):
    LINE.clear()
    seqs, length, width = layer_input.shape
    assert seqs == 1
    tp, dp, ctx = lax.axis_size("tp"), lax.axis_size("dp"), lax.axis_size("ctx")
    lw, hidden = w_q.shape[1], w_in.shape[1]
    heads = lw // HEAD
    ids = jnp.stack([lax.axis_index("dp"), lax.axis_index("ctx"), lax.axis_index("tp")]).astype(jnp.int32)
    share = length // tp
    half = length // 2
    spread = heads == ctx and heads % 2 == 0 and half % BQ == 0 and tp % 2 == 0

    def exchange(parts, first=0):
        return [p if first + k == 0 else swap(p, "ctx", first + k) for k, p in enumerate(parts)]

    def exchange_tp(parts):
        return [p if d == 0 else swap(p, "tp", d) for d, p in zip(order(tp), parts)]

    def over_dp(parts):
        return [gather(p, "dp") for p in parts]

    def arrange_tokens(value):
        table = value.reshape(tp, share)
        picked = [lax.dynamic_index_in_dim(table, ids[2] ^ d, 0, keepdims=False) for d in order(tp)]
        return jnp.stack(picked).reshape(length)

    def lined(parts):
        return [in_line(p) for p in parts]

    w_qkv = gather(step(lambda *w: jnp.concatenate(w, axis=1), w_q, w_k, w_v), "dp")
    vectors = jnp.stack([ln1_gain, ln1_bias, ln2_gain, ln2_bias])
    tall = chips(step(lambda *w: jnp.concatenate(w), w_out, w_o, jnp.pad(vectors, ((0, 12), (0, 0)))))
    x = arrange(ids, layer_input.reshape(length, width), tp, dp, order(tp))
    docs = arrange_tokens(in_line(segments).reshape(length))
    places = arrange_tokens(in_line(positions).reshape(length)).astype(F32)
    freq = 10000.0 ** (-(jnp.arange(LANES, dtype=jnp.int32) % (HEAD // 2)).astype(F32) * 2.0 / HEAD)
    angles = places[:, None] * freq[None, :]
    middle = ctx // 2
    near = [j for j, d in enumerate(order(tp)) if d in (1, tp // 2)]
    far = [j for j, d in enumerate(order(tp)) if d not in (0, 1, tp // 2)]

    if spread:
        all_docs = jnp.concatenate([docs] + [swap(docs, "ctx", e) for e in range(1, ctx)])
        side = jnp.where(jnp.arange(LANES) % HEAD < HEAD // 2, -1.0, 1.0)
        cosine, sine = step(lambda t: (jnp.cos(t), jnp.sin(t) * side[None, :]), angles)
        out_grad = arrange(ids, cotangent.reshape(length, width), tp, dp, [0])
        lane = jnp.arange(LANES)[None, :]
        in_docs = (lane >= HEAD) & (lane < HEAD + DOCS)
        folded = (lane >= HEAD + DOCS) & (lane < HEAD + DOCS + 3)
        due(w_qkv)
        wi_far = chips(in_line(w_in))
        wi = gather(in_line(w_in), "dp")
        kv = call(
            functools.partial(project_body, dp=dp, n=heads),
            [shape((length + half, LANES), BF16)] * ctx,
            ids,
            x,
            *w_qkv,
            cosine,
            sine,
            in_specs=[SMEM] + [FULL] * (3 + dp),
            flops=6 * length * width * lw,
            name="project",
        )
        kv = exchange(kv)
        marks = step(lambda d: jnp.where(in_docs, lane - HEAD != d[:, None], folded).astype(BF16), all_docs)
        due(tall, kv, wi_far)
        tall_cores = [[swap(in_line(p), "tp", 1)] for p in tall]
        tall_own = gather(in_line(tall[0]), "dp")
        wi = [[p, *chips(in_line(p))[1:]] for p in wi[1:]]
        o, log = attend(kv, marks, 0, middle)
        outs, logs = [o], [log]
        mixed = exchange(o)
        due(wi, tall_cores)
        wi = [q for p in zip(wi_far, *wi) for q in p]
        tall = [tall_own] + over_dp(lined(tall[1:]))
        few = len(wi) // 2
        wi_cores = [swap(p, "tp", 1) for p in lined(wi[:few])]
        o, log = attend(kv, marks, middle, ctx - middle)
        outs.append(o)
        logs.append(log)
        due(wi_cores, tall[0])
        mixed.extend(exchange(lined(o), middle))
        wi = wi + wi_cores + [swap(p, "tp", 1) for p in lined(wi[few:])]
        due(mixed, wi)
        attended = call(
            functools.partial(unpack_body, n=heads),
            [shape((share, lw), BF16)] * tp,
            ids,
            *mixed,
            in_specs=[SMEM] + [FULL] * ctx,
            name="unpack",
        )
        due(tall)
        tall_cores = [c + [swap(in_line(q), "tp", 1) for q in p[1:]] for c, p in zip(tall_cores, tall)]
        tall = [q for p in tall + tall_cores for q in p]
    else:
        wi = [list(p) for p in zip(*[chips(p) for p in gather(w_in, "dp")])]
        wi = cores([q for p in wi for q in p])
        tall = cores([q for p in over_dp(tall) for q in p])
        out_grad = arrange(ids, cotangent.reshape(length, width), tp, dp, [0])
        joined = jnp.concatenate(w_qkv)
        mixed, attend_backward = gathered_attention(
            x, [joined[:, k * lw : (k + 1) * lw] for k in range(3)], angles, docs
        )
        attended = [mixed[j * share : (j + 1) * share] for j in range(tp)]

    received = exchange_tp(attended)
    forwarded, hidden_low, act = forward(received, out_grad, x, tall, wi, tp, dp)
    second_low, out_low, *forwarded = forwarded
    act = list(act)
    for j in near:
        act[j] = swap(act[j], "tp", order(tp)[j])
    rows, first_grad, pre, grads = backward([second_low, *forwarded], tall, wi, tp, dp, lw)
    due([act[j] for j in near])
    grads = exchange_tp(lined(grads))

    if spread:
        packed = call(
            functools.partial(pack_body, tp=tp, n=heads),
            [shape((half, LANES), BF16)] * ctx,
            ids,
            *grads,
            in_specs=[SMEM] + [FULL] * tp,
            name="pack",
        )
        packed = exchange(packed)
        due(packed[:middle])
    else:
        due(grads)
    second_low = chips(in_line(second_low))
    for j in far:
        act[j] = swap(in_line(act[j]), "tp", order(tp)[j])
    hidden_low = chips(in_line(hidden_low))
    if spread:
        query_grads, carried = attend_back(
            packed[:middle], outs[0], kv, logs[0], marks, None, None, 0, False
        )
        due(packed)
    due(second_low, act, hidden_low)
    second_low = second_low + [swap(p, "tp", 1) for p in lined(second_low)]
    hidden_low = hidden_low + [swap(p, "tp", 1) for p in lined(hidden_low)]
    rows = chips(in_line(rows))
    due(second_low)
    left = product(act, second_low)
    pre = list(pre)
    for j in far + near:
        pre[j] = swap(in_line(pre[j]), "tp", order(tp)[j])
    due(hidden_low)
    out_sum = GradSum(ids, 1, *left)
    if spread:
        pieces = attend_back(
            packed[middle:], outs[1], kv, logs[1], marks, carried, query_grads, middle, True
        )
    due(rows, pre, out_sum.got)
    rows = rows + [swap(p, "tp", 1) for p in lined(rows)]
    if spread:
        pieces = exchange(lined(pieces))
    out_sum.halve()
    left = products(pre, hidden_low, attended, rows, ctx)
    in_sum = GradSum(ids, 1, *left)
    if spread:
        due(pieces)
        out_sum.halve()
        whole, send, keep = call(
            functools.partial(input_grad_body, dp=dp, n=heads),
            [shape((length, 3 * lw), BF16), shape((half, width), BF16), shape((half, width), F32)],
            ids,
            *pieces,
            *w_qkv,
            cosine,
            sine,
            in_specs=[SMEM] + [FULL] * (ctx + dp + 2),
            flops=6 * length * width * lw,
            name="input_grad",
        )
    else:
        out_sum.halve()
        whole = attend_backward(jnp.concatenate(grads))
        total = lax.dot_general(whole, joined, NT, preferred_element_type=F32)
        send, keep = total[half:].astype(BF16), total[:half]
    got = swap(send, "tp", 1)
    mid = width // 2
    send = step(lambda l, r: over_rows(l[:, mid:], r).astype(BF16), x, whole)
    qkv_send = in_line(send)
    in_sum.halve()
    qkv_sum = GradSum(ids, 0, qkv_send, step(lambda l, r: over_rows(l[:, :mid], r), x, whole))
    out_sum.merge()
    keep, got = scatter(None, keep, "tp", 0, got)
    out_low = chips(in_line(out_low))
    in_sum.halve()
    qkv_sum.halve()
    out_sum.last()
    low = step(lambda l, k, f: (f + k + l.astype(F32)).astype(BF16), got, keep, first_grad)
    low = chips(low)
    qkv_sum.halve()
    in_sum.merge()
    output = place(ids, cores(out_low), tp, dp, length)
    qkv_sum.merge()
    in_sum.last()
    (w_out_grad,) = out_sum.columns([width // dp])
    qkv_sum.last()
    input_grad = place(ids, cores(low), tp, dp, length)
    w_in_grad, w_o_grad, terms = in_sum.rows(hidden, lw)
    w_q_grad, w_k_grad, w_v_grad = qkv_sum.columns([lw] * 3)
    return (
        output[None],
        input_grad[None],
        w_q_grad,
        w_k_grad,
        w_v_grad,
        w_o_grad,
        w_in_grad,
        w_out_grad,
        terms[0],
        terms[1],
        terms[2],
        terms[3],
    )


def solution(mesh):
    return jax.shard_map(
        body,
        mesh=mesh,
        in_specs=(
            P("dp", "ctx", None),
            P("dp", "ctx"),
            P("dp", "ctx"),
            P("dp", "tp"),
            P("dp", "tp"),
            P("dp", "tp"),
            P("tp", "dp"),
            P("dp", "tp"),
            P("tp", "dp"),
            P("dp"),
            P("dp"),
            P("dp"),
            P("dp"),
            P("dp", "ctx", None),
        ),
        out_specs=(
            P("dp", "ctx", None),
            P("dp", "ctx", None),
            P("dp", "tp"),
            P("dp", "tp"),
            P("dp", "tp"),
            P("tp", "dp"),
            P("dp", "tp"),
            P("tp", "dp"),
            P("dp"),
            P("dp"),
            P("dp"),
            P("dp"),
        ),
        check_vma=False,
    )
```

```python
import functools

import jax
import jax.numpy as jnp
from jax import lax
from jax.experimental import pallas as pl
from jax.experimental.pallas import tpu as pltpu
from jax.sharding import PartitionSpec as P

D = 1024
H = 16
HEAD = D // H
LANES = 128
DOCS = 17

NEG_BIG = -1e30
SQRT_HALF = 0.7071067811865476
INV_SQRT_TAU = 0.3989422804014327
LOG2E = 1.4426950408889634
LN2 = 0.6931471805599453
F32 = jnp.float32
BF16 = jnp.bfloat16
NT = (((1,), (1,)), ((), ()))
VMEM_LIMIT = 60 * 1024 * 1024


def order(n):
    found, bit = [0], n >> 1
    while bit:
        found = found + [d | bit for d in found]
        bit >>= 1
    return found


def swap(value, axis, bit):
    n = lax.axis_size(axis)
    return lax.ppermute(value, axis, [(i, i ^ bit) for i in range(n)])


def gather(value, axis):
    parts, bit = [value], lax.axis_size(axis) >> 1
    while bit:
        parts = parts + [swap(p, axis, bit) for p in parts]
        bit >>= 1
    return parts


def chips(value):
    parts, bit = [value], lax.axis_size("tp") >> 1
    while bit > 1:
        parts = parts + [swap(p, "tp", bit) for p in parts]
        bit >>= 1
    return parts


def cores(parts):
    return parts + [swap(p, "tp", 1) for p in parts]


def after(value, *others):
    return lax.optimization_barrier((value, *others))[0]


LINE = []


def in_line(value):
    return after(value, *LINE) if LINE else value


def due(*values):
    LINE.extend(jax.tree.leaves(values))


def step(function, *args):
    result = function(in_line(args[0]), *args[1:])
    LINE[:] = [result[0] if isinstance(result, (list, tuple)) else result]
    return result


def part_of(value, dim, start, size):
    return lax.slice_in_dim(value, start, start + size, axis=dim)


def split_sum(got, keep, dim):
    half = keep.shape[dim] // 2
    upper = part_of(keep, dim, half, half) + part_of(got, dim, half, half).astype(F32)
    return upper.astype(BF16), part_of(keep, dim, 0, half) + part_of(got, dim, 0, half).astype(F32)


def scatter(send, keep, axis, dim, got=None):
    n, bit = lax.axis_size(axis), 1
    while True:
        got = swap(send, axis, bit) if got is None else got
        bit <<= 1
        if bit >= n:
            return keep, got
        send, keep = step(functools.partial(split_sum, dim=dim), got, keep)
        got = None


def call(body, out_shape, *args, grid=None, in_specs=None, out_specs=None, scratch=(), flops=0, trans=0, name=None):
    extra = {}
    if grid is not None:
        extra["grid"] = grid
    if in_specs is not None:
        extra["in_specs"] = in_specs
    if out_specs is not None:
        extra["out_specs"] = out_specs
    args = list(args)
    first = 1 if args[0].shape == (3,) else 0
    args[first] = in_line(args[first])
    result = pl.pallas_call(
        body,
        out_shape=out_shape,
        scratch_shapes=list(scratch),
        compiler_params=pltpu.CompilerParams(vmem_limit_bytes=VMEM_LIMIT),
        cost_estimate=pl.CostEstimate(flops=1, bytes_accessed=1, transcendentals=0),
        name=name,
        **extra,
    )(*args)
    LINE[:] = [result[0] if isinstance(result, (list, tuple)) else result]
    return result


def shape(dims, dtype):
    return jax.ShapeDtypeStruct(dims, dtype)


SMEM = pl.BlockSpec(memory_space=pltpu.SMEM)
FULL = pl.BlockSpec(memory_space=pltpu.VMEM)


def whole_block(value):
    return pl.BlockSpec(value.shape, lambda i: (0,) * len(value.shape))


def arrange_body(ids, src, out, *, tp, dp, shares):
    rows, width = src.shape
    share, cols = rows // tp, width // dp
    for j, d in enumerate(shares):
        for e, f in enumerate(order(dp)):
            row = pl.multiple_of((ids[2] ^ d) * share, share)
            col = pl.multiple_of((ids[0] ^ f) * cols, cols)
            out[j * share : (j + 1) * share, e * cols : (e + 1) * cols] = src[pl.ds(row, share), pl.ds(col, cols)]


def arrange(ids, src, tp, dp, shares):
    rows = src.shape[0] // tp * len(shares)
    return call(
        functools.partial(arrange_body, tp=tp, dp=dp, shares=shares),
        shape((rows, src.shape[1]), src.dtype),
        ids,
        src,
        in_specs=[SMEM, FULL],
        name="arrange",
    )


def place_body(ids, *refs, tp, dp, first):
    *parts, out = refs
    rows, width = out.shape
    share, cols = rows // tp, width // dp
    for j, d in enumerate(order(tp)):
        for e, f in enumerate(order(dp)):
            row = pl.multiple_of((ids[2] ^ d) * share, share)
            col = pl.multiple_of((ids[0] ^ f) * cols, cols)
            block = parts[j][first : first + share, e * cols : (e + 1) * cols]
            out[pl.ds(row, share), pl.ds(col, cols)] = block.astype(F32)


def place(ids, parts, tp, dp, rows, first=0):
    return call(
        functools.partial(place_body, tp=tp, dp=dp, first=first),
        shape((rows, parts[0].shape[1]), F32),
        ids,
        *parts,
        in_specs=[SMEM] + [FULL] * len(parts),
        name="place",
    )


def halve_body(ids, got, keep, send, left, *, bit):
    rows = send.shape[0]
    mine = (ids[1] // bit) % 2
    at = pl.multiple_of((1 - mine) * rows, rows)
    send[...] = (keep[pl.ds(at, rows), :] + got[pl.ds(at, rows), :].astype(F32)).astype(BF16)
    at = pl.multiple_of(mine * rows, rows)
    left[...] = keep[pl.ds(at, rows), :] + got[pl.ds(at, rows), :].astype(F32)


def merge_body(got, keep, out):
    out[...] = (keep[...] + got[...].astype(F32)).astype(BF16)


def row_of(who, n, rows):
    at, bit, size = 0, 1, n * rows
    while bit < n:
        size //= 2
        at = at + ((who // bit) % 2) * size
        bit *= 2
    return pl.multiple_of(at, rows)


def product_body(*refs, tp):
    left, right = refs[:tp], refs[tp : 2 * tp]
    send, keep, tall, wide = refs[2 * tp :]
    share = left[0].shape[0]
    for j in range(tp):
        tall[j * share : (j + 1) * share, :] = left[j][...]
        wide[j * share : (j + 1) * share, :] = right[j][...]
    mid = send.shape[1]
    for c in spans(tall.shape[1], CB):
        total = over_rows(tall[:, c], wide[...])
        keep[c, :] = total[:, :mid]
        send[c, :] = total[:, mid:].astype(BF16)


def products_body(*refs, tp):
    pre, hidden, attended, rows = (refs[k * tp : (k + 1) * tp] for k in range(4))
    send, keep, tall, wide, thin, broad = refs[4 * tp :]
    share = pre[0].shape[0]
    mid = send.shape[1]
    terms = None
    for j in range(tp):
        there = slice(j * share, (j + 1) * share)
        tall[there, :] = pre[j][...]
        wide[there, :] = hidden[j][...]
        thin[there, :] = attended[j][...]
        broad[there, :] = rows[j][:share, :]
        term = rows[j][share:, :].astype(F32)
        terms = term if terms is None else terms + term
    at = 0
    for left, right in ((tall, wide), (thin, broad)):
        for c in spans(left.shape[1], CB):
            total = over_rows(left[:, c], right[...])
            size = total.shape[0]
            keep[at : at + size, :] = total[:, :mid]
            send[at : at + size, :] = total[:, mid:].astype(BF16)
            at += size
    keep[at : at + 16, :] = terms[:, :mid]
    send[at : at + 16, :] = terms[:, mid:].astype(BF16)
    at += 16
    if at < send.shape[0]:
        keep[at:, :] = jnp.zeros((send.shape[0] - at, mid), F32)
        send[at:, :] = jnp.zeros((send.shape[0] - at, mid), BF16)


def product(left, right):
    tp, (share, m), n = len(left), left[0].shape, right[0].shape[1]
    return call(
        functools.partial(product_body, tp=tp),
        [shape((m, n // 2), BF16), shape((m, n // 2), F32)],
        *left,
        *right,
        scratch=[pltpu.VMEM((tp * share, m), BF16), pltpu.VMEM((tp * share, n), BF16)],
        flops=2 * tp * share * m * n,
        name="product",
    )


def products(pre, hidden, attended, rows, ctx):
    tp, (share, m), n, lw = len(pre), pre[0].shape, hidden[0].shape[1], attended[0].shape[1]
    total = -(-(m + lw + 16) // (16 * ctx)) * 16 * ctx
    return call(
        functools.partial(products_body, tp=tp),
        [shape((total, n // 2), BF16), shape((total, n // 2), F32)],
        *pre,
        *hidden,
        *attended,
        *rows,
        scratch=[pltpu.VMEM((tp * share, w), BF16) for w in (m, n, lw, n)],
        flops=2 * tp * share * (m + lw) * n,
        name="products",
    )


def place_columns_body(ids, *refs, n, widths):
    parts, outs = refs[:n], refs[n:]
    rows = parts[0].shape[0]
    for e, part in zip(order(n), parts):
        at = row_of(ids[1] ^ e, n, rows)
        lane = 0
        for out, width in zip(outs, widths):
            out[pl.ds(at, rows), :] = part[:, lane : lane + width].astype(F32)
            lane += width


def place_rows_body(ids, *refs, n):
    parts, (first, second, terms, whole) = refs[:n], refs[n:]
    rows = parts[0].shape[0]
    for e, part in zip(order(n), parts):
        at = row_of(ids[1] ^ e, n, rows)
        whole[pl.ds(at, rows), :] = part[...].astype(F32)
    hidden, middle = first.shape[1], second.shape[0]
    first[...] = whole[:hidden, :].T
    second[...] = whole[hidden : hidden + middle, :]
    terms[...] = whole[hidden + middle : hidden + middle + 8, :]


class GradSum:
    def __init__(self, ids, dim, send, keep):
        self.ids, self.dim, self.keep = ids, dim, keep
        self.got = swap(send, "dp", 1)
        self.bit = 0

    def halve(self):
        if self.bit == 0:
            self.keep, self.got = scatter(None, self.keep, "dp", self.dim, self.got)
        self.bit = max(1, 2 * self.bit)
        rows, cols = self.keep.shape
        send, self.keep = call(
            functools.partial(halve_body, bit=self.bit),
            [shape((rows // 2, cols), BF16), shape((rows // 2, cols), F32)],
            self.ids,
            self.got,
            self.keep,
            in_specs=[SMEM, FULL, FULL],
            name="halve",
        )
        self.got = swap(send, "ctx", self.bit)

    def merge(self):
        while 2 * self.bit < lax.axis_size("ctx"):
            self.halve()
        self.parts = [call(merge_body, shape(self.keep.shape, BF16), self.got, self.keep, name="merge")]
        bit = self.bit
        while bit > 1:
            self.parts = self.parts + [swap(p, "ctx", bit) for p in self.parts]
            bit >>= 1

    def last(self):
        due(self.parts)
        self.parts = self.parts + [swap(p, "ctx", 1) for p in [in_line(p) for p in self.parts]]

    def columns(self, widths):
        n = len(self.parts)
        rows = self.parts[0].shape[0] * n
        return call(
            functools.partial(place_columns_body, n=n, widths=widths),
            [shape((rows, w), F32) for w in widths],
            self.ids,
            *self.parts,
            in_specs=[SMEM] + [FULL] * n,
            name="place_columns",
        )

    def rows(self, hidden, middle):
        n = len(self.parts)
        rows, cols = self.parts[0].shape
        return call(
            functools.partial(place_rows_body, n=n),
            [shape((cols, hidden), F32), shape((middle, cols), F32), shape((8, cols), F32)],
            self.ids,
            *self.parts,
            in_specs=[SMEM] + [FULL] * n,
            scratch=[pltpu.VMEM((n * rows, cols), F32)],
            name="place_rows",
        )


def over_rows(left, right):
    return lax.dot_general(left, right, (((0,), (0,)), ((), ())), preferred_element_type=F32)


def swap_halves(tile, lane):
    return jnp.where(lane % HEAD < HEAD // 2, pltpu.roll(tile, LANES - HEAD // 2, 1), pltpu.roll(tile, HEAD // 2, 1))


def turn(tile):
    return pltpu.roll(tile, HEAD, 1)


def pick(me, values, index):
    chosen = values[index]
    for i in range(1, len(values)):
        chosen = jnp.where(me == i, values[i ^ index], chosen)
    return chosen


def rows_dot(x, pieces, start, size):
    total, at = None, 0
    for w in pieces:
        depth = w.shape[0]
        term = jnp.dot(x[:, at : at + depth], w[:, start : start + size], preferred_element_type=F32)
        total = term if total is None else total + term
        at += depth
    return total


def project_body(ids, x, *refs, dp, n):
    ws = refs[:dp]
    cosine, sine = refs[dp], refs[dp + 1]
    outs = refs[dp + 2 :]
    me = ids[1]
    step = 256
    length = x.shape[0]
    half = length // 2
    width = n * HEAD
    lane = lax.broadcasted_iota(jnp.int32, (step, LANES), 1)
    for i in range(half // step):
        sides = []
        for h in range(2):
            rows = slice(h * half + i * step, h * half + (i + 1) * step)
            total = rows_dot(x[rows, :], ws, 0, 3 * width)
            tiles = [total[:, t * LANES : (t + 1) * LANES] for t in range(3 * n // 2)]
            tiles = [
                tile * cosine[rows, :] + swap_halves(tile, lane) * sine[rows, :] if t < n else tile
                for t, tile in enumerate(tiles)
            ]
            heads, pairs = [], []
            for t in range(n // 2):
                qt, kt, vt = tiles[t] * (HEAD**-0.5 * LOG2E), tiles[n // 2 + t], tiles[n + t]
                pairs.append(jnp.where(lane < HEAD, kt, turn(vt)))
                pairs.append(jnp.where(lane < HEAD, turn(kt), vt))
                heads.extend([qt, turn(qt)] if h == 0 else [turn(qt), qt])
            sides.append(heads)
            for e in range(n):
                outs[e][rows, :] = pick(me, pairs, e).astype(BF16)
        packed = [jnp.where(lane < HEAD, lo, hi) for lo, hi in zip(*sides)]
        for e in range(n):
            outs[e][length + i * step : length + (i + 1) * step, :] = pick(me, packed, e).astype(BF16)


def unpack_pairs(me, packed, n, h, lane):
    tiles = []
    for t in range(n // 2):
        lo, hi = pick(me, packed, 2 * t), pick(me, packed, 2 * t + 1)
        if h == 0:
            tiles.append(jnp.where(lane < HEAD, lo, turn(hi)))
        else:
            tiles.append(jnp.where(lane < HEAD, turn(lo), hi))
    return tiles


def unpack_body(ids, *refs, n):
    packed, outs = refs[:n], refs[n:]
    half, share = packed[0].shape[0], outs[0].shape[0]
    lane = lax.broadcasted_iota(jnp.int32, (share, LANES), 1)
    for i in range(half // share):
        pieces = [p[i * share : (i + 1) * share, :].astype(F32) for p in packed]
        for h in range(2):
            tiles = unpack_pairs(ids[1], pieces, n, h, lane)
            out = outs[h * (half // share) + i]
            for t, tile in enumerate(tiles):
                out[:, t * LANES : (t + 1) * LANES] = tile.astype(BF16)


def pack_body(ids, *refs, tp, n):
    parts, outs = refs[:tp], refs[tp:]
    half, share = outs[0].shape[0], parts[0].shape[0]
    lane = lax.broadcasted_iota(jnp.int32, (share, LANES), 1)
    for i in range(half // share):
        sides = []
        for h in range(2):
            grad = parts[h * (half // share) + i]
            heads = []
            for t in range(n // 2):
                tile = grad[:, t * LANES : (t + 1) * LANES].astype(F32)
                heads.extend([tile, turn(tile)] if h == 0 else [turn(tile), tile])
            sides.append(heads)
        packed = [jnp.where(lane < HEAD, lo, hi) for lo, hi in zip(*sides)]
        for e in range(n):
            outs[e][i * share : (i + 1) * share, :] = pick(ids[1], packed, e).astype(BF16)


BQ = 256
KC = 1024


def fill_keys(kv, marks, ka, va):
    size = kv[0].shape[0] // 3 * 2
    lane = lax.broadcasted_iota(jnp.int32, (size, LANES), 1)
    ones = jnp.where(lane < 3, 1.0, 0.0).astype(BF16)
    for e, ref in enumerate(kv):
        rows = slice(e * size, (e + 1) * size)
        both = ref[:size, :]
        ka[rows, :] = jnp.where(lane < HEAD, both, marks[rows, :])
        va[rows, :] = jnp.where(lane < HEAD, ones, both)


def query_marks(marks, row, lane):
    there = (lane >= HEAD) & (lane < HEAD + DOCS)
    bias = (marks[pl.ds(row, BQ), :].astype(F32) - 1.0) * -NEG_BIG
    return jnp.where(there, bias, 0.0)


def block_of(i, half, length, first):
    block, h = i // 2, i % 2
    blocks = half // BQ
    token = (first + block // blocks) * length + h * half + (block % blocks) * BQ
    return pl.multiple_of(block * BQ, BQ), h, pl.multiple_of(token, BQ)


def attend_body(*refs, m, n, first):
    kv, marks = refs[:n], refs[n]
    outs, lse = refs[n + 1 : n + 1 + m], refs[n + 1 + m]
    qs, ka, va, os = refs[n + 2 + m :]
    half = kv[0].shape[0] // 3
    length = 2 * half
    i = pl.program_id(0)

    @pl.when(i == 0)
    def _():
        fill_keys(kv, marks, ka, va)
        for e in range(m):
            qs[e * half : (e + 1) * half, :] = kv[first + e][length:, :]

    at, h, token = block_of(i, half, length, first)
    lane = lax.broadcasted_iota(jnp.int32, (BQ, LANES), 1)
    q = qs[pl.ds(at, BQ), :].astype(F32)
    q = jnp.where(h == 1, turn(q), q)
    q = jnp.where(lane < HEAD, q, query_marks(marks, token, lane)).astype(BF16)
    scores, top = [], None
    for j in range(n * length // KC):
        s = lax.dot_general(q, ka[j * KC : (j + 1) * KC, :], NT, preferred_element_type=F32)
        scores.append(s)
        for t in range(KC // LANES):
            tile = s[:, t * LANES : (t + 1) * LANES]
            top = tile if top is None else jnp.maximum(top, tile)
    top = jnp.max(top, axis=1, keepdims=True)
    total = jnp.zeros((BQ, LANES), F32)
    for j, s in enumerate(scores):
        p = jnp.exp2(s - top).astype(BF16)
        total += jnp.dot(p, va[j * KC : (j + 1) * KC, :], preferred_element_type=F32)
    weight = total[:, :1]
    o = total / weight
    o = jnp.where(h == 0, turn(o), o)
    log = jnp.broadcast_to(top + jnp.log2(weight), (BQ, LANES))
    other = (lane < HEAD) & (h == 1)
    os[pl.ds(at, BQ), :] = jnp.where(other, os[pl.ds(at, BQ), :], o)
    lse[pl.ds(at, BQ), :] = jnp.where(other, lse[pl.ds(at, BQ), :], log)

    @pl.when(i == pl.num_programs(0) - 1)
    def _():
        for e in range(m):
            outs[e][...] = os[e * half : (e + 1) * half, :].astype(BF16)


def attend(kv, marks, first, m):
    n, half = len(kv), kv[0].shape[0] // 3
    length = 2 * half
    steps = m * 2 * half // BQ
    args = [*kv, marks]
    outs = [shape((half, LANES), BF16)] * m + [shape((m * half, LANES), F32)]
    out = call(
        functools.partial(attend_body, m=m, n=n, first=first),
        outs,
        *args,
        grid=(steps,),
        in_specs=[whole_block(a) for a in args],
        out_specs=[whole_block(o) for o in outs],
        scratch=[
            pltpu.VMEM((m * half, LANES), BF16),
            pltpu.VMEM((n * length, LANES), BF16),
            pltpu.VMEM((n * length, LANES), BF16),
            pltpu.VMEM((m * half, LANES), F32),
        ],
        flops=4 * steps * BQ * n * length * 256,
        trans=steps * BQ * n * length,
        name="attend",
    )
    return out[:m], out[m]


def split3(value):
    high = value.astype(BF16).astype(F32)
    rest = value - high
    middle = rest.astype(BF16).astype(F32)
    return high, middle, rest - middle


def attend_back_body(*refs, m, n, first, start, end):
    grads, outs = (refs[k * m : (k + 1) * m] for k in range(2))
    kv, lse, marks = refs[2 * m : 2 * m + n], refs[2 * m + n], refs[2 * m + n + 1]
    at = 2 * m + n + 2
    before = None
    if not start:
        before, at = refs[at], at + 1
    if end:
        earlier, at = refs[at : at + n - m], at + n - m
        results, at = refs[at : at + n], at + n
        qs, gs, os, ds_, ka, va, acc = refs[at:]
    else:
        dqs, at = refs[at : at + m], at + m
        acc, at = refs[at], at + 1
        qs, gs, os, ds_, ka, va = refs[at:]
    half = kv[0].shape[0] // 3
    length = 2 * half
    i = pl.program_id(0)

    @pl.when(i == 0)
    def _():
        fill_keys(kv, marks, ka, va)
        for e in range(m):
            rows = slice(e * half, (e + 1) * half)
            qs[rows, :] = kv[first + e][length:, :]
            gs[rows, :] = grads[e][...]
            os[rows, :] = outs[e][...]
        acc[...] = jnp.zeros_like(acc) if start else before[...]

    row, h, token = block_of(i, half, length, first)
    lane = lax.broadcasted_iota(jnp.int32, (BQ, LANES), 1)
    here = pl.ds(row, BQ)
    q = qs[here, :].astype(F32)
    g = gs[here, :].astype(F32)
    o = os[here, :].astype(F32)
    log = lse[here, :]
    q = jnp.where(h == 1, turn(q), q)
    g = jnp.where(h == 0, turn(g), g)
    o = jnp.where(h == 0, turn(o), o)
    log = jnp.where(h == 1, turn(log), log)[:, :1]
    dot = jnp.sum(jnp.where(lane >= HEAD, g * o, 0.0), axis=1, keepdims=True)
    b0, b1, b2 = split3(-log)
    q_marks = query_marks(marks, token, lane)
    first_lane = HEAD + DOCS
    qa = jnp.where(lane == first_lane, b0, q_marks)
    qa = jnp.where(lane == first_lane + 1, b1, qa)
    qa = jnp.where(lane == first_lane + 2, b2, qa)
    qa = jnp.where(lane < HEAD, q, qa).astype(BF16)
    b0, b1, b2 = split3(-dot)
    ga = jnp.where(lane == 0, b0, jnp.where(lane == 1, b1, jnp.where(lane == 2, b2, 0.0)))
    ga = jnp.where(lane >= HEAD, g, ga).astype(BF16)
    q_t = q.T[:HEAD].astype(BF16)
    g_t = g.T[HEAD:].astype(BF16)
    total = jnp.zeros((BQ, LANES), F32)
    for j in range(n * length // KC):
        cols = slice(j * KC, (j + 1) * KC)
        s = lax.dot_general(qa, ka[cols, :], NT, preferred_element_type=F32)
        t = lax.dot_general(ga, va[cols, :], NT, preferred_element_type=F32)
        p = jnp.exp2(s)
        ds = (p * t).astype(BF16)
        p = p.astype(BF16)
        acc[HEAD:, cols] += jnp.dot(g_t, p, preferred_element_type=F32)
        acc[:HEAD, cols] += jnp.dot(q_t, ds, preferred_element_type=F32)
        total += jnp.dot(ds, ka[cols, :], preferred_element_type=F32)
    total = total * (HEAD**-0.5)
    total = jnp.where(h == 1, turn(total), total)
    other = (lane < HEAD) & (h == 1)
    ds_[here, :] = jnp.where(other, ds_[here, :], total)

    @pl.when(i == pl.num_programs(0) - 1)
    def _():
        if not end:
            for e in range(m):
                dqs[e][...] = ds_[e * half : (e + 1) * half, :].astype(BF16)
        else:
            for e in range(n):
                if e < n - m:
                    results[e][:half, :] = earlier[e][...]
                else:
                    at = (e - n + m) * half
                    results[e][:half, :] = ds_[at : at + half, :].astype(BF16)
                cols = slice(e * length, (e + 1) * length)
                turned = acc[:, cols].T
                key_lane = lax.broadcasted_iota(jnp.int32, (length, LANES), 1)
                results[e][half:, :] = jnp.where(key_lane < HEAD, turned * LN2, turned).astype(BF16)


def attend_back(grads, outs, kv, lse, marks, before, earlier, first, end):
    m, n, half = len(grads), len(kv), kv[0].shape[0] // 3
    length = 2 * half
    steps = m * 2 * half // BQ
    start = before is None
    args = [*grads, *outs, *kv, lse, marks] + ([] if start else [before]) + (list(earlier) if end else [])
    if end:
        results = [shape((half + length, LANES), BF16)] * n
    else:
        results = [shape((half, LANES), BF16)] * m + [shape((LANES, n * length), F32)]
    out = call(
        functools.partial(attend_back_body, m=m, n=n, first=first, start=start, end=end),
        results,
        *args,
        grid=(steps,),
        in_specs=[whole_block(a) for a in args],
        out_specs=[whole_block(o) for o in results],
        scratch=[pltpu.VMEM((m * half, LANES), BF16)] * 3
        + [pltpu.VMEM((m * half, LANES), F32)]
        + [pltpu.VMEM((n * length, LANES), BF16)] * 2
        + ([pltpu.VMEM((LANES, n * length), F32)] if end else []),
        flops=10 * steps * BQ * n * length * 256,
        trans=steps * BQ * n * length,
        name="attend_back",
    )
    return out if end else (out[:m], out[m])


def input_grad_body(ids, *refs, dp, n):
    pieces, ws = refs[:n], refs[n : n + dp]
    cosine, sine, whole, send, keep = refs[n + dp :]
    me = ids[1]
    half = send.shape[0]
    step = 256
    lane = lax.broadcasted_iota(jnp.int32, (step, LANES), 1)
    for h, target in ((1, send), (0, keep)):
        for i in range(half // step):
            rows = slice(h * half + i * step, h * half + (i + 1) * step)
            there = slice(i * step, (i + 1) * step)
            dq = [p[there, :].astype(F32) for p in pieces]
            kv = [p[half + rows.start : half + rows.stop, :].astype(F32) for p in pieces]
            qt = unpack_pairs(me, dq, n, h, lane)
            kt = unpack_pairs(me, kv, n, 0, lane)
            vt = unpack_pairs(me, kv, n, 1, lane)
            back = [x * cosine[rows, :] - swap_halves(x, lane) * sine[rows, :] for x in qt + kt]
            low = jnp.concatenate(back + vt, axis=1).astype(BF16)
            whole[rows, :] = low
            col = 0
            for w in ws:
                size = w.shape[0]
                total = lax.dot_general(low, w[...], NT, preferred_element_type=F32)
                target[there, col : col + size] = total.astype(target.dtype)
                col += size


def normed_of(value):
    centered = value - jnp.mean(value, axis=-1, keepdims=True)
    inverse = lax.rsqrt(jnp.mean(centered * centered, axis=-1, keepdims=True) + 1e-05)
    return centered * inverse, inverse


def back_of(grad, normed, inverse, gain):
    scaled = grad * gain
    inner = (
        scaled
        - jnp.mean(scaled, axis=-1, keepdims=True)
        - normed * jnp.mean(scaled * normed, axis=-1, keepdims=True)
    )
    return inverse * inner


RB = 64
CB = 512


def spans(total, size):
    size = min(size, total)
    return [slice(i, i + size) for i in range(0, total, size)]


class Copies:
    def __init__(self, sems):
        self.sems, self.count, self.groups = sems, 0, {}

    def start(self, group, src, dst):
        copy = pltpu.make_async_copy(src, dst, self.sems.at[self.count])
        copy.start()
        self.count += 1
        self.groups.setdefault(group, []).append(copy)

    def wait(self, group):
        for copy in self.groups[group]:
            copy.wait()


def weight_copies(copies, wod, wi, tp, dp, heads, gains, wi_all, wd_all, x=None, tokens=None):
    hidden = wi[0].shape[1]
    cols = wi[0].shape[0]
    lw = wod[0].shape[0] - hidden - 16

    def small():
        for f in range(dp):
            src = wod[f].at[pl.ds(hidden + lw, 16), :]
            copies.start("small", src, gains.at[:, pl.ds(f * cols, cols)])
        for d in range(tp):
            for f in range(dp):
                src = wod[d * dp + f].at[pl.ds(hidden, lw), :]
                copies.start("small", src, heads.at[pl.ds(d * lw, lw), pl.ds(f * cols, cols)])
        if x is not None:
            copies.start("small", x.at[pl.ds(0, tokens.shape[0]), :], tokens)

    def large():
        for d in range(tp):
            for f in range(dp):
                copies.start(d, wi[d * dp + f], wi_all.at[d, pl.ds(f * cols, cols), :])
                src = wod[d * dp + f].at[pl.ds(0, hidden), :]
                copies.start(d, src, wd_all.at[d, :, pl.ds(f * cols, cols)])

    return small, large


def forward_body(*refs, tp, dp):
    received, cotangent, x = refs[:tp], refs[tp], refs[tp + 1]
    at = tp + 2
    wod, wi = refs[at : at + tp * dp], refs[at + tp * dp : at + 2 * tp * dp]
    at += 2 * tp * dp
    second_low, out_low, slope, normed, inverse, second, terms, lows = refs[at : at + 8]
    act = refs[at + 8 : at + 8 + tp]
    heads, gains, wi_all, wd_all, tokens, attended, acc, sems = refs[at + 8 + tp :]
    share, width = tokens.shape
    hidden = wi[0].shape[1]
    lw = received[0].shape[1]
    copies = Copies(sems)
    small, large = weight_copies(copies, wod, wi, tp, dp, heads, gains, wi_all, wd_all, x, tokens)
    small()
    large()
    for j in range(tp):
        attended[:, j * lw : (j + 1) * lw] = received[j][...]
    copies.wait("small")
    for c in spans(width, CB):
        mixed = jnp.dot(attended[...], heads[:, c], preferred_element_type=F32)
        acc[:, c] = mixed + tokens[:, c].astype(F32)
    gain = gains[...].astype(F32)
    for b in spans(share, RB):
        n, r = normed_of(acc[b, :])
        out = n * gain[0:1, :] + gain[1:2, :]
        acc[b, :] = out
        lows[b, :] = out.astype(BF16)
        normed[b, :] = n
        inverse[b, :] = jnp.broadcast_to(r, (r.shape[0], LANES))
    for d in range(tp):
        copies.wait(d)
        for c in spans(hidden, CB):
            h = jnp.dot(lows[...], wi_all[d, :, c], preferred_element_type=F32)
            phi = 0.5 * (1.0 + lax.erf(h * SQRT_HALF))
            act[d][:, c] = (h * phi).astype(BF16)
            there = slice(d * hidden + c.start, d * hidden + c.stop)
            slope[:, there] = (phi + h * jnp.exp(-0.5 * h * h) * INV_SQRT_TAU).astype(BF16)
        for c in spans(width, CB):
            acc[:, c] += jnp.dot(act[d][...], wd_all[d, :, c], preferred_element_type=F32)
    sums = [jnp.zeros((1, width), F32)] * 2
    for b in spans(share, RB):
        n, r = normed_of(acc[b, :])
        out_low[b, :] = (n * gain[2:3, :] + gain[3:4, :]).astype(BF16)
        grad = cotangent[b, :].astype(F32)
        result = back_of(grad, n, r, gain[2:3, :])
        second[b, :] = result
        second_low[b, :] = result.astype(BF16)
        sums = [sums[0] + jnp.sum(grad * n, axis=0, keepdims=True), sums[1] + jnp.sum(grad, axis=0, keepdims=True)]
    terms[0:1, :], terms[1:2, :] = sums


def middle_scratch(tp, dp, lw, hidden, width, share):
    return [
        pltpu.VMEM((tp * lw, width), BF16),
        pltpu.VMEM((16, width), BF16),
        pltpu.VMEM((tp, width, hidden), BF16),
        pltpu.VMEM((tp, hidden, width), BF16),
    ]


ANY = pl.BlockSpec(memory_space=pl.ANY)


def forward(received, cotangent, x, wod, wi, tp, dp):
    (share, lw), (cols, hidden) = received[0].shape, wi[0].shape
    width = cols * dp
    outs = [
        shape((share, width), BF16),
        shape((share, width), BF16),
        shape((share, tp * hidden), BF16),
        shape((share, width), F32),
        shape((share, LANES), F32),
        shape((share, width), F32),
        shape((2, width), F32),
        shape((share, width), BF16),
    ]
    out = call(
        functools.partial(forward_body, tp=tp, dp=dp),
        outs + [shape((share, hidden), BF16)] * tp,
        *received,
        cotangent,
        x,
        *wod,
        *wi,
        in_specs=[FULL] * (tp + 1) + [ANY] * (1 + 2 * tp * dp),
        scratch=middle_scratch(tp, dp, lw, hidden, width, share)
        + [
            pltpu.VMEM((share, width), BF16),
            pltpu.VMEM((share, tp * lw), BF16),
            pltpu.VMEM((share, width), F32),
            pltpu.SemaphoreType.DMA((dp + tp * dp * 3 + 1,)),
        ],
        flops=2 * share * width * (tp * lw + 2 * tp * hidden),
        trans=3 * share * tp * hidden,
        name="forward",
    )
    return out[:7], out[7], out[8:]


def backward_body(*refs, tp, dp):
    second_low, slope, normed, inverse, second, terms = refs[:6]
    wod, wi = refs[6 : 6 + tp * dp], refs[6 + tp * dp : 6 + 2 * tp * dp]
    at = 6 + 2 * tp * dp
    rows, first = refs[at], refs[at + 1]
    pre, grads = refs[at + 2 : at + 2 + tp], refs[at + 2 + tp : at + 2 + 2 * tp]
    heads, gains, wi_all, wd_all, acc, edge, sems = refs[at + 2 + 2 * tp :]
    share, width = second_low.shape
    hidden, lw = pre[0].shape[1], grads[0].shape[1]
    copies = Copies(sems)
    small, large = weight_copies(copies, wod, wi, tp, dp, heads, gains, wi_all, wd_all)
    large()
    small()
    acc[...] = second[...]
    for d in range(tp):
        copies.wait(d)
        for c in spans(hidden, CB):
            grad = lax.dot_general(second_low[...], wd_all[d, c, :], NT, preferred_element_type=F32)
            there = slice(d * hidden + c.start, d * hidden + c.stop)
            pre[d][:, c] = (grad * slope[:, there].astype(F32)).astype(BF16)
        for c in spans(width, CB):
            acc[:, c] += lax.dot_general(pre[d][...], wi_all[d, c, :], NT, preferred_element_type=F32)
    copies.wait("small")
    gain = gains[...].astype(F32)
    sums = [jnp.zeros((1, width), F32)] * 2
    for b in spans(share, RB):
        grad, n = acc[b, :], normed[b, :]
        result = back_of(grad, n, inverse[b, :1], gain[0:1, :])
        first[b, :] = result
        rows[b, :] = result.astype(BF16)
        sums = [sums[0] + jnp.sum(grad * n, axis=0, keepdims=True), sums[1] + jnp.sum(grad, axis=0, keepdims=True)]
    for j in range(tp):
        part = lax.dot_general(rows[:share, :], heads[j * lw : (j + 1) * lw, :], NT, preferred_element_type=F32)
        grads[j][...] = part.astype(BF16)
    edge[...] = jnp.zeros_like(edge)
    edge[0:1, :], edge[1:2, :] = sums
    edge[2:4, :] = terms[...]
    rows[share:, :] = edge[...].astype(BF16)


def backward(forwarded, wod, wi, tp, dp, lw):
    cols, hidden = wi[0].shape
    share, width = forwarded[0].shape
    out = call(
        functools.partial(backward_body, tp=tp, dp=dp),
        [shape((share + 16, width), BF16), shape((share, width), F32)]
        + [shape((share, hidden), BF16)] * tp
        + [shape((share, lw), BF16)] * tp,
        *forwarded,
        *wod,
        *wi,
        in_specs=[FULL] * 6 + [ANY] * (2 * tp * dp),
        scratch=middle_scratch(tp, dp, lw, hidden, width, share)
        + [
            pltpu.VMEM((share, width), F32),
            pltpu.VMEM((16, width), F32),
            pltpu.SemaphoreType.DMA((dp + tp * dp * 3,)),
        ],
        flops=2 * share * width * (tp * lw + 2 * tp * hidden),
        name="backward",
    )
    return out[0], out[1], out[2 : 2 + tp], out[2 + tp :]


def rotate_heads(values, angles, sign):
    half = HEAD // 2
    cosine = jnp.cos(angles)[:, None, :half]
    sine = sign * jnp.sin(angles)[:, None, :half]
    first, second = values[..., :half], values[..., half:]
    return jnp.concatenate([first * cosine - second * sine, second * cosine + first * sine], axis=-1)


def gathered_attention(tokens, weights, angles, docs):
    rows, width = tokens.shape[0], weights[0].shape[1]
    heads = width // HEAD
    scale = HEAD**-0.5

    def project(w):
        return jnp.dot(tokens, w, preferred_element_type=F32).reshape(rows, heads, HEAD)

    q = rotate_heads(project(weights[0]), angles, 1.0).astype(BF16)
    k = rotate_heads(project(weights[1]), angles, 1.0).astype(BF16)
    v = project(weights[2]).astype(BF16)
    keys = jnp.concatenate(gather(k, "ctx"))
    values = jnp.concatenate(gather(v, "ctx"))
    all_docs = jnp.concatenate(gather(docs, "ctx"))

    def masked():
        s = jnp.einsum("qhd,khd->hqk", q, keys, preferred_element_type=F32) * scale
        return jnp.where(docs[None, :, None] == all_docs[None, None, :], s, NEG_BIG)

    s = masked()
    top = jnp.max(s, axis=-1, keepdims=True)
    p = jnp.exp(s - top)
    total = jnp.sum(p, axis=-1)
    out = jnp.einsum("hqk,khd->qhd", p.astype(BF16), values, preferred_element_type=F32)
    out = out / total.T[..., None]
    log = top[..., 0] + jnp.log(total)

    def backward(grad):
        grad = grad.astype(BF16).reshape(rows, heads, HEAD)
        dot = jnp.sum(grad.astype(F32) * out, axis=-1).T
        p = jnp.exp(masked() - log[..., None])
        dv = jnp.einsum("hqk,qhd->khd", p.astype(BF16), grad, preferred_element_type=F32)
        dp = jnp.einsum("qhd,khd->hqk", grad, values, preferred_element_type=F32)
        ds = (p * (dp - dot[..., None])).astype(BF16)
        dq = jnp.einsum("hqk,khd->qhd", ds, keys, preferred_element_type=F32) * scale
        dk = jnp.einsum("hqk,qhd->khd", ds, q, preferred_element_type=F32) * scale

        def owned(value):
            half = value.shape[0] // 2
            keep, got = scatter(value[half:].astype(BF16), value[:half], "ctx", 0)
            return keep + got.astype(F32)

        dq = rotate_heads(dq, angles, -1.0)
        dk = rotate_heads(owned(dk), angles, -1.0)
        return jnp.concatenate([x.astype(BF16).reshape(rows, width) for x in (dq, dk, owned(dv))], axis=1)

    return out.astype(BF16).reshape(rows, width), backward


def body(
    layer_input,
    segments,
    positions,
    w_q,
    w_k,
    w_v,
    w_o,
    w_in,
    w_out,
    ln1_gain,
    ln1_bias,
    ln2_gain,
    ln2_bias,
    cotangent,
):
    LINE.clear()
    seqs, length, width = layer_input.shape
    assert seqs == 1
    tp, dp, ctx = lax.axis_size("tp"), lax.axis_size("dp"), lax.axis_size("ctx")
    lw, hidden = w_q.shape[1], w_in.shape[1]
    heads = lw // HEAD
    ids = jnp.stack([lax.axis_index("dp"), lax.axis_index("ctx"), lax.axis_index("tp")]).astype(jnp.int32)
    share = length // tp
    half = length // 2
    spread = heads == ctx and heads % 2 == 0 and half % BQ == 0 and tp % 2 == 0

    def exchange(parts, first=0):
        return [p if first + k == 0 else swap(p, "ctx", first + k) for k, p in enumerate(parts)]

    def exchange_tp(parts):
        return [p if d == 0 else swap(p, "tp", d) for d, p in zip(order(tp), parts)]

    def over_dp(parts):
        return [gather(p, "dp") for p in parts]

    def arrange_tokens(value):
        table = value.reshape(tp, share)
        picked = [lax.dynamic_index_in_dim(table, ids[2] ^ d, 0, keepdims=False) for d in order(tp)]
        return jnp.stack(picked).reshape(length)

    def lined(parts):
        return [in_line(p) for p in parts]

    w_qkv = gather(step(lambda *w: jnp.concatenate(w, axis=1), w_q, w_k, w_v), "dp")
    vectors = jnp.stack([ln1_gain, ln1_bias, ln2_gain, ln2_bias])
    tall = chips(step(lambda *w: jnp.concatenate(w), w_out, w_o, jnp.pad(vectors, ((0, 12), (0, 0)))))
    x = arrange(ids, layer_input.reshape(length, width), tp, dp, order(tp))
    docs = arrange_tokens(in_line(segments).reshape(length))
    places = arrange_tokens(in_line(positions).reshape(length)).astype(F32)
    freq = 10000.0 ** (-(jnp.arange(LANES, dtype=jnp.int32) % (HEAD // 2)).astype(F32) * 2.0 / HEAD)
    angles = places[:, None] * freq[None, :]
    middle = ctx // 2
    near = [j for j, d in enumerate(order(tp)) if d in (1, tp // 2)]
    far = [j for j, d in enumerate(order(tp)) if d not in (0, 1, tp // 2)]

    if spread:
        all_docs = jnp.concatenate([docs] + [swap(docs, "ctx", e) for e in range(1, ctx)])
        side = jnp.where(jnp.arange(LANES) % HEAD < HEAD // 2, -1.0, 1.0)
        cosine, sine = step(lambda t: (jnp.cos(t), jnp.sin(t) * side[None, :]), angles)
        out_grad = arrange(ids, cotangent.reshape(length, width), tp, dp, [0])
        lane = jnp.arange(LANES)[None, :]
        in_docs = (lane >= HEAD) & (lane < HEAD + DOCS)
        folded = (lane >= HEAD + DOCS) & (lane < HEAD + DOCS + 3)
        due(w_qkv, all_docs)
        wi = gather(in_line(w_in), "dp")
        kv = call(
            functools.partial(project_body, dp=dp, n=heads),
            [shape((length + half, LANES), BF16)] * ctx,
            ids,
            x,
            *w_qkv,
            cosine,
            sine,
            in_specs=[SMEM] + [FULL] * (3 + dp),
            flops=6 * length * width * lw,
            name="project",
        )
        kv = exchange(kv)
        marks = step(lambda d: jnp.where(in_docs, lane - HEAD != d[:, None], folded).astype(BF16), all_docs)
        wi_far = chips(in_line(w_in))
        due(tall, kv, wi_far)
        tall_cores = [[swap(in_line(p), "tp", 1)] for p in tall]
        tall_own = gather(in_line(tall[0]), "dp")
        wi = [[p, *chips(in_line(p))[1:]] for p in wi[1:]]
        o, log = attend(kv, marks, 0, middle)
        outs, logs = [o], [log]
        mixed = exchange(o)
        due(wi, tall_cores)
        wi = [q for p in zip(wi_far, *wi) for q in p]
        tall = [tall_own] + over_dp(lined(tall[1:]))
        few = len(wi) // 2
        wi_cores = [swap(p, "tp", 1) for p in lined(wi[:few])]
        o, log = attend(kv, marks, middle, ctx - middle)
        outs.append(o)
        logs.append(log)
        due(wi_cores, tall[0])
        mixed.extend(exchange(lined(o), middle))
        wi = wi + wi_cores + [swap(p, "tp", 1) for p in lined(wi[few:])]
        due(mixed, wi)
        attended = call(
            functools.partial(unpack_body, n=heads),
            [shape((share, lw), BF16)] * tp,
            ids,
            *mixed,
            in_specs=[SMEM] + [FULL] * ctx,
            name="unpack",
        )
        due(tall)
        tall_cores = [c + [swap(in_line(q), "tp", 1) for q in p[1:]] for c, p in zip(tall_cores, tall)]
        tall = [q for p in tall + tall_cores for q in p]
    else:
        wi = [list(p) for p in zip(*[chips(p) for p in gather(w_in, "dp")])]
        wi = cores([q for p in wi for q in p])
        tall = cores([q for p in over_dp(tall) for q in p])
        out_grad = arrange(ids, cotangent.reshape(length, width), tp, dp, [0])
        joined = jnp.concatenate(w_qkv)
        mixed, attend_backward = gathered_attention(
            x, [joined[:, k * lw : (k + 1) * lw] for k in range(3)], angles, docs
        )
        attended = [mixed[j * share : (j + 1) * share] for j in range(tp)]

    received = exchange_tp(attended)
    forwarded, hidden_low, act = forward(received, out_grad, x, tall, wi, tp, dp)
    second_low, out_low, *forwarded = forwarded
    act = list(act)
    for j in near:
        act[j] = swap(act[j], "tp", order(tp)[j])
    rows, first_grad, pre, grads = backward([second_low, *forwarded], tall, wi, tp, dp, lw)
    due([act[j] for j in near])
    grads = exchange_tp(lined(grads))

    if spread:
        packed = call(
            functools.partial(pack_body, tp=tp, n=heads),
            [shape((half, LANES), BF16)] * ctx,
            ids,
            *grads,
            in_specs=[SMEM] + [FULL] * tp,
            name="pack",
        )
        packed = exchange(packed)
        due(packed[:middle])
    else:
        due(grads)
    second_low = chips(in_line(second_low))
    for j in far:
        act[j] = swap(in_line(act[j]), "tp", order(tp)[j])
    hidden_low = chips(in_line(hidden_low))
    if spread:
        query_grads, carried = attend_back(
            packed[:middle], outs[0], kv, logs[0], marks, None, None, 0, False
        )
        due(packed)
    due(second_low, act, hidden_low)
    second_low = second_low + [swap(p, "tp", 1) for p in lined(second_low)]
    hidden_low = hidden_low + [swap(p, "tp", 1) for p in lined(hidden_low)]
    rows = chips(in_line(rows))
    due(second_low)
    left = product(act, second_low)
    pre = list(pre)
    for j in far + near:
        pre[j] = swap(in_line(pre[j]), "tp", order(tp)[j])
    due(hidden_low)
    out_sum = GradSum(ids, 1, *left)
    if spread:
        pieces = attend_back(
            packed[middle:], outs[1], kv, logs[1], marks, carried, query_grads, middle, True
        )
    due(rows, pre, out_sum.got)
    rows = rows + [swap(p, "tp", 1) for p in lined(rows)]
    if spread:
        pieces = exchange(lined(pieces))
    out_sum.halve()
    left = products(pre, hidden_low, attended, rows, ctx)
    in_sum = GradSum(ids, 1, *left)
    if spread:
        due(pieces)
        out_sum.halve()
        whole, send, keep = call(
            functools.partial(input_grad_body, dp=dp, n=heads),
            [shape((length, 3 * lw), BF16), shape((half, width), BF16), shape((half, width), F32)],
            ids,
            *pieces,
            *w_qkv,
            cosine,
            sine,
            in_specs=[SMEM] + [FULL] * (ctx + dp + 2),
            flops=6 * length * width * lw,
            name="input_grad",
        )
    else:
        out_sum.halve()
        whole = attend_backward(jnp.concatenate(grads))
        total = lax.dot_general(whole, joined, NT, preferred_element_type=F32)
        send, keep = total[half:].astype(BF16), total[:half]
    got = swap(send, "tp", 1)
    mid = width // 2
    send = step(lambda l, r: over_rows(l[:, mid:], r).astype(BF16), x, whole)
    qkv_send = in_line(send)
    in_sum.halve()
    qkv_sum = GradSum(ids, 0, qkv_send, step(lambda l, r: over_rows(l[:, :mid], r), x, whole))
    out_sum.merge()
    keep, got = scatter(None, keep, "tp", 0, got)
    out_low = chips(in_line(out_low))
    in_sum.halve()
    qkv_sum.halve()
    out_sum.last()
    low = step(lambda l, k, f: (f + k + l.astype(F32)).astype(BF16), got, keep, first_grad)
    low = chips(low)
    qkv_sum.halve()
    in_sum.merge()
    due(out_low)
    output = place(ids, out_low + [swap(p, "tp", 1) for p in lined(out_low)], tp, dp, length)
    qkv_sum.merge()
    in_sum.last()
    (w_out_grad,) = out_sum.columns([width // dp])
    qkv_sum.last()
    due(low)
    input_grad = place(ids, low + [swap(p, "tp", 1) for p in lined(low)], tp, dp, length)
    w_in_grad, w_o_grad, terms = in_sum.rows(hidden, lw)
    w_q_grad, w_k_grad, w_v_grad = qkv_sum.columns([lw] * 3)
    return (
        output[None],
        input_grad[None],
        w_q_grad,
        w_k_grad,
        w_v_grad,
        w_o_grad,
        w_in_grad,
        w_out_grad,
        terms[0],
        terms[1],
        terms[2],
        terms[3],
    )


def solution(mesh):
    return jax.shard_map(
        body,
        mesh=mesh,
        in_specs=(
            P("dp", "ctx", None),
            P("dp", "ctx"),
            P("dp", "ctx"),
            P("dp", "tp"),
            P("dp", "tp"),
            P("dp", "tp"),
            P("tp", "dp"),
            P("dp", "tp"),
            P("tp", "dp"),
            P("dp"),
            P("dp"),
            P("dp"),
            P("dp"),
            P("dp", "ctx", None),
        ),
        out_specs=(
            P("dp", "ctx", None),
            P("dp", "ctx", None),
            P("dp", "tp"),
            P("dp", "tp"),
            P("dp", "tp"),
            P("tp", "dp"),
            P("dp", "tp"),
            P("tp", "dp"),
            P("dp"),
            P("dp"),
            P("dp"),
            P("dp"),
        ),
        check_vma=False,
    )
```

```python
import functools

import jax
import jax.numpy as jnp
from jax import lax
from jax.experimental import pallas as pl
from jax.experimental.pallas import tpu as pltpu
from jax.sharding import PartitionSpec as P

D = 1024
H = 16
HEAD = D // H
LANES = 128
DOCS = 17

NEG_BIG = -1e30
SQRT_HALF = 0.7071067811865476
INV_SQRT_TAU = 0.3989422804014327
LOG2E = 1.4426950408889634
LN2 = 0.6931471805599453
F32 = jnp.float32
BF16 = jnp.bfloat16
NT = (((1,), (1,)), ((), ()))
VMEM_LIMIT = 60 * 1024 * 1024


def order(n):
    found, bit = [0], n >> 1
    while bit:
        found = found + [d | bit for d in found]
        bit >>= 1
    return found


def swap(value, axis, bit):
    n = lax.axis_size(axis)
    return lax.ppermute(value, axis, [(i, i ^ bit) for i in range(n)])


def gather(value, axis):
    parts, bit = [value], lax.axis_size(axis) >> 1
    while bit:
        parts = parts + [swap(p, axis, bit) for p in parts]
        bit >>= 1
    return parts


def chips(value):
    parts, bit = [value], lax.axis_size("tp") >> 1
    while bit > 1:
        parts = parts + [swap(p, "tp", bit) for p in parts]
        bit >>= 1
    return parts


def cores(parts):
    return parts + [swap(p, "tp", 1) for p in parts]


def after(value, *others):
    return lax.optimization_barrier((value, *others))[0]


LINE = []


def in_line(value):
    return after(value, *LINE) if LINE else value


def due(*values):
    LINE.extend(jax.tree.leaves(values))


def step(function, *args):
    result = function(in_line(args[0]), *args[1:])
    LINE[:] = [result[0] if isinstance(result, (list, tuple)) else result]
    return result


def part_of(value, dim, start, size):
    return lax.slice_in_dim(value, start, start + size, axis=dim)


def split_sum(got, keep, dim):
    half = keep.shape[dim] // 2
    upper = part_of(keep, dim, half, half) + part_of(got, dim, half, half).astype(F32)
    return upper.astype(BF16), part_of(keep, dim, 0, half) + part_of(got, dim, 0, half).astype(F32)


def scatter(send, keep, axis, dim, got=None):
    n, bit = lax.axis_size(axis), 1
    while True:
        got = swap(send, axis, bit) if got is None else got
        bit <<= 1
        if bit >= n:
            return keep, got
        send, keep = step(functools.partial(split_sum, dim=dim), got, keep)
        got = None


def call(body, out_shape, *args, grid=None, in_specs=None, out_specs=None, scratch=(), flops=0, trans=0, name=None):
    extra = {}
    if grid is not None:
        extra["grid"] = grid
    if in_specs is not None:
        extra["in_specs"] = in_specs
    if out_specs is not None:
        extra["out_specs"] = out_specs
    args = list(args)
    first = 1 if args[0].shape == (3,) else 0
    args[first] = in_line(args[first])
    result = pl.pallas_call(
        body,
        out_shape=out_shape,
        scratch_shapes=list(scratch),
        compiler_params=pltpu.CompilerParams(vmem_limit_bytes=VMEM_LIMIT),
        cost_estimate=pl.CostEstimate(flops=1, bytes_accessed=1, transcendentals=0),
        name=name,
        **extra,
    )(*args)
    LINE[:] = [result[0] if isinstance(result, (list, tuple)) else result]
    return result


def shape(dims, dtype):
    return jax.ShapeDtypeStruct(dims, dtype)


SMEM = pl.BlockSpec(memory_space=pltpu.SMEM)
FULL = pl.BlockSpec(memory_space=pltpu.VMEM)


def whole_block(value):
    return pl.BlockSpec(value.shape, lambda i: (0,) * len(value.shape))


def arrange_body(ids, src, out, *, tp, dp, shares):
    rows, width = src.shape
    share, cols = rows // tp, width // dp
    for j, d in enumerate(shares):
        for e, f in enumerate(order(dp)):
            row = pl.multiple_of((ids[2] ^ d) * share, share)
            col = pl.multiple_of((ids[0] ^ f) * cols, cols)
            out[j * share : (j + 1) * share, e * cols : (e + 1) * cols] = src[pl.ds(row, share), pl.ds(col, cols)]


def arrange(ids, src, tp, dp, shares):
    rows = src.shape[0] // tp * len(shares)
    return call(
        functools.partial(arrange_body, tp=tp, dp=dp, shares=shares),
        shape((rows, src.shape[1]), src.dtype),
        ids,
        src,
        in_specs=[SMEM, FULL],
        name="arrange",
    )


def place_body(ids, *refs, tp, dp, first):
    *parts, out = refs
    rows, width = out.shape
    share, cols = rows // tp, width // dp
    for j, d in enumerate(order(tp)):
        for e, f in enumerate(order(dp)):
            row = pl.multiple_of((ids[2] ^ d) * share, share)
            col = pl.multiple_of((ids[0] ^ f) * cols, cols)
            block = parts[j][first : first + share, e * cols : (e + 1) * cols]
            out[pl.ds(row, share), pl.ds(col, cols)] = block.astype(F32)


def place(ids, parts, tp, dp, rows, first=0):
    return call(
        functools.partial(place_body, tp=tp, dp=dp, first=first),
        shape((rows, parts[0].shape[1]), F32),
        ids,
        *parts,
        in_specs=[SMEM] + [FULL] * len(parts),
        name="place",
    )


def halve_body(ids, got, keep, send, left, *, bit):
    rows = send.shape[0]
    mine = (ids[1] // bit) % 2
    at = pl.multiple_of((1 - mine) * rows, rows)
    send[...] = (keep[pl.ds(at, rows), :] + got[pl.ds(at, rows), :].astype(F32)).astype(BF16)
    at = pl.multiple_of(mine * rows, rows)
    left[...] = keep[pl.ds(at, rows), :] + got[pl.ds(at, rows), :].astype(F32)


def merge_body(got, keep, out):
    out[...] = (keep[...] + got[...].astype(F32)).astype(BF16)


def row_of(who, n, rows):
    at, bit, size = 0, 1, n * rows
    while bit < n:
        size //= 2
        at = at + ((who // bit) % 2) * size
        bit *= 2
    return pl.multiple_of(at, rows)


def product_body(*refs, tp):
    left, right = refs[:tp], refs[tp : 2 * tp]
    send, keep, tall, wide = refs[2 * tp :]
    share = left[0].shape[0]
    for j in range(tp):
        tall[j * share : (j + 1) * share, :] = left[j][...]
        wide[j * share : (j + 1) * share, :] = right[j][...]
    mid = send.shape[1]
    for c in spans(tall.shape[1], CB):
        total = over_rows(tall[:, c], wide[...])
        keep[c, :] = total[:, :mid]
        send[c, :] = total[:, mid:].astype(BF16)


def products_body(*refs, tp):
    pre, hidden, attended, rows = (refs[k * tp : (k + 1) * tp] for k in range(4))
    send, keep, tall, wide, thin, broad = refs[4 * tp :]
    share = pre[0].shape[0]
    mid = send.shape[1]
    terms = None
    for j in range(tp):
        there = slice(j * share, (j + 1) * share)
        tall[there, :] = pre[j][...]
        wide[there, :] = hidden[j][...]
        thin[there, :] = attended[j][...]
        broad[there, :] = rows[j][:share, :]
        term = rows[j][share:, :].astype(F32)
        terms = term if terms is None else terms + term
    at = 0
    for left, right in ((tall, wide), (thin, broad)):
        for c in spans(left.shape[1], CB):
            total = over_rows(left[:, c], right[...])
            size = total.shape[0]
            keep[at : at + size, :] = total[:, :mid]
            send[at : at + size, :] = total[:, mid:].astype(BF16)
            at += size
    keep[at : at + 16, :] = terms[:, :mid]
    send[at : at + 16, :] = terms[:, mid:].astype(BF16)
    at += 16
    if at < send.shape[0]:
        keep[at:, :] = jnp.zeros((send.shape[0] - at, mid), F32)
        send[at:, :] = jnp.zeros((send.shape[0] - at, mid), BF16)


def product(left, right):
    tp, (share, m), n = len(left), left[0].shape, right[0].shape[1]
    return call(
        functools.partial(product_body, tp=tp),
        [shape((m, n // 2), BF16), shape((m, n // 2), F32)],
        *left,
        *right,
        scratch=[pltpu.VMEM((tp * share, m), BF16), pltpu.VMEM((tp * share, n), BF16)],
        flops=2 * tp * share * m * n,
        name="product",
    )


def products(pre, hidden, attended, rows, ctx):
    tp, (share, m), n, lw = len(pre), pre[0].shape, hidden[0].shape[1], attended[0].shape[1]
    total = -(-(m + lw + 16) // (16 * ctx)) * 16 * ctx
    return call(
        functools.partial(products_body, tp=tp),
        [shape((total, n // 2), BF16), shape((total, n // 2), F32)],
        *pre,
        *hidden,
        *attended,
        *rows,
        scratch=[pltpu.VMEM((tp * share, w), BF16) for w in (m, n, lw, n)],
        flops=2 * tp * share * (m + lw) * n,
        name="products",
    )


def place_columns_body(ids, *refs, n, widths):
    parts, outs = refs[:n], refs[n:]
    rows = parts[0].shape[0]
    for e, part in zip(order(n), parts):
        at = row_of(ids[1] ^ e, n, rows)
        lane = 0
        for out, width in zip(outs, widths):
            out[pl.ds(at, rows), :] = part[:, lane : lane + width].astype(F32)
            lane += width


def place_rows_body(ids, *refs, n):
    parts, (first, second, terms, whole) = refs[:n], refs[n:]
    rows = parts[0].shape[0]
    for e, part in zip(order(n), parts):
        at = row_of(ids[1] ^ e, n, rows)
        whole[pl.ds(at, rows), :] = part[...].astype(F32)
    hidden, middle = first.shape[1], second.shape[0]
    first[...] = whole[:hidden, :].T
    second[...] = whole[hidden : hidden + middle, :]
    terms[...] = whole[hidden + middle : hidden + middle + 8, :]


class GradSum:
    def __init__(self, ids, dim, send, keep):
        self.ids, self.dim, self.keep = ids, dim, keep
        self.got = swap(send, "dp", 1)
        self.bit = 0

    def halve(self):
        if self.bit == 0:
            self.keep, self.got = scatter(None, self.keep, "dp", self.dim, self.got)
        self.bit = max(1, 2 * self.bit)
        rows, cols = self.keep.shape
        send, self.keep = call(
            functools.partial(halve_body, bit=self.bit),
            [shape((rows // 2, cols), BF16), shape((rows // 2, cols), F32)],
            self.ids,
            self.got,
            self.keep,
            in_specs=[SMEM, FULL, FULL],
            name="halve",
        )
        self.got = swap(send, "ctx", self.bit)

    def merge(self):
        while 2 * self.bit < lax.axis_size("ctx"):
            self.halve()
        self.parts = [call(merge_body, shape(self.keep.shape, BF16), self.got, self.keep, name="merge")]
        bit = self.bit
        while bit > 1:
            self.parts = self.parts + [swap(p, "ctx", bit) for p in self.parts]
            bit >>= 1

    def last(self):
        due(self.parts)
        self.parts = self.parts + [swap(p, "ctx", 1) for p in [in_line(p) for p in self.parts]]

    def columns(self, widths):
        n = len(self.parts)
        rows = self.parts[0].shape[0] * n
        return call(
            functools.partial(place_columns_body, n=n, widths=widths),
            [shape((rows, w), F32) for w in widths],
            self.ids,
            *self.parts,
            in_specs=[SMEM] + [FULL] * n,
            name="place_columns",
        )

    def rows(self, hidden, middle):
        n = len(self.parts)
        rows, cols = self.parts[0].shape
        return call(
            functools.partial(place_rows_body, n=n),
            [shape((cols, hidden), F32), shape((middle, cols), F32), shape((8, cols), F32)],
            self.ids,
            *self.parts,
            in_specs=[SMEM] + [FULL] * n,
            scratch=[pltpu.VMEM((n * rows, cols), F32)],
            name="place_rows",
        )


def over_rows(left, right):
    return lax.dot_general(left, right, (((0,), (0,)), ((), ())), preferred_element_type=F32)


def swap_halves(tile, lane):
    return jnp.where(lane % HEAD < HEAD // 2, pltpu.roll(tile, LANES - HEAD // 2, 1), pltpu.roll(tile, HEAD // 2, 1))


def turn(tile):
    return pltpu.roll(tile, HEAD, 1)


def pick(me, values, index):
    chosen = values[index]
    for i in range(1, len(values)):
        chosen = jnp.where(me == i, values[i ^ index], chosen)
    return chosen


def rows_dot(x, pieces, start, size):
    total, at = None, 0
    for w in pieces:
        depth = w.shape[0]
        term = jnp.dot(x[:, at : at + depth], w[:, start : start + size], preferred_element_type=F32)
        total = term if total is None else total + term
        at += depth
    return total


def project_body(ids, x, *refs, dp, n):
    ws = refs[:dp]
    cosine, sine = refs[dp], refs[dp + 1]
    outs = refs[dp + 2 :]
    me = ids[1]
    step = 256
    length = x.shape[0]
    half = length // 2
    width = n * HEAD
    lane = lax.broadcasted_iota(jnp.int32, (step, LANES), 1)
    for i in range(half // step):
        sides = []
        for h in range(2):
            rows = slice(h * half + i * step, h * half + (i + 1) * step)
            total = rows_dot(x[rows, :], ws, 0, 3 * width)
            tiles = [total[:, t * LANES : (t + 1) * LANES] for t in range(3 * n // 2)]
            tiles = [
                tile * cosine[rows, :] + swap_halves(tile, lane) * sine[rows, :] if t < n else tile
                for t, tile in enumerate(tiles)
            ]
            heads, pairs = [], []
            for t in range(n // 2):
                qt, kt, vt = tiles[t] * (HEAD**-0.5 * LOG2E), tiles[n // 2 + t], tiles[n + t]
                pairs.append(jnp.where(lane < HEAD, kt, turn(vt)))
                pairs.append(jnp.where(lane < HEAD, turn(kt), vt))
                heads.extend([qt, turn(qt)] if h == 0 else [turn(qt), qt])
            sides.append(heads)
            for e in range(n):
                outs[e][rows, :] = pick(me, pairs, e).astype(BF16)
        packed = [jnp.where(lane < HEAD, lo, hi) for lo, hi in zip(*sides)]
        for e in range(n):
            outs[e][length + i * step : length + (i + 1) * step, :] = pick(me, packed, e).astype(BF16)


def unpack_pairs(me, packed, n, h, lane):
    tiles = []
    for t in range(n // 2):
        lo, hi = pick(me, packed, 2 * t), pick(me, packed, 2 * t + 1)
        if h == 0:
            tiles.append(jnp.where(lane < HEAD, lo, turn(hi)))
        else:
            tiles.append(jnp.where(lane < HEAD, turn(lo), hi))
    return tiles


def unpack_body(ids, *refs, n):
    packed, outs = refs[:n], refs[n:]
    half, share = packed[0].shape[0], outs[0].shape[0]
    lane = lax.broadcasted_iota(jnp.int32, (share, LANES), 1)
    for i in range(half // share):
        pieces = [p[i * share : (i + 1) * share, :].astype(F32) for p in packed]
        for h in range(2):
            tiles = unpack_pairs(ids[1], pieces, n, h, lane)
            out = outs[h * (half // share) + i]
            for t, tile in enumerate(tiles):
                out[:, t * LANES : (t + 1) * LANES] = tile.astype(BF16)


def pack_body(ids, *refs, tp, n):
    parts, outs = refs[:tp], refs[tp:]
    half, share = outs[0].shape[0], parts[0].shape[0]
    lane = lax.broadcasted_iota(jnp.int32, (share, LANES), 1)
    for i in range(half // share):
        sides = []
        for h in range(2):
            grad = parts[h * (half // share) + i]
            heads = []
            for t in range(n // 2):
                tile = grad[:, t * LANES : (t + 1) * LANES].astype(F32)
                heads.extend([tile, turn(tile)] if h == 0 else [turn(tile), tile])
            sides.append(heads)
        packed = [jnp.where(lane < HEAD, lo, hi) for lo, hi in zip(*sides)]
        for e in range(n):
            outs[e][i * share : (i + 1) * share, :] = pick(ids[1], packed, e).astype(BF16)


BQ = 256
KC = 2048


def fill_keys(kv, marks, ka, va):
    size = kv[0].shape[0] // 3 * 2
    lane = lax.broadcasted_iota(jnp.int32, (size, LANES), 1)
    ones = jnp.where(lane < 3, 1.0, 0.0).astype(BF16)
    for e, ref in enumerate(kv):
        rows = slice(e * size, (e + 1) * size)
        both = ref[:size, :]
        ka[rows, :] = jnp.where(lane < HEAD, both, marks[rows, :])
        va[rows, :] = jnp.where(lane < HEAD, ones, both)


def query_marks(marks, row, lane):
    there = (lane >= HEAD) & (lane < HEAD + DOCS)
    bias = (marks[pl.ds(row, BQ), :].astype(F32) - 1.0) * -NEG_BIG
    return jnp.where(there, bias, 0.0)


def block_of(i, half, length, first):
    block, h = i // 2, i % 2
    blocks = half // BQ
    token = (first + block // blocks) * length + h * half + (block % blocks) * BQ
    return pl.multiple_of(block * BQ, BQ), h, pl.multiple_of(token, BQ)


def attend_body(*refs, m, n, first):
    kv, marks = refs[:n], refs[n]
    outs, lse = refs[n + 1 : n + 1 + m], refs[n + 1 + m]
    qs, ka, va, os = refs[n + 2 + m :]
    half = kv[0].shape[0] // 3
    length = 2 * half
    i = pl.program_id(0)

    @pl.when(i == 0)
    def _():
        fill_keys(kv, marks, ka, va)
        for e in range(m):
            qs[e * half : (e + 1) * half, :] = kv[first + e][length:, :]

    at, h, token = block_of(i, half, length, first)
    lane = lax.broadcasted_iota(jnp.int32, (BQ, LANES), 1)
    q = qs[pl.ds(at, BQ), :].astype(F32)
    q = jnp.where(h == 1, turn(q), q)
    q = jnp.where(lane < HEAD, q, query_marks(marks, token, lane)).astype(BF16)
    scores, top = [], None
    for j in range(n * length // KC):
        s = lax.dot_general(q, ka[j * KC : (j + 1) * KC, :], NT, preferred_element_type=F32)
        scores.append(s)
        for t in range(KC // LANES):
            tile = s[:, t * LANES : (t + 1) * LANES]
            top = tile if top is None else jnp.maximum(top, tile)
    top = jnp.max(top, axis=1, keepdims=True)
    total = jnp.zeros((BQ, LANES), F32)
    for j, s in enumerate(scores):
        p = jnp.exp2(s - top).astype(BF16)
        total += jnp.dot(p, va[j * KC : (j + 1) * KC, :], preferred_element_type=F32)
    weight = total[:, :1]
    o = total / weight
    o = jnp.where(h == 0, turn(o), o)
    log = jnp.broadcast_to(top + jnp.log2(weight), (BQ, LANES))
    other = (lane < HEAD) & (h == 1)
    os[pl.ds(at, BQ), :] = jnp.where(other, os[pl.ds(at, BQ), :], o)
    lse[pl.ds(at, BQ), :] = jnp.where(other, lse[pl.ds(at, BQ), :], log)

    @pl.when(i == pl.num_programs(0) - 1)
    def _():
        for e in range(m):
            outs[e][...] = os[e * half : (e + 1) * half, :].astype(BF16)


def attend(kv, marks, first, m):
    n, half = len(kv), kv[0].shape[0] // 3
    length = 2 * half
    steps = m * 2 * half // BQ
    args = [*kv, marks]
    outs = [shape((half, LANES), BF16)] * m + [shape((m * half, LANES), F32)]
    out = call(
        functools.partial(attend_body, m=m, n=n, first=first),
        outs,
        *args,
        grid=(steps,),
        in_specs=[whole_block(a) for a in args],
        out_specs=[whole_block(o) for o in outs],
        scratch=[
            pltpu.VMEM((m * half, LANES), BF16),
            pltpu.VMEM((n * length, LANES), BF16),
            pltpu.VMEM((n * length, LANES), BF16),
            pltpu.VMEM((m * half, LANES), F32),
        ],
        flops=4 * steps * BQ * n * length * 256,
        trans=steps * BQ * n * length,
        name="attend",
    )
    return out[:m], out[m]


def split3(value):
    high = value.astype(BF16).astype(F32)
    rest = value - high
    middle = rest.astype(BF16).astype(F32)
    return high, middle, rest - middle


def attend_back_body(*refs, m, n, first, start, end):
    grads, outs = (refs[k * m : (k + 1) * m] for k in range(2))
    kv, lse, marks = refs[2 * m : 2 * m + n], refs[2 * m + n], refs[2 * m + n + 1]
    at = 2 * m + n + 2
    before = None
    if not start:
        before, at = refs[at], at + 1
    if end:
        earlier, at = refs[at : at + n - m], at + n - m
        results, at = refs[at : at + n], at + n
        qs, gs, os, ds_, ka, va, acc = refs[at:]
    else:
        dqs, at = refs[at : at + m], at + m
        acc, at = refs[at], at + 1
        qs, gs, os, ds_, ka, va = refs[at:]
    half = kv[0].shape[0] // 3
    length = 2 * half
    i = pl.program_id(0)

    @pl.when(i == 0)
    def _():
        fill_keys(kv, marks, ka, va)
        for e in range(m):
            rows = slice(e * half, (e + 1) * half)
            qs[rows, :] = kv[first + e][length:, :]
            gs[rows, :] = grads[e][...]
            os[rows, :] = outs[e][...]
        acc[...] = jnp.zeros_like(acc) if start else before[...]

    row, h, token = block_of(i, half, length, first)
    lane = lax.broadcasted_iota(jnp.int32, (BQ, LANES), 1)
    here = pl.ds(row, BQ)
    q = qs[here, :].astype(F32)
    g = gs[here, :].astype(F32)
    o = os[here, :].astype(F32)
    log = lse[here, :]
    q = jnp.where(h == 1, turn(q), q)
    g = jnp.where(h == 0, turn(g), g)
    o = jnp.where(h == 0, turn(o), o)
    log = jnp.where(h == 1, turn(log), log)[:, :1]
    dot = jnp.sum(jnp.where(lane >= HEAD, g * o, 0.0), axis=1, keepdims=True)
    b0, b1, b2 = split3(-log)
    q_marks = query_marks(marks, token, lane)
    first_lane = HEAD + DOCS
    qa = jnp.where(lane == first_lane, b0, q_marks)
    qa = jnp.where(lane == first_lane + 1, b1, qa)
    qa = jnp.where(lane == first_lane + 2, b2, qa)
    qa = jnp.where(lane < HEAD, q, qa).astype(BF16)
    b0, b1, b2 = split3(-dot)
    ga = jnp.where(lane == 0, b0, jnp.where(lane == 1, b1, jnp.where(lane == 2, b2, 0.0)))
    ga = jnp.where(lane >= HEAD, g, ga).astype(BF16)
    q_t = q.T[:HEAD].astype(BF16)
    g_t = g.T[HEAD:].astype(BF16)
    total = jnp.zeros((BQ, LANES), F32)
    for j in range(n * length // KC):
        cols = slice(j * KC, (j + 1) * KC)
        s = lax.dot_general(qa, ka[cols, :], NT, preferred_element_type=F32)
        t = lax.dot_general(ga, va[cols, :], NT, preferred_element_type=F32)
        p = jnp.exp2(s)
        ds = (p * t).astype(BF16)
        p = p.astype(BF16)
        acc[HEAD:, cols] += jnp.dot(g_t, p, preferred_element_type=F32)
        acc[:HEAD, cols] += jnp.dot(q_t, ds, preferred_element_type=F32)
        total += jnp.dot(ds, ka[cols, :], preferred_element_type=F32)
    total = total * (HEAD**-0.5)
    total = jnp.where(h == 1, turn(total), total)
    other = (lane < HEAD) & (h == 1)
    ds_[here, :] = jnp.where(other, ds_[here, :], total)

    @pl.when(i == pl.num_programs(0) - 1)
    def _():
        if not end:
            for e in range(m):
                dqs[e][...] = ds_[e * half : (e + 1) * half, :].astype(BF16)
        else:
            for e in range(n):
                if e < n - m:
                    results[e][:half, :] = earlier[e][...]
                else:
                    at = (e - n + m) * half
                    results[e][:half, :] = ds_[at : at + half, :].astype(BF16)
                cols = slice(e * length, (e + 1) * length)
                turned = acc[:, cols].T
                key_lane = lax.broadcasted_iota(jnp.int32, (length, LANES), 1)
                results[e][half:, :] = jnp.where(key_lane < HEAD, turned * LN2, turned).astype(BF16)


def attend_back(grads, outs, kv, lse, marks, before, earlier, first, end):
    m, n, half = len(grads), len(kv), kv[0].shape[0] // 3
    length = 2 * half
    steps = m * 2 * half // BQ
    start = before is None
    args = [*grads, *outs, *kv, lse, marks] + ([] if start else [before]) + (list(earlier) if end else [])
    if end:
        results = [shape((half + length, LANES), BF16)] * n
    else:
        results = [shape((half, LANES), BF16)] * m + [shape((LANES, n * length), F32)]
    out = call(
        functools.partial(attend_back_body, m=m, n=n, first=first, start=start, end=end),
        results,
        *args,
        grid=(steps,),
        in_specs=[whole_block(a) for a in args],
        out_specs=[whole_block(o) for o in results],
        scratch=[pltpu.VMEM((m * half, LANES), BF16)] * 3
        + [pltpu.VMEM((m * half, LANES), F32)]
        + [pltpu.VMEM((n * length, LANES), BF16)] * 2
        + ([pltpu.VMEM((LANES, n * length), F32)] if end else []),
        flops=10 * steps * BQ * n * length * 256,
        trans=steps * BQ * n * length,
        name="attend_back",
    )
    return out if end else (out[:m], out[m])


def input_grad_body(ids, *refs, dp, n):
    pieces, ws = refs[:n], refs[n : n + dp]
    cosine, sine, whole, send, keep = refs[n + dp :]
    me = ids[1]
    half = send.shape[0]
    step = 256
    lane = lax.broadcasted_iota(jnp.int32, (step, LANES), 1)
    for h, target in ((1, send), (0, keep)):
        for i in range(half // step):
            rows = slice(h * half + i * step, h * half + (i + 1) * step)
            there = slice(i * step, (i + 1) * step)
            dq = [p[there, :].astype(F32) for p in pieces]
            kv = [p[half + rows.start : half + rows.stop, :].astype(F32) for p in pieces]
            qt = unpack_pairs(me, dq, n, h, lane)
            kt = unpack_pairs(me, kv, n, 0, lane)
            vt = unpack_pairs(me, kv, n, 1, lane)
            back = [x * cosine[rows, :] - swap_halves(x, lane) * sine[rows, :] for x in qt + kt]
            low = jnp.concatenate(back + vt, axis=1).astype(BF16)
            whole[rows, :] = low
            col = 0
            for w in ws:
                size = w.shape[0]
                total = lax.dot_general(low, w[...], NT, preferred_element_type=F32)
                target[there, col : col + size] = total.astype(target.dtype)
                col += size


def normed_of(value):
    centered = value - jnp.mean(value, axis=-1, keepdims=True)
    inverse = lax.rsqrt(jnp.mean(centered * centered, axis=-1, keepdims=True) + 1e-05)
    return centered * inverse, inverse


def back_of(grad, normed, inverse, gain):
    scaled = grad * gain
    inner = (
        scaled
        - jnp.mean(scaled, axis=-1, keepdims=True)
        - normed * jnp.mean(scaled * normed, axis=-1, keepdims=True)
    )
    return inverse * inner


RB = 64
CB = 512


def spans(total, size):
    size = min(size, total)
    return [slice(i, i + size) for i in range(0, total, size)]


class Copies:
    def __init__(self, sems):
        self.sems, self.count, self.groups = sems, 0, {}

    def start(self, group, src, dst):
        copy = pltpu.make_async_copy(src, dst, self.sems.at[self.count])
        copy.start()
        self.count += 1
        self.groups.setdefault(group, []).append(copy)

    def wait(self, group):
        for copy in self.groups[group]:
            copy.wait()


def weight_copies(copies, wod, wi, tp, dp, heads, gains, wi_all, wd_all, x=None, tokens=None):
    hidden = wi[0].shape[1]
    cols = wi[0].shape[0]
    lw = wod[0].shape[0] - hidden - 16

    def small():
        for f in range(dp):
            src = wod[f].at[pl.ds(hidden + lw, 16), :]
            copies.start("small", src, gains.at[:, pl.ds(f * cols, cols)])
        for d in range(tp):
            for f in range(dp):
                src = wod[d * dp + f].at[pl.ds(hidden, lw), :]
                copies.start("small", src, heads.at[pl.ds(d * lw, lw), pl.ds(f * cols, cols)])
        if x is not None:
            copies.start("small", x.at[pl.ds(0, tokens.shape[0]), :], tokens)

    def large():
        for d in range(tp):
            for f in range(dp):
                copies.start(d, wi[d * dp + f], wi_all.at[d, pl.ds(f * cols, cols), :])
                src = wod[d * dp + f].at[pl.ds(0, hidden), :]
                copies.start(d, src, wd_all.at[d, :, pl.ds(f * cols, cols)])

    return small, large


def forward_body(*refs, tp, dp):
    received, cotangent, x = refs[:tp], refs[tp], refs[tp + 1]
    at = tp + 2
    wod, wi = refs[at : at + tp * dp], refs[at + tp * dp : at + 2 * tp * dp]
    at += 2 * tp * dp
    second_low, out_low, slope, normed, inverse, second, terms, lows = refs[at : at + 8]
    act = refs[at + 8 : at + 8 + tp]
    heads, gains, wi_all, wd_all, tokens, attended, acc, sems = refs[at + 8 + tp :]
    share, width = tokens.shape
    hidden = wi[0].shape[1]
    lw = received[0].shape[1]
    copies = Copies(sems)
    small, large = weight_copies(copies, wod, wi, tp, dp, heads, gains, wi_all, wd_all, x, tokens)
    small()
    large()
    for j in range(tp):
        attended[:, j * lw : (j + 1) * lw] = received[j][...]
    copies.wait("small")
    for c in spans(width, CB):
        mixed = jnp.dot(attended[...], heads[:, c], preferred_element_type=F32)
        acc[:, c] = mixed + tokens[:, c].astype(F32)
    gain = gains[...].astype(F32)
    for b in spans(share, RB):
        n, r = normed_of(acc[b, :])
        out = n * gain[0:1, :] + gain[1:2, :]
        acc[b, :] = out
        lows[b, :] = out.astype(BF16)
        normed[b, :] = n
        inverse[b, :] = jnp.broadcast_to(r, (r.shape[0], LANES))
    for d in range(tp):
        copies.wait(d)
        for c in spans(hidden, CB):
            h = jnp.dot(lows[...], wi_all[d, :, c], preferred_element_type=F32)
            phi = 0.5 * (1.0 + lax.erf(h * SQRT_HALF))
            act[d][:, c] = (h * phi).astype(BF16)
            there = slice(d * hidden + c.start, d * hidden + c.stop)
            slope[:, there] = (phi + h * jnp.exp(-0.5 * h * h) * INV_SQRT_TAU).astype(BF16)
        for c in spans(width, CB):
            acc[:, c] += jnp.dot(act[d][...], wd_all[d, :, c], preferred_element_type=F32)
    sums = [jnp.zeros((1, width), F32)] * 2
    for b in spans(share, RB):
        n, r = normed_of(acc[b, :])
        out_low[b, :] = (n * gain[2:3, :] + gain[3:4, :]).astype(BF16)
        grad = cotangent[b, :].astype(F32)
        result = back_of(grad, n, r, gain[2:3, :])
        second[b, :] = result
        second_low[b, :] = result.astype(BF16)
        sums = [sums[0] + jnp.sum(grad * n, axis=0, keepdims=True), sums[1] + jnp.sum(grad, axis=0, keepdims=True)]
    terms[0:1, :], terms[1:2, :] = sums


def middle_scratch(tp, dp, lw, hidden, width, share):
    return [
        pltpu.VMEM((tp * lw, width), BF16),
        pltpu.VMEM((16, width), BF16),
        pltpu.VMEM((tp, width, hidden), BF16),
        pltpu.VMEM((tp, hidden, width), BF16),
    ]


ANY = pl.BlockSpec(memory_space=pl.ANY)


def forward(received, cotangent, x, wod, wi, tp, dp):
    (share, lw), (cols, hidden) = received[0].shape, wi[0].shape
    width = cols * dp
    outs = [
        shape((share, width), BF16),
        shape((share, width), BF16),
        shape((share, tp * hidden), BF16),
        shape((share, width), F32),
        shape((share, LANES), F32),
        shape((share, width), F32),
        shape((2, width), F32),
        shape((share, width), BF16),
    ]
    out = call(
        functools.partial(forward_body, tp=tp, dp=dp),
        outs + [shape((share, hidden), BF16)] * tp,
        *received,
        cotangent,
        x,
        *wod,
        *wi,
        in_specs=[FULL] * (tp + 1) + [ANY] * (1 + 2 * tp * dp),
        scratch=middle_scratch(tp, dp, lw, hidden, width, share)
        + [
            pltpu.VMEM((share, width), BF16),
            pltpu.VMEM((share, tp * lw), BF16),
            pltpu.VMEM((share, width), F32),
            pltpu.SemaphoreType.DMA((dp + tp * dp * 3 + 1,)),
        ],
        flops=2 * share * width * (tp * lw + 2 * tp * hidden),
        trans=3 * share * tp * hidden,
        name="forward",
    )
    return out[:7], out[7], out[8:]


def backward_body(*refs, tp, dp):
    second_low, slope, normed, inverse, second, terms = refs[:6]
    wod, wi = refs[6 : 6 + tp * dp], refs[6 + tp * dp : 6 + 2 * tp * dp]
    at = 6 + 2 * tp * dp
    rows, first = refs[at], refs[at + 1]
    pre, grads = refs[at + 2 : at + 2 + tp], refs[at + 2 + tp : at + 2 + 2 * tp]
    heads, gains, wi_all, wd_all, acc, edge, sems = refs[at + 2 + 2 * tp :]
    share, width = second_low.shape
    hidden, lw = pre[0].shape[1], grads[0].shape[1]
    copies = Copies(sems)
    small, large = weight_copies(copies, wod, wi, tp, dp, heads, gains, wi_all, wd_all)
    large()
    small()
    acc[...] = second[...]
    for d in range(tp):
        copies.wait(d)
        for c in spans(hidden, CB):
            grad = lax.dot_general(second_low[...], wd_all[d, c, :], NT, preferred_element_type=F32)
            there = slice(d * hidden + c.start, d * hidden + c.stop)
            pre[d][:, c] = (grad * slope[:, there].astype(F32)).astype(BF16)
        for c in spans(width, CB):
            acc[:, c] += lax.dot_general(pre[d][...], wi_all[d, c, :], NT, preferred_element_type=F32)
    copies.wait("small")
    gain = gains[...].astype(F32)
    sums = [jnp.zeros((1, width), F32)] * 2
    for b in spans(share, RB):
        grad, n = acc[b, :], normed[b, :]
        result = back_of(grad, n, inverse[b, :1], gain[0:1, :])
        first[b, :] = result
        rows[b, :] = result.astype(BF16)
        sums = [sums[0] + jnp.sum(grad * n, axis=0, keepdims=True), sums[1] + jnp.sum(grad, axis=0, keepdims=True)]
    for j in range(tp):
        part = lax.dot_general(rows[:share, :], heads[j * lw : (j + 1) * lw, :], NT, preferred_element_type=F32)
        grads[j][...] = part.astype(BF16)
    edge[...] = jnp.zeros_like(edge)
    edge[0:1, :], edge[1:2, :] = sums
    edge[2:4, :] = terms[...]
    rows[share:, :] = edge[...].astype(BF16)


def backward(forwarded, wod, wi, tp, dp, lw):
    cols, hidden = wi[0].shape
    share, width = forwarded[0].shape
    out = call(
        functools.partial(backward_body, tp=tp, dp=dp),
        [shape((share + 16, width), BF16), shape((share, width), F32)]
        + [shape((share, hidden), BF16)] * tp
        + [shape((share, lw), BF16)] * tp,
        *forwarded,
        *wod,
        *wi,
        in_specs=[FULL] * 6 + [ANY] * (2 * tp * dp),
        scratch=middle_scratch(tp, dp, lw, hidden, width, share)
        + [
            pltpu.VMEM((share, width), F32),
            pltpu.VMEM((16, width), F32),
            pltpu.SemaphoreType.DMA((dp + tp * dp * 3,)),
        ],
        flops=2 * share * width * (tp * lw + 2 * tp * hidden),
        name="backward",
    )
    return out[0], out[1], out[2 : 2 + tp], out[2 + tp :]


def rotate_heads(values, angles, sign):
    half = HEAD // 2
    cosine = jnp.cos(angles)[:, None, :half]
    sine = sign * jnp.sin(angles)[:, None, :half]
    first, second = values[..., :half], values[..., half:]
    return jnp.concatenate([first * cosine - second * sine, second * cosine + first * sine], axis=-1)


def gathered_attention(tokens, weights, angles, docs):
    rows, width = tokens.shape[0], weights[0].shape[1]
    heads = width // HEAD
    scale = HEAD**-0.5

    def project(w):
        return jnp.dot(tokens, w, preferred_element_type=F32).reshape(rows, heads, HEAD)

    q = rotate_heads(project(weights[0]), angles, 1.0).astype(BF16)
    k = rotate_heads(project(weights[1]), angles, 1.0).astype(BF16)
    v = project(weights[2]).astype(BF16)
    keys = jnp.concatenate(gather(k, "ctx"))
    values = jnp.concatenate(gather(v, "ctx"))
    all_docs = jnp.concatenate(gather(docs, "ctx"))

    def masked():
        s = jnp.einsum("qhd,khd->hqk", q, keys, preferred_element_type=F32) * scale
        return jnp.where(docs[None, :, None] == all_docs[None, None, :], s, NEG_BIG)

    s = masked()
    top = jnp.max(s, axis=-1, keepdims=True)
    p = jnp.exp(s - top)
    total = jnp.sum(p, axis=-1)
    out = jnp.einsum("hqk,khd->qhd", p.astype(BF16), values, preferred_element_type=F32)
    out = out / total.T[..., None]
    log = top[..., 0] + jnp.log(total)

    def backward(grad):
        grad = grad.astype(BF16).reshape(rows, heads, HEAD)
        dot = jnp.sum(grad.astype(F32) * out, axis=-1).T
        p = jnp.exp(masked() - log[..., None])
        dv = jnp.einsum("hqk,qhd->khd", p.astype(BF16), grad, preferred_element_type=F32)
        dp = jnp.einsum("qhd,khd->hqk", grad, values, preferred_element_type=F32)
        ds = (p * (dp - dot[..., None])).astype(BF16)
        dq = jnp.einsum("hqk,khd->qhd", ds, keys, preferred_element_type=F32) * scale
        dk = jnp.einsum("hqk,qhd->khd", ds, q, preferred_element_type=F32) * scale

        def owned(value):
            half = value.shape[0] // 2
            keep, got = scatter(value[half:].astype(BF16), value[:half], "ctx", 0)
            return keep + got.astype(F32)

        dq = rotate_heads(dq, angles, -1.0)
        dk = rotate_heads(owned(dk), angles, -1.0)
        return jnp.concatenate([x.astype(BF16).reshape(rows, width) for x in (dq, dk, owned(dv))], axis=1)

    return out.astype(BF16).reshape(rows, width), backward


def body(
    layer_input,
    segments,
    positions,
    w_q,
    w_k,
    w_v,
    w_o,
    w_in,
    w_out,
    ln1_gain,
    ln1_bias,
    ln2_gain,
    ln2_bias,
    cotangent,
):
    LINE.clear()
    seqs, length, width = layer_input.shape
    assert seqs == 1
    tp, dp, ctx = lax.axis_size("tp"), lax.axis_size("dp"), lax.axis_size("ctx")
    lw, hidden = w_q.shape[1], w_in.shape[1]
    heads = lw // HEAD
    ids = jnp.stack([lax.axis_index("dp"), lax.axis_index("ctx"), lax.axis_index("tp")]).astype(jnp.int32)
    share = length // tp
    half = length // 2
    spread = heads == ctx and heads % 2 == 0 and half % BQ == 0 and tp % 2 == 0

    def exchange(parts, first=0):
        return [p if first + k == 0 else swap(p, "ctx", first + k) for k, p in enumerate(parts)]

    def exchange_tp(parts):
        return [p if d == 0 else swap(p, "tp", d) for d, p in zip(order(tp), parts)]

    def over_dp(parts):
        return [gather(p, "dp") for p in parts]

    def arrange_tokens(value):
        table = value.reshape(tp, share)
        picked = [lax.dynamic_index_in_dim(table, ids[2] ^ d, 0, keepdims=False) for d in order(tp)]
        return jnp.stack(picked).reshape(length)

    def lined(parts):
        return [in_line(p) for p in parts]

    w_qkv = gather(step(lambda *w: jnp.concatenate(w, axis=1), w_q, w_k, w_v), "dp")
    vectors = jnp.stack([ln1_gain, ln1_bias, ln2_gain, ln2_bias])
    tall = chips(step(lambda *w: jnp.concatenate(w), w_out, w_o, jnp.pad(vectors, ((0, 12), (0, 0)))))
    x = arrange(ids, layer_input.reshape(length, width), tp, dp, order(tp))
    docs = arrange_tokens(in_line(segments).reshape(length))
    places = arrange_tokens(in_line(positions).reshape(length)).astype(F32)
    freq = 10000.0 ** (-(jnp.arange(LANES, dtype=jnp.int32) % (HEAD // 2)).astype(F32) * 2.0 / HEAD)
    angles = places[:, None] * freq[None, :]
    middle = ctx // 2
    near = [j for j, d in enumerate(order(tp)) if d in (1, tp // 2)]
    far = [j for j, d in enumerate(order(tp)) if d not in (0, 1, tp // 2)]

    if spread:
        all_docs = jnp.concatenate([docs] + [swap(docs, "ctx", e) for e in range(1, ctx)])
        side = jnp.where(jnp.arange(LANES) % HEAD < HEAD // 2, -1.0, 1.0)
        cosine, sine = step(lambda t: (jnp.cos(t), jnp.sin(t) * side[None, :]), angles)
        out_grad = arrange(ids, cotangent.reshape(length, width), tp, dp, [0])
        lane = jnp.arange(LANES)[None, :]
        in_docs = (lane >= HEAD) & (lane < HEAD + DOCS)
        folded = (lane >= HEAD + DOCS) & (lane < HEAD + DOCS + 3)
        due(w_qkv, all_docs)
        wi = gather(in_line(w_in), "dp")
        kv = call(
            functools.partial(project_body, dp=dp, n=heads),
            [shape((length + half, LANES), BF16)] * ctx,
            ids,
            x,
            *w_qkv,
            cosine,
            sine,
            in_specs=[SMEM] + [FULL] * (3 + dp),
            flops=6 * length * width * lw,
            name="project",
        )
        kv = exchange(kv)
        marks = step(lambda d: jnp.where(in_docs, lane - HEAD != d[:, None], folded).astype(BF16), all_docs)
        wi_far = chips(in_line(w_in))
        due(tall, kv, wi_far)
        tall_cores = [[swap(in_line(p), "tp", 1)] for p in tall]
        tall_own = gather(in_line(tall[0]), "dp")
        wi = [[p, *chips(in_line(p))[1:]] for p in wi[1:]]
        o, log = attend(kv, marks, 0, middle)
        outs, logs = [o], [log]
        mixed = exchange(o)
        due(wi, tall_cores)
        wi = [q for p in zip(wi_far, *wi) for q in p]
        tall = [tall_own] + over_dp(lined(tall[1:]))
        few = len(wi) // 2
        wi_cores = [swap(p, "tp", 1) for p in lined(wi[:few])]
        o, log = attend(kv, marks, middle, ctx - middle)
        outs.append(o)
        logs.append(log)
        due(wi_cores, tall[0])
        mixed.extend(exchange(lined(o), middle))
        wi = wi + wi_cores + [swap(p, "tp", 1) for p in lined(wi[few:])]
        due(mixed, wi)
        attended = call(
            functools.partial(unpack_body, n=heads),
            [shape((share, lw), BF16)] * tp,
            ids,
            *mixed,
            in_specs=[SMEM] + [FULL] * ctx,
            name="unpack",
        )
        due(tall)
        tall_cores = [c + [swap(in_line(q), "tp", 1) for q in p[1:]] for c, p in zip(tall_cores, tall)]
        tall = [q for p in tall + tall_cores for q in p]
    else:
        wi = [list(p) for p in zip(*[chips(p) for p in gather(w_in, "dp")])]
        wi = cores([q for p in wi for q in p])
        tall = cores([q for p in over_dp(tall) for q in p])
        out_grad = arrange(ids, cotangent.reshape(length, width), tp, dp, [0])
        joined = jnp.concatenate(w_qkv)
        mixed, attend_backward = gathered_attention(
            x, [joined[:, k * lw : (k + 1) * lw] for k in range(3)], angles, docs
        )
        attended = [mixed[j * share : (j + 1) * share] for j in range(tp)]

    received = exchange_tp(attended)
    forwarded, hidden_low, act = forward(received, out_grad, x, tall, wi, tp, dp)
    second_low, out_low, *forwarded = forwarded
    act = list(act)
    for j in near:
        act[j] = swap(act[j], "tp", order(tp)[j])
    rows, first_grad, pre, grads = backward([second_low, *forwarded], tall, wi, tp, dp, lw)
    due([act[j] for j in near])
    grads = exchange_tp(lined(grads))

    if spread:
        packed = call(
            functools.partial(pack_body, tp=tp, n=heads),
            [shape((half, LANES), BF16)] * ctx,
            ids,
            *grads,
            in_specs=[SMEM] + [FULL] * tp,
            name="pack",
        )
        packed = exchange(packed)
        due(packed[:middle])
    else:
        due(grads)
    second_low = chips(in_line(second_low))
    for j in far:
        act[j] = swap(in_line(act[j]), "tp", order(tp)[j])
    hidden_low = chips(in_line(hidden_low))
    if spread:
        query_grads, carried = attend_back(
            packed[:middle], outs[0], kv, logs[0], marks, None, None, 0, False
        )
        due(packed)
    due(second_low, act, hidden_low)
    second_low = second_low + [swap(p, "tp", 1) for p in lined(second_low)]
    hidden_low = hidden_low + [swap(p, "tp", 1) for p in lined(hidden_low)]
    rows = chips(in_line(rows))
    due(second_low)
    left = product(act, second_low)
    pre = list(pre)
    for j in far + near:
        pre[j] = swap(in_line(pre[j]), "tp", order(tp)[j])
    due(hidden_low)
    out_sum = GradSum(ids, 1, *left)
    if spread:
        pieces = attend_back(
            packed[middle:], outs[1], kv, logs[1], marks, carried, query_grads, middle, True
        )
    due(rows, pre, out_sum.got)
    rows = rows + [swap(p, "tp", 1) for p in lined(rows)]
    if spread:
        pieces = exchange(lined(pieces))
    out_sum.halve()
    left = products(pre, hidden_low, attended, rows, ctx)
    in_sum = GradSum(ids, 1, *left)
    if spread:
        due(pieces)
        out_sum.halve()
        whole, send, keep = call(
            functools.partial(input_grad_body, dp=dp, n=heads),
            [shape((length, 3 * lw), BF16), shape((half, width), BF16), shape((half, width), F32)],
            ids,
            *pieces,
            *w_qkv,
            cosine,
            sine,
            in_specs=[SMEM] + [FULL] * (ctx + dp + 2),
            flops=6 * length * width * lw,
            name="input_grad",
        )
    else:
        out_sum.halve()
        whole = attend_backward(jnp.concatenate(grads))
        total = lax.dot_general(whole, joined, NT, preferred_element_type=F32)
        send, keep = total[half:].astype(BF16), total[:half]
    got = swap(send, "tp", 1)
    mid = width // 2
    send = step(lambda l, r: over_rows(l[:, mid:], r).astype(BF16), x, whole)
    qkv_send = in_line(send)
    in_sum.halve()
    qkv_sum = GradSum(ids, 0, qkv_send, step(lambda l, r: over_rows(l[:, :mid], r), x, whole))
    out_sum.merge()
    keep, got = scatter(None, keep, "tp", 0, got)
    out_low = chips(in_line(out_low))
    in_sum.halve()
    qkv_sum.halve()
    out_sum.last()
    low = step(lambda l, k, f: (f + k + l.astype(F32)).astype(BF16), got, keep, first_grad)
    low = chips(low)
    qkv_sum.halve()
    in_sum.merge()
    due(out_low)
    output = place(ids, out_low + [swap(p, "tp", 1) for p in lined(out_low)], tp, dp, length)
    qkv_sum.merge()
    in_sum.last()
    (w_out_grad,) = out_sum.columns([width // dp])
    qkv_sum.last()
    due(low)
    input_grad = place(ids, low + [swap(p, "tp", 1) for p in lined(low)], tp, dp, length)
    w_in_grad, w_o_grad, terms = in_sum.rows(hidden, lw)
    w_q_grad, w_k_grad, w_v_grad = qkv_sum.columns([lw] * 3)
    return (
        output[None],
        input_grad[None],
        w_q_grad,
        w_k_grad,
        w_v_grad,
        w_o_grad,
        w_in_grad,
        w_out_grad,
        terms[0],
        terms[1],
        terms[2],
        terms[3],
    )


def solution(mesh):
    return jax.shard_map(
        body,
        mesh=mesh,
        in_specs=(
            P("dp", "ctx", None),
            P("dp", "ctx"),
            P("dp", "ctx"),
            P("dp", "tp"),
            P("dp", "tp"),
            P("dp", "tp"),
            P("tp", "dp"),
            P("dp", "tp"),
            P("tp", "dp"),
            P("dp"),
            P("dp"),
            P("dp"),
            P("dp"),
            P("dp", "ctx", None),
        ),
        out_specs=(
            P("dp", "ctx", None),
            P("dp", "ctx", None),
            P("dp", "tp"),
            P("dp", "tp"),
            P("dp", "tp"),
            P("tp", "dp"),
            P("dp", "tp"),
            P("tp", "dp"),
            P("dp"),
            P("dp"),
            P("dp"),
            P("dp"),
        ),
        check_vma=False,
    )
```
